32 devices in a mesh: batch: 16 (over z, y, core), mod: 2 (over x).
Axes of the slice: x: 2, y: 2, z: 4, core: 2. Of those that a mesh axis runs over, the one named last changes fastest.
Arguments:
- hidden_in: bfloat16 [64, 256, 768], P('batch', 'mod'), may hold values from -6 to 6
- text_mask: int32 [64, 128], P('batch'), may hold values 0 or 1
- region_count: int32 [64], P('batch'), may hold values from 10 to 100, as said below
- w_query: bfloat16 [768, 768], replicated, may hold values from -0.21875 to 0.21875
- b_query: bfloat16 [768], replicated, may hold values from -3 to 3
- w_key: bfloat16 [768, 768], replicated, may hold values from -0.21875 to 0.21875
- w_value: bfloat16 [768, 768], replicated, may hold values from -0.21875 to 0.21875
- b_value: bfloat16 [768], replicated, may hold values from -3 to 3
- w_attn_out: bfloat16 [768, 768], replicated, may hold values from -2 to 2
- b_attn_out: bfloat16 [768], replicated, may hold values from -3 to 3
- gain_attn: bfloat16 [768], replicated, may hold values from 0.099609375 to 1.8984375
- shift_attn: bfloat16 [768], replicated, may hold values from -3 to 3
- w_inner: bfloat16 [768, 3072], replicated, may hold values from -0.21875 to 0.21875
- b_inner: bfloat16 [3072], replicated, may hold values from -3 to 3
- w_outer: bfloat16 [3072, 768], replicated, may hold values from -0.21875 to 0.21875
- b_outer: bfloat16 [768], replicated, may hold values from -3 to 3
- gain_ffn: bfloat16 [768], replicated, may hold values from 0.099609375 to 1.8984375
- shift_ffn: bfloat16 [768], replicated, may hold values from -3 to 3
- cotangent: bfloat16 [64, 256, 768], P('batch', 'mod'), may hold values from -6 to 6
Outputs:
- layer_out: bfloat16 [64, 256, 768], P('batch', 'mod')
- input_grad: bfloat16 [64, 256, 768], P('batch', 'mod')
- grad_w_query: float32 [768, 768], replicated
- grad_b_query: float32 [768], replicated
- key_weight_gradient: float32 [768, 768], replicated
- grad_w_value: float32 [768, 768], replicated
- grad_b_value: float32 [768], replicated
- grad_w_attn_out: float32 [768, 768], replicated
- attention_output_bias_gradient: float32 [768], replicated
- grad_gain_attn: float32 [768], replicated
- grad_shift_attn: float32 [768], replicated
- grad_w_inner: float32 [768, 3072], replicated
- grad_b_inner: float32 [3072], replicated
- grad_w_outer: float32 [3072, 768], replicated
- grad_b_outer: float32 [768], replicated
- grad_gain_ffn: float32 [768], replicated
- grad_shift_ffn: float32 [768], replicated
The draws below stay inside these ranges and needn't reach their ends.
Inputs may be any that keep to these rules, and one draw needn't show every extreme that they name: `region_count`: every draw has a sequence with exactly 100 regions and one with exactly 10.
All inputs are finite; a program needn't handle non-finite values. No bound on the sum of `text_mask` on one device may be relied on, other than what follows from the above.
Results may differ from the reference program's by a relative error of at most 0.018.
Values may be sent and summed in bfloat16 or wider, within the bound.
A program may use at most 192 MiB of HBM per device.

```python
import math
import jax
import jax.numpy as jnp
from jax import lax

D = 768
HEADS = 12
HEAD_DIM = 64
FF = 3072
TEXT_LEN = 128
REGION_LEAST = 10
REGION_MOST = 100
SEQS = 64


def draw_region_count(key, part):
    first, second, third = jax.random.split(jax.random.fold_in(key, 17), 3)
    counts = jnp.maximum(jax.random.randint(first, (SEQS,), REGION_LEAST, REGION_MOST + 1), jax.random.randint(second, (SEQS,), REGION_LEAST, REGION_MOST + 1))
    picks = jax.random.permutation(third, SEQS)
    counts = counts.at[picks[0]].set(REGION_MOST)
    counts = counts.at[picks[1]].set(REGION_LEAST)
    return counts.astype(jnp.int32)


def touch_ends(values, own_key, least, high):
    dims = values.shape
    spot = [jax.random.randint(jax.random.fold_in(own_key, axis), (), 0, dims[axis]) for axis in range(len(dims))]
    values = values.at[tuple(spot)].set(least)
    longest = dims.index(max(dims))
    spot[longest] = (spot[longest] + 1) % dims[longest]
    return values.at[tuple(spot)].set(high)


def levels(key, extent, shards, low, top_value):
    loudness, own = 1.0, jax.random.fold_in(key, 6)
    for dim, shards_of in shards:
        steps = jnp.exp(jax.random.uniform(jax.random.fold_in(own, dim), (shards_of,), jnp.float32, low / len(shards), top_value / len(shards)))
        loudness = loudness * jnp.repeat(steps, extent[dim] // shards_of).reshape([-1 if axis == dim else 1 for axis in range(len(extent))])
    return loudness


def centred(rng, shape, deviation, limit, shards=(), held_as=jnp.bfloat16):
    values = jax.random.normal(rng, shape, jnp.float32) * deviation
    if len(shards) > 0:
        values = levels(rng, shape, shards, -0.22, 0.18) * values
    return jnp.clip(values, min=-limit, max=limit).astype(held_as)


def setup_inputs(seed: int = 0) -> dict:
    splits = jax.random.split(jax.random.key(seed), 20)
    return {
        "hidden_in": centred(splits[0], (SEQS, 2 * TEXT_LEN, D), 1.0, 6.0, ((0, 16), (1, 2))),
        "text_mask": touch_ends((jax.random.randint(splits[1], (SEQS, TEXT_LEN), 0, 8) < 7).astype(jnp.int32), jax.random.fold_in(splits[1], 1), 0, 1),
        "region_count": draw_region_count(jax.random.fold_in(splits[19], 71), 0),
        "w_query": centred(splits[3], (D, D), D ** -0.5, 0.21875),
        "b_query": centred(splits[4], (D,), 0.5, 3.0),
        "w_key": centred(splits[5], (D, D), D ** -0.5, 0.21875),
        "w_value": centred(splits[6], (D, D), D ** -0.5, 0.21875),
        "b_value": centred(splits[7], (D,), 0.5, 3.0),
        "w_attn_out": centred(splits[8], (D, D), (max(8, D // 96)) ** -0.5, 2.0),
        "b_attn_out": centred(splits[9], (D,), 0.5, 3.0),
        "gain_attn": jnp.clip(1.0 + 0.18 * jax.random.normal(splits[10], (D,), jnp.float32), 0.099609375, 1.8984375).astype(jnp.bfloat16),
        "shift_attn": centred(splits[11], (D,), 0.5, 3.0),
        "w_inner": centred(splits[12], (D, FF), D ** -0.5, 0.21875),
        "b_inner": centred(splits[13], (FF,), 0.5, 3.0),
        "w_outer": centred(splits[14], (FF, D), (FF // 4) ** -0.5, 0.21875),
        "b_outer": centred(splits[15], (D,), 0.5, 3.0),
        "gain_ffn": jnp.clip(1.0 + 0.18 * jax.random.normal(splits[16], (D,), jnp.float32), 0.099609375, 1.8984375).astype(jnp.bfloat16),
        "shift_ffn": centred(splits[17], (D,), 0.5, 3.0),
        "cotangent": centred(splits[18], (SEQS, 2 * TEXT_LEN, D), 1.0, 6.0, ((0, 16), (1, 2))),
    }


@jax.custom_vjp
def low(v):
    return lax.optimization_barrier(v.astype(jnp.bfloat16)).astype(jnp.float32)

@jax.custom_vjp
def low_back(v):
    return v

def low_keep(v):
    return (low(v), None)

def low_pass(kept, grad):
    return (grad,)

def back_keep(v):
    return (v, None)

def back_low(kept, grad):
    return (low(grad),)
low.defvjp(low_keep, low_pass)
low_back.defvjp(back_keep, back_low)
epsilon = 1e-05

def matmul(left_operand, right_operand):
    return jnp.einsum('jtm,mu->jtu', left_operand, right_operand, precision=lax.Precision.HIGHEST)

def layer_norm(rows, gain_vec, shift_vec):
    centre = rows - lax.optimization_barrier(jnp.mean(rows, axis=-1, keepdims=True))
    factor = lax.rsqrt(lax.optimization_barrier(jnp.mean(centre * centre, axis=-1, keepdims=True)) + epsilon)
    return centre * factor * gain_vec + shift_vec

def one_block(params, rows, valid):
    w_query, b_query, w_key, w_value, b_value, w_attn_out, b_attn_out, gain_attn, shift_attn, w_inner, b_inner, w_outer, b_outer, gain_ffn, shift_ffn = params
    seq_count, sequence_length, width = rows.shape
    query = low_back(low(matmul(rows, w_query) + b_query))
    key_rows = low_back(low(matmul(rows, w_key)))
    value_rows = low_back(low(matmul(rows, w_value) + b_value))
    query_h = query.reshape(seq_count, sequence_length, HEADS, HEAD_DIM)
    key_h = key_rows.reshape(seq_count, sequence_length, HEADS, HEAD_DIM)
    value_h = value_rows.reshape(seq_count, sequence_length, HEADS, HEAD_DIM)
    scores = jnp.einsum('sqhe,skhe->shqk', query_h, key_h, precision=lax.Precision.HIGHEST) / jnp.sqrt(jnp.float32(HEAD_DIM))
    scores = low_back(scores)
    masked = jnp.where(valid[:, None, None, :], scores, jnp.float32(-1000000000.0))
    probs = low(jax.nn.softmax(masked, axis=-1))
    context = jnp.einsum('shqk,skhe->sqhe', probs, value_h, precision=lax.Precision.HIGHEST)
    context = low_back(low(context.reshape(seq_count, sequence_length, width)))
    branch = low_back(matmul(context, w_attn_out) + b_attn_out)
    mid = layer_norm(rows + branch, gain_attn, shift_attn)
    pre = low_back(matmul(low(mid), w_inner) + b_inner)
    act = low(jax.nn.gelu(pre, approximate=False))
    ffn = low_back(matmul(act, w_outer) + b_outer)
    return layer_norm(mid + ffn, gain_ffn, shift_ffn)

def reference(hidden_in, text_mask, region_count, w_query, b_query, w_key, w_value, b_value, w_attn_out, b_attn_out, gain_attn, shift_attn, w_inner, b_inner, w_outer, b_outer, gain_ffn, shift_ffn, cotangent):
    params = tuple((member.astype(jnp.float32) for member in (w_query, b_query, w_key, w_value, b_value, w_attn_out, b_attn_out, gain_attn, shift_attn, w_inner, b_inner, w_outer, b_outer, gain_ffn, shift_ffn)))
    rows = hidden_in.astype(jnp.float32)
    group = math.gcd(SEQS, max(1, 4096 // (2 * TEXT_LEN)))
    blocks = SEQS // group
    slots = jnp.arange(TEXT_LEN, dtype=jnp.int32)[None, :] < region_count[:, None]
    valid = jnp.concatenate((text_mask == 1, slots), axis=1)

    def forward(params, rows):
        grouped = rows.reshape(blocks, group, 2 * TEXT_LEN, D)
        masks = valid.reshape(blocks, group, 2 * TEXT_LEN)
        stepper = jax.checkpoint(lambda pair: one_block(params, pair[0], pair[1]))
        result = lax.map(stepper, (grouped, masks))
        return result.reshape(SEQS, 2 * TEXT_LEN, D)
    output, pullback = jax.vjp(forward, params, rows)
    grads, input_grad = pullback(cotangent.astype(jnp.float32))
    return (output.astype(jnp.bfloat16), input_grad.astype(jnp.bfloat16), grads[0], grads[1], grads[2], grads[3], grads[4], grads[5], grads[6], grads[7], grads[8], grads[9], grads[10], grads[11], grads[12], grads[13], grads[14])
```

```python
import functools

import jax
import jax.numpy as jnp
from jax import lax
from jax.experimental import pallas as pl
from jax.experimental.pallas import tpu as pltpu
from jax.sharding import PartitionSpec as P

HEADS = 12
MESH = pl.DeviceIdType.MESH
ROWS = 256
LANES = 768


class Wire:
    def __init__(self, extra_bits):
        self.b = lax.axis_index("batch")
        self.m = lax.axis_index("mod")
        self.core = lax.rem(self.b, 2)
        self.y = lax.rem(self.b // 2, 2)
        self.z = lax.rem(self.b // 4, 4)
        self.extra_bits = extra_bits

    def flip(self, bit):
        own = lax.rem(self.b // (1 << bit), 2)
        return (self.b + (1 - 2 * own) * (1 << bit), self.m)

    def peer(self, dim):
        if dim == "x":
            return (self.b, 1 - self.m)
        if dim == "y":
            return self.flip(1)
        if dim == "core":
            return self.flip(0)
        if dim == "up":
            return (self.b + 4, self.m)
        if dim == "down":
            return (self.b - 4, self.m)
        return self.flip(dim)

    def coord(self, dim):
        return self.m if dim == "x" else self.y

    def barrier(self):
        bar = pltpu.get_barrier_semaphore()
        peers = [self.peer(d) for d in ("core", "x", "y")]
        peers += [self.flip(bit) for bit in range(2, 4 + self.extra_bits)]
        for who in peers:
            pl.semaphore_signal(bar, inc=1, device_id=who, device_id_type=MESH)
        mid_low, mid_high = self.z == 1, self.z == 2

        @pl.when(mid_low)
        def _():
            pl.semaphore_signal(bar, inc=1, device_id=self.peer("up"), device_id_type=MESH)

        @pl.when(mid_high)
        def _():
            pl.semaphore_signal(bar, inc=1, device_id=self.peer("down"), device_id_type=MESH)

        pl.semaphore_wait(bar, len(peers) + jnp.where(mid_low | mid_high, 1, 0))


def plan_sizes(kinds, extra_bits):
    rows = sems = 0
    for kind in kinds:
        n = ROWS
        rows += ROWS
        sems += 1
        order = "xyz" if kind == "A" else "yxz" if kind == "B" else "zxy" if kind == "C" else "zyx"
        for dim in order:
            if dim == "z":
                rows += 6 * (n // 4)
                n //= 4
            else:
                rows += n // 2
                n //= 2
        rows += extra_bits * n
        sems += 6 + 6 + 4 + extra_bits + 1
    return rows, sems


def add_rows(acc, at, rb, rb_at, n):
    step = min(n, 64)

    def body(i, carry):
        d = pl.multiple_of(at + i * step, 16)
        s = pl.multiple_of(rb_at + i * step, 16)
        total = acc[pl.ds(d, step), :].astype(jnp.float32) + rb[pl.ds(s, step), :].astype(jnp.float32)
        acc[pl.ds(d, step), :] = total.astype(jnp.bfloat16)
        return carry

    if n == step:
        body(0, 0)
    else:
        lax.fori_loop(0, n // step, body, 0)


class Tasks:
    def __init__(self, wire, kinds, acc, sib, fin, rb, ssem, rsem):
        self.w, self.acc, self.sib, self.fin, self.rb = wire, acc, sib, fin, rb
        self.ssem, self.rsem = ssem, rsem
        self.rb_at = 0
        self.sem_at = 0
        self.homes = []
        self.steps = [self.build(t, kind) for t, kind in enumerate(kinds)]

    def space(self, n):
        at = self.rb_at
        self.rb_at += n
        return at

    def copy(self, src, dst, who):
        k = self.sem_at
        self.sem_at += 1
        return lambda: pltpu.make_async_remote_copy(
            src_ref=src(), dst_ref=dst(), send_sem=self.ssem.at[k], recv_sem=self.rsem.at[k], device_id=who, device_id_type=MESH
        )

    def rows(self, at, n):
        return self.acc.at[pl.ds(pl.multiple_of(at, 16), n), :]

    def build(self, t, kind):
        w = self.w
        steps = []
        home = t * ROWS
        at0 = self.space(ROWS)

        def done(at, n):
            return self.rb.at[pl.ds(pl.multiple_of(at + (at0 - home), 16), n), :]

        def keep(at, n):
            self.rb[pl.ds(pl.multiple_of(at + (at0 - home), 16), n), :] = self.acc[pl.ds(pl.multiple_of(at, 16), n), :]

        def exchange(src, dst, who, then):
            cp = self.copy(src, dst, who)

            def begin():
                cp().start()

            def finish():
                cp().wait()
                then()

            steps.append((begin, finish))

        def reduce(dim, base, n):
            half, a = n // 2, w.coord(dim)
            at = self.space(half)
            kept = base + a * half
            sent = base + (1 - a) * half
            exchange(
                lambda: self.rows(sent, half),
                lambda: self.rb.at[pl.ds(at, half), :],
                w.peer(dim),
                lambda: add_rows(self.acc, kept, self.rb, at, half),
            )
            return kept, half

        def gather(dim, base, n):
            exchange(lambda: done(base, n), lambda: done(base, n), w.peer(dim), lambda: None)

        def line_reduce(base, n):
            q, z, zz = n // 4, w.z, 3 - w.z
            for s in (1, 2, 3):
                up_at, down_at = self.space(q), self.space(q)
                up_sends, up_gets = (z < 3) & (s >= z + 1), (z >= 1) & (s >= z)
                down_sends, down_gets = (zz < 3) & (s >= zz + 1), (zz >= 1) & (s >= zz)
                up_src = base + jnp.clip(4 - s + z, 0, 3) * q
                down_src = base + jnp.clip(s + z - 4, 0, 3) * q
                up_add = base + jnp.clip(3 - s + z, 0, 3) * q
                down_add = base + jnp.clip(s - 3 + z, 0, 3) * q
                up = self.copy(lambda v=up_src: self.rows(v, q), lambda v=up_at: self.rb.at[pl.ds(v, q), :], w.peer("up"))
                down = self.copy(lambda v=down_src: self.rows(v, q), lambda v=down_at: self.rb.at[pl.ds(v, q), :], w.peer("down"))
                steps.append(line_step(up, down, up_sends, up_gets, down_sends, down_gets,
                                       lambda a=up_add, r=up_at: add_rows(self.acc, a, self.rb, r, q),
                                       lambda a=down_add, r=down_at: add_rows(self.acc, a, self.rb, r, q)))
            return base + z * q, q

        def line_gather(base, q):
            z = w.z
            for s in (1, 2, 3):
                up_sends, up_gets = (z < 3) & (z - (s - 1) >= 0), z - s >= 0
                down_sends, down_gets = (z > 0) & (z + (s - 1) <= 3), z + s <= 3
                up_src = base + jnp.clip(z - s + 1, 0, 3) * q
                down_src = base + jnp.clip(z + s - 1, 0, 3) * q
                up = self.copy(lambda v=up_src: done(v, q), lambda v=up_src: done(v, q), w.peer("up"))
                down = self.copy(lambda v=down_src: done(v, q), lambda v=down_src: done(v, q), w.peer("down"))
                steps.append(line_step(up, down, up_sends, up_gets, down_sends, down_gets, None, None))

        def line_step(up, down, up_sends, up_gets, down_sends, down_gets, up_then, down_then):
            def begin():
                @pl.when(up_sends)
                def _():
                    up().start()

                @pl.when(down_sends)
                def _():
                    down().start()

            def finish():
                for cp, gets, then in ((up, up_gets, up_then), (down, down_gets, down_then)):
                    @pl.when(gets)
                    def _(cp=cp, then=then):
                        cp().wait_recv()
                        if then is not None:
                            then()

                for cp, sends in ((up, up_sends), (down, down_sends)):
                    @pl.when(sends)
                    def _(cp=cp):
                        cp().wait_send()

            return begin, finish

        def then_keep(base, n):
            begin, finish = steps.pop()

            def finish_and_keep():
                finish()
                keep(base, n)

            steps.append((begin, finish_and_keep))

        def widen(base, n):
            for bit in range(4, 4 + w.extra_bits):
                at = self.space(n)
                exchange(
                    lambda: self.rows(base, n),
                    lambda at=at: self.rb.at[pl.ds(at, n), :],
                    w.peer(bit),
                    lambda at=at: add_rows(self.acc, base, self.rb, at, n),
                )

        exchange(
            lambda: self.sib.at[pl.ds(home, ROWS), :],
            lambda: self.rb.at[pl.ds(at0, ROWS), :],
            w.peer("core"),
            lambda: add_rows(self.acc, home, self.rb, at0, ROWS),
        )
        if kind in "AB":
            d1, d2 = ("x", "y") if kind == "A" else ("y", "x")
            b1, n1 = reduce(d1, home, ROWS)
            b2, n2 = reduce(d2, b1, n1)
            b3, n3 = line_reduce(b2, n2)
            widen(b3, n3)
            then_keep(b3, n3)
            line_gather(b2, n3)
            gather(d2, b2, n2)
            gather(d1, b1, n1)
        else:
            d1, d2 = ("x", "y") if kind == "C" else ("y", "x")
            b1, n1 = line_reduce(home, ROWS)
            b2, n2 = reduce(d1, b1, n1)
            b3, n3 = reduce(d2, b2, n2)
            widen(b3, n3)
            then_keep(b3, n3)
            gather(d2, b3, n3)
            gather(d1, b2, n2)
            line_gather(home, n1)
        exchange(
            lambda: self.rb.at[pl.ds(at0, ROWS), :],
            lambda: self.fin.at[pl.ds(home, ROWS), :],
            w.peer("core"),
            lambda: None,
        )
        self.homes.append(at0)
        return steps

    def op(self, t, p):
        steps = self.steps[t]
        if p > 0:
            steps[p - 1][1]()
        if p < len(steps):
            steps[p][0]()


KINDS = "ABCABDABCABDABCABD"
START = tuple(t // 3 for t in range(18))
SMALL = 16


def block_of(refs, half, t):
    outer, inner, attn = refs
    if t < 6:
        return outer.at[pl.ds(pl.multiple_of(half * 1536 + t * ROWS, ROWS), ROWS), :]
    if t < 12:
        i, j = (t - 6) % 3, (t - 6) // 3
        return inner.at[pl.ds(i * ROWS, ROWS), pl.ds(pl.multiple_of((half * 2 + j) * LANES, LANES), LANES)]
    return attn.at[pl.ds(pl.multiple_of(half * 1536 + (t - 12) * ROWS, ROWS), ROWS), :]


def sum_kernel(extra_bits, g_outer, g_inner, g_attn, small_in, s_outer, s_inner, s_attn, small_out,
               acc, sib, fin, rb, small, small_rb, ssem, rsem, lsem, vsem):
    w = Wire(extra_bits)
    count = len(KINDS)
    ins, outs = (g_outer, g_inner, g_attn), (s_outer, s_inner, s_attn)

    def load(t, who):
        half, buf = (w.core, acc) if who == 0 else (1 - w.core, sib)
        return pltpu.make_async_copy(block_of(ins, half, t), buf.at[pl.ds(t * ROWS, ROWS), :], lsem.at[2 * t + who])

    def store(t, who):
        if who == 0:
            half, source = w.core, rb.at[pl.ds(tasks.homes[t], ROWS), :]
        else:
            half, source = 1 - w.core, fin.at[pl.ds(t * ROWS, ROWS), :]
        return pltpu.make_async_copy(source, block_of(outs, half, t), lsem.at[2 * t + who])

    for t in range(count):
        load(t, 1).start()
        load(t, 0).start()
    w.barrier()
    tasks = Tasks(w, KINDS, acc, sib, fin, rb, ssem, rsem)

    small[0] = small_in[...]
    hops = ["core", "x", "y"] + list(range(2, 4 + extra_bits))

    def small_copy(k):
        return pltpu.make_async_remote_copy(
            src_ref=small.at[k], dst_ref=small_rb.at[k], send_sem=vsem.at[0, k], recv_sem=vsem.at[1, k],
            device_id=w.peer(hops[k]), device_id_type=MESH)

    def small_op(k):
        if k > 0:
            small_copy(k - 1).wait()
            small[k] = small[k - 1] + small_rb[k - 1]
        if k < len(hops):
            small_copy(k).start()

    ops = [(START[t] + p, t, p) for t in range(count) for p in range(len(tasks.steps[t]) + 1)]
    ops += [(k + 1, count, k) for k in range(len(hops) + 1)]
    for _, t, p in sorted(ops):
        if t == count:
            small_op(p)
            continue
        if p == 0:
            load(t, 1).wait()
        if p == 1:
            load(t, 0).wait()
        tasks.op(t, p)
        if p == len(tasks.steps[t]):
            store(t, 0).start()
            store(t, 1).start()
    small_out[...] = small[len(hops)]
    for t in range(count):
        store(t, 0).wait()
        store(t, 1).wait()


def sum_gradients(g_outer, g_inner, g_attn, small_in):
    extra_bits = (lax.axis_size("batch") // 16).bit_length() - 1
    rows, sems = plan_sizes(KINDS, extra_bits)
    hops = 5 + extra_bits
    count = len(KINDS)
    hbm = pl.BlockSpec(memory_space=pl.ANY)
    vmem = pl.BlockSpec(memory_space=pltpu.VMEM)
    return pl.pallas_call(
        functools.partial(sum_kernel, extra_bits),
        out_shape=(
            jax.ShapeDtypeStruct(g_outer.shape, jnp.bfloat16),
            jax.ShapeDtypeStruct(g_inner.shape, jnp.bfloat16),
            jax.ShapeDtypeStruct(g_attn.shape, jnp.bfloat16),
            jax.ShapeDtypeStruct(small_in.shape, jnp.float32),
        ),
        in_specs=[hbm, hbm, hbm, vmem],
        out_specs=(hbm, hbm, hbm, vmem),
        scratch_shapes=[
            pltpu.VMEM((count * ROWS, LANES), jnp.bfloat16),
            pltpu.VMEM((count * ROWS, LANES), jnp.bfloat16),
            pltpu.VMEM((count * ROWS, LANES), jnp.bfloat16),
            pltpu.VMEM((rows, LANES), jnp.bfloat16),
            pltpu.VMEM((hops + 1, SMALL, LANES), jnp.float32),
            pltpu.VMEM((hops, SMALL, LANES), jnp.float32),
            pltpu.SemaphoreType.DMA((sems,)),
            pltpu.SemaphoreType.DMA((sems,)),
            pltpu.SemaphoreType.DMA((2 * count,)),
            pltpu.SemaphoreType.DMA((2, hops)),
        ],
        compiler_params=pltpu.CompilerParams(collective_id=1, has_side_effects=True, vmem_limit_bytes=60 << 20),
    )(g_outer, g_inner, g_attn, small_in)


epsilon = 1e-05


def partner_2(block, axis, distance):
    count = lax.axis_size(axis)
    route = []
    for low in range(count):
        high = low | 1 << distance
        if high != low and high < count:
            route += [(low, high), (high, low)]
    return lax.ppermute(block, axis, route)


def linear(rows, weight_matrix):
    return lax.dot_general(
        rows,
        weight_matrix,
        (((rows.ndim - 1,), (0,)), ((), ())),
        preferred_element_type=jnp.float32,
    )


def back_linear(gradient_row_block, weight_matrix):
    return jnp.einsum(
        "nhr,gr->nhg", gradient_row_block, weight_matrix, preferred_element_type=jnp.float32
    )


def weight_grad(layer_inputs, gradient_row_block):
    return jnp.einsum(
        "try,tro->yo", layer_inputs, gradient_row_block, preferred_element_type=jnp.float32
    )


def row_total(values):
    return jnp.sum(values.astype(jnp.float32), axis=(0, 1))


def layer_norm(rows):
    centre = rows - jnp.mean(rows, axis=-1, keepdims=True)
    factor = lax.rsqrt(jnp.mean(centre * centre, axis=-1, keepdims=True) + epsilon)
    return (centre * factor, factor)


def norm_back(gradient_row_block, normed, factor):
    return factor * (
        gradient_row_block
        - jnp.mean(gradient_row_block, axis=-1, keepdims=True)
        - normed * jnp.mean(gradient_row_block * normed, axis=-1, keepdims=True)
    )


def on_device(
    hidden_in,
    text_mask,
    region_count,
    w_query,
    b_query,
    w_key,
    w_value,
    b_value,
    w_attn_out,
    b_attn_out,
    gain_attn,
    shift_attn,
    w_inner,
    b_inner,
    w_outer,
    b_outer,
    gain_ffn,
    shift_ffn,
    cotangent,
):
    seq_count, half_len, width = hidden_in.shape
    head_size = width // HEADS
    factor_qk = 1.0 / jnp.sqrt(jnp.float32(head_size))
    text_half = lax.axis_index("mod") == 0
    rows_in = hidden_in.astype(jnp.float32)
    query = linear(hidden_in, w_query) + b_query.astype(jnp.float32)
    query_b = query.astype(jnp.bfloat16)
    key_b = linear(hidden_in, w_key).astype(jnp.bfloat16)
    value_b = (linear(hidden_in, w_value) + b_value.astype(jnp.float32)).astype(jnp.bfloat16)
    partner = partner_2(jnp.stack((key_b, value_b)), "mod", 0)
    all_keys = jnp.where(
        text_half,
        jnp.concatenate((key_b, partner[0]), axis=1),
        jnp.concatenate((partner[0], key_b), axis=1),
    )
    all_values = jnp.where(
        text_half,
        jnp.concatenate((value_b, partner[1]), axis=1),
        jnp.concatenate((partner[1], value_b), axis=1),
    )
    slot_ok = lax.broadcasted_iota(jnp.int32, (seq_count, half_len), 1) < region_count[:, None]
    valid = jnp.concatenate((text_mask == 1, slot_ok), axis=1)[:, None, None, :]
    query_h = query_b.reshape(seq_count, half_len, HEADS, head_size)
    key_h = all_keys.reshape(seq_count, 2 * half_len, HEADS, head_size)
    value_h = all_values.reshape(seq_count, 2 * half_len, HEADS, head_size)

    def masked_scores():
        scores = (
            jnp.einsum("sqhe,skhe->shqk", query_h, key_h, preferred_element_type=jnp.float32)
            * factor_qk
        )
        return jnp.where(valid, scores, jnp.float32(-1000000000.0))

    masked = masked_scores()
    highest = jnp.max(masked, axis=-1, keepdims=True)
    expo = jnp.exp(masked - highest)
    totals = jnp.sum(expo, axis=-1, keepdims=True)
    log_total = highest + jnp.log(totals)
    probs_b = (expo / totals).astype(jnp.bfloat16)
    context_b = (
        jnp.einsum("shqk,skhe->sqhe", probs_b, value_h, preferred_element_type=jnp.float32)
        .reshape(seq_count, half_len, width)
        .astype(jnp.bfloat16)
    )
    branch = linear(context_b, w_attn_out) + b_attn_out.astype(jnp.float32)
    normed_one, factor_one = layer_norm(rows_in + branch)
    middle = normed_one * gain_attn.astype(jnp.float32) + shift_attn.astype(jnp.float32)
    middle_b = middle.astype(jnp.bfloat16)
    pre_act = linear(middle_b, w_inner) + b_inner.astype(jnp.float32)
    activ, gelu_back = jax.vjp(lambda values: jax.nn.gelu(values, approximate=False), pre_act)
    activ_b = activ.astype(jnp.bfloat16)
    ffn_out = linear(activ_b, w_outer) + b_outer.astype(jnp.float32)
    normed_two, factor_two = layer_norm(middle + ffn_out)
    layer_out = (normed_two * gain_ffn.astype(jnp.float32) + shift_ffn.astype(jnp.float32)).astype(
        jnp.bfloat16
    )
    upstream = cotangent.astype(jnp.float32)
    grad_gain_ffn = jnp.sum(upstream * normed_two, axis=(0, 1))
    grad_shift_ffn = jnp.sum(upstream, axis=(0, 1))
    d_res_two = norm_back(upstream * gain_ffn.astype(jnp.float32), normed_two, factor_two)
    d_ffn_b = d_res_two.astype(jnp.bfloat16)
    grad_b_outer = row_total(d_ffn_b)
    grad_w_outer = weight_grad(activ_b, d_ffn_b)
    d_activ = back_linear(d_ffn_b, w_outer)
    d_pre_b = gelu_back(d_activ)[0].astype(jnp.bfloat16)
    grad_b_inner = row_total(d_pre_b)
    grad_w_inner = weight_grad(middle_b, d_pre_b)
    d_middle = d_res_two + back_linear(d_pre_b, w_inner)
    grad_gain_attn = jnp.sum(d_middle * normed_one, axis=(0, 1))
    grad_shift_attn = jnp.sum(d_middle, axis=(0, 1))
    d_res_one = norm_back(d_middle * gain_attn.astype(jnp.float32), normed_one, factor_one)
    d_branch_b = d_res_one.astype(jnp.bfloat16)
    attention_output_bias_gradient = row_total(d_branch_b)
    grad_w_attn_out = weight_grad(context_b, d_branch_b)
    d_context_b = back_linear(d_branch_b, w_attn_out).astype(jnp.bfloat16)
    d_context_h = d_context_b.reshape(seq_count, half_len, HEADS, head_size)
    probs_again = jnp.exp(masked_scores() - log_total)
    probs_low = probs_again.astype(jnp.bfloat16)
    d_probs = jnp.einsum(
        "sqhe,skhe->shqk", d_context_h, value_h, preferred_element_type=jnp.float32
    )
    d_scores_b = (
        probs_again * (d_probs - jnp.sum(probs_again * d_probs, axis=-1, keepdims=True))
    ).astype(jnp.bfloat16)
    d_query_b = (
        (
            jnp.einsum("shqk,skhe->sqhe", d_scores_b, key_h, preferred_element_type=jnp.float32)
            * factor_qk
        )
        .reshape(seq_count, half_len, width)
        .astype(jnp.bfloat16)
    )
    d_keys_all = (
        jnp.einsum("shqk,sqhe->skhe", d_scores_b, query_h, preferred_element_type=jnp.float32)
        * factor_qk
    ).reshape(seq_count, 2 * half_len, width)
    d_values_all = jnp.einsum(
        "shqk,sqhe->skhe", probs_low, d_context_h, preferred_element_type=jnp.float32
    ).reshape(seq_count, 2 * half_len, width)
    lower_keys, upper_keys = (d_keys_all[:, :half_len], d_keys_all[:, half_len:])
    lower_values, upper_values = (d_values_all[:, :half_len], d_values_all[:, half_len:])
    own_keys = jnp.where(text_half, lower_keys, upper_keys)
    own_values = jnp.where(text_half, lower_values, upper_values)
    other_keys = jnp.where(text_half, upper_keys, lower_keys)
    other_values = jnp.where(text_half, upper_values, lower_values)
    returned = partner_2(
        jnp.stack((other_keys, other_values)).astype(jnp.bfloat16), "mod", 0
    ).astype(jnp.float32)
    d_key_b = (own_keys + returned[0]).astype(jnp.bfloat16)
    d_value_b = (own_values + returned[1]).astype(jnp.bfloat16)
    grad_b_query = row_total(d_query_b)
    grad_b_value = row_total(d_value_b)
    grad_w_query = weight_grad(hidden_in, d_query_b)
    key_weight_gradient = weight_grad(hidden_in, d_key_b)
    grad_w_value = weight_grad(hidden_in, d_value_b)
    input_grad = (
        d_res_one
        + back_linear(d_query_b, w_query)
        + back_linear(d_key_b, w_key)
        + back_linear(d_value_b, w_value)
    ).astype(jnp.bfloat16)
    g_outer = grad_w_outer.astype(jnp.bfloat16)
    g_inner = grad_w_inner.astype(jnp.bfloat16)
    g_attn = jnp.concatenate(
        [g.astype(jnp.bfloat16) for g in (grad_w_query, key_weight_gradient, grad_w_value, grad_w_attn_out)]
    )
    small_in = jnp.concatenate(
        [
            grad_b_query, grad_b_value, attention_output_bias_gradient, grad_gain_attn, grad_shift_attn,
            grad_b_inner, grad_b_outer, grad_gain_ffn, grad_shift_ffn, jnp.zeros((4 * width,), jnp.float32),
        ]
    ).reshape(SMALL, width)
    s_outer, s_inner, s_attn, s_small = sum_gradients(g_outer, g_inner, g_attn, small_in)
    wide = s_attn.astype(jnp.float32).reshape(4, width, width)
    return (
        layer_out,
        input_grad,
        wide[0],
        s_small[0],
        wide[1],
        wide[2],
        s_small[1],
        wide[3],
        s_small[2],
        s_small[3],
        s_small[4],
        s_inner.astype(jnp.float32),
        s_small[5:9].reshape(-1),
        s_outer.astype(jnp.float32),
        s_small[9],
        s_small[10],
        s_small[11],
    )


def solution(mesh):
    in_specs = (
        P("batch", "mod", None),
        P("batch", None),
        P("batch"),
        P(),
        P(),
        P(),
        P(),
        P(),
        P(),
        P(),
        P(),
        P(),
        P(),
        P(),
        P(),
        P(),
        P(),
        P(),
        P("batch", "mod", None),
    )
    out_specs = (
        P("batch", "mod", None),
        P("batch", "mod", None),
        P(),
        P(),
        P(),
        P(),
        P(),
        P(),
        P(),
        P(),
        P(),
        P(),
        P(),
        P(),
        P(),
        P(),
        P(),
    )
    return jax.shard_map(
        on_device, mesh=mesh, in_specs=in_specs, out_specs=out_specs, check_vma=False
    )
```

```python
import functools

import jax
import jax.numpy as jnp
from jax import lax
from jax.experimental import pallas as pl
from jax.experimental.pallas import tpu as pltpu
from jax.sharding import PartitionSpec as P

MESH = pl.DeviceIdType.MESH
ROWS = 256
LANES = 768


class Wire:
    def __init__(self, extra_bits):
        self.b = lax.axis_index("batch")
        self.m = lax.axis_index("mod")
        self.core = lax.rem(self.b, 2)
        self.y = lax.rem(self.b // 2, 2)
        self.z = lax.rem(self.b // 4, 4)
        self.extra_bits = extra_bits

    def flip(self, bit):
        own = lax.rem(self.b // (1 << bit), 2)
        return (self.b + (1 - 2 * own) * (1 << bit), self.m)

    def peer(self, dim):
        if dim == "x":
            return (self.b, 1 - self.m)
        if dim == "y":
            return self.flip(1)
        if dim == "core":
            return self.flip(0)
        if dim == "up":
            return (self.b + 4, self.m)
        if dim == "down":
            return (self.b - 4, self.m)
        return self.flip(dim)

    def coord(self, dim):
        return self.m if dim == "x" else self.y

    def barrier(self):
        bar = pltpu.get_barrier_semaphore()
        peers = [self.peer(d) for d in ("core", "x", "y")]
        peers += [self.flip(bit) for bit in range(2, 4 + self.extra_bits)]
        for who in peers:
            pl.semaphore_signal(bar, inc=1, device_id=who, device_id_type=MESH)
        mid_low, mid_high = self.z == 1, self.z == 2

        @pl.when(mid_low)
        def _():
            pl.semaphore_signal(bar, inc=1, device_id=self.peer("up"), device_id_type=MESH)

        @pl.when(mid_high)
        def _():
            pl.semaphore_signal(bar, inc=1, device_id=self.peer("down"), device_id_type=MESH)

        pl.semaphore_wait(bar, len(peers) + jnp.where(mid_low | mid_high, 1, 0))


def plan_sizes(kinds, extra_bits):
    rows = sems = 0
    for kind in kinds:
        n = ROWS
        rows += ROWS
        sems += 1
        order = "xyz" if kind == "A" else "yxz" if kind == "B" else "zxy" if kind == "C" else "zyx"
        for dim in order:
            if dim == "z":
                rows += 6 * (n // 4)
                n //= 4
            else:
                rows += n // 2
                n //= 2
        rows += extra_bits * n
        sems += 6 + 6 + 4 + extra_bits + 1
    return rows, sems


def add_rows(acc, at, rb, rb_at, n):
    step = min(n, 64)

    def body(i, carry):
        d = pl.multiple_of(at + i * step, 16)
        s = pl.multiple_of(rb_at + i * step, 16)
        total = acc[pl.ds(d, step), :].astype(jnp.float32) + rb[pl.ds(s, step), :].astype(jnp.float32)
        acc[pl.ds(d, step), :] = total.astype(jnp.bfloat16)
        return carry

    if n == step:
        body(0, 0)
    else:
        lax.fori_loop(0, n // step, body, 0)


class Tasks:
    def __init__(self, wire, kinds, acc, sib, fin, rb, ssem, rsem):
        self.w, self.acc, self.sib, self.fin, self.rb = wire, acc, sib, fin, rb
        self.ssem, self.rsem = ssem, rsem
        self.rb_at = 0
        self.sem_at = 0
        self.homes = []
        self.steps = [self.build(t, kind) for t, kind in enumerate(kinds)]

    def space(self, n):
        at = self.rb_at
        self.rb_at += n
        return at

    def copy(self, src, dst, who):
        k = self.sem_at
        self.sem_at += 1
        return lambda: pltpu.make_async_remote_copy(
            src_ref=src(), dst_ref=dst(), send_sem=self.ssem.at[k], recv_sem=self.rsem.at[k], device_id=who, device_id_type=MESH
        )

    def rows(self, at, n):
        return self.acc.at[pl.ds(pl.multiple_of(at, 16), n), :]

    def build(self, t, kind):
        w = self.w
        steps = []
        home = t * ROWS
        at0 = self.space(ROWS)

        def done(at, n):
            return self.rb.at[pl.ds(pl.multiple_of(at + (at0 - home), 16), n), :]

        def keep(at, n):
            self.rb[pl.ds(pl.multiple_of(at + (at0 - home), 16), n), :] = self.acc[pl.ds(pl.multiple_of(at, 16), n), :]

        def exchange(src, dst, who, then):
            cp = self.copy(src, dst, who)

            def begin():
                cp().start()

            def finish():
                cp().wait()
                then()

            steps.append((begin, finish))

        def reduce(dim, base, n):
            half, a = n // 2, w.coord(dim)
            at = self.space(half)
            kept = base + a * half
            sent = base + (1 - a) * half
            exchange(
                lambda: self.rows(sent, half),
                lambda: self.rb.at[pl.ds(at, half), :],
                w.peer(dim),
                lambda: add_rows(self.acc, kept, self.rb, at, half),
            )
            return kept, half

        def gather(dim, base, n):
            exchange(lambda: done(base, n), lambda: done(base, n), w.peer(dim), lambda: None)

        def line_reduce(base, n):
            q, z, zz = n // 4, w.z, 3 - w.z
            for s in (1, 2, 3):
                up_at, down_at = self.space(q), self.space(q)
                up_sends, up_gets = (z < 3) & (s >= z + 1), (z >= 1) & (s >= z)
                down_sends, down_gets = (zz < 3) & (s >= zz + 1), (zz >= 1) & (s >= zz)
                up_src = base + jnp.clip(4 - s + z, 0, 3) * q
                down_src = base + jnp.clip(s + z - 4, 0, 3) * q
                up_add = base + jnp.clip(3 - s + z, 0, 3) * q
                down_add = base + jnp.clip(s - 3 + z, 0, 3) * q
                up = self.copy(lambda v=up_src: self.rows(v, q), lambda v=up_at: self.rb.at[pl.ds(v, q), :], w.peer("up"))
                down = self.copy(lambda v=down_src: self.rows(v, q), lambda v=down_at: self.rb.at[pl.ds(v, q), :], w.peer("down"))
                steps.append(line_step(up, down, up_sends, up_gets, down_sends, down_gets,
                                       lambda a=up_add, r=up_at: add_rows(self.acc, a, self.rb, r, q),
                                       lambda a=down_add, r=down_at: add_rows(self.acc, a, self.rb, r, q)))
            return base + z * q, q

        def line_gather(base, q):
            z = w.z
            for s in (1, 2, 3):
                up_sends, up_gets = (z < 3) & (z - (s - 1) >= 0), z - s >= 0
                down_sends, down_gets = (z > 0) & (z + (s - 1) <= 3), z + s <= 3
                up_src = base + jnp.clip(z - s + 1, 0, 3) * q
                down_src = base + jnp.clip(z + s - 1, 0, 3) * q
                up = self.copy(lambda v=up_src: done(v, q), lambda v=up_src: done(v, q), w.peer("up"))
                down = self.copy(lambda v=down_src: done(v, q), lambda v=down_src: done(v, q), w.peer("down"))
                steps.append(line_step(up, down, up_sends, up_gets, down_sends, down_gets, None, None))

        def line_step(up, down, up_sends, up_gets, down_sends, down_gets, up_then, down_then):
            def begin():
                @pl.when(up_sends)
                def _():
                    up().start()

                @pl.when(down_sends)
                def _():
                    down().start()

            def finish():
                for cp, gets, then in ((up, up_gets, up_then), (down, down_gets, down_then)):
                    @pl.when(gets)
                    def _(cp=cp, then=then):
                        cp().wait_recv()
                        if then is not None:
                            then()

                for cp, sends in ((up, up_sends), (down, down_sends)):
                    @pl.when(sends)
                    def _(cp=cp):
                        cp().wait_send()

            return begin, finish

        def then_keep(base, n):
            begin, finish = steps.pop()

            def finish_and_keep():
                finish()
                keep(base, n)

            steps.append((begin, finish_and_keep))

        def widen(base, n):
            for bit in range(4, 4 + w.extra_bits):
                at = self.space(n)
                exchange(
                    lambda: self.rows(base, n),
                    lambda at=at: self.rb.at[pl.ds(at, n), :],
                    w.peer(bit),
                    lambda at=at: add_rows(self.acc, base, self.rb, at, n),
                )

        exchange(
            lambda: self.sib.at[pl.ds(home, ROWS), :],
            lambda: self.rb.at[pl.ds(at0, ROWS), :],
            w.peer("core"),
            lambda: add_rows(self.acc, home, self.rb, at0, ROWS),
        )
        if kind in "AB":
            d1, d2 = ("x", "y") if kind == "A" else ("y", "x")
            b1, n1 = reduce(d1, home, ROWS)
            b2, n2 = reduce(d2, b1, n1)
            b3, n3 = line_reduce(b2, n2)
            widen(b3, n3)
            then_keep(b3, n3)
            line_gather(b2, n3)
            gather(d2, b2, n2)
            gather(d1, b1, n1)
        else:
            d1, d2 = ("x", "y") if kind == "C" else ("y", "x")
            b1, n1 = line_reduce(home, ROWS)
            b2, n2 = reduce(d1, b1, n1)
            b3, n3 = reduce(d2, b2, n2)
            widen(b3, n3)
            then_keep(b3, n3)
            gather(d2, b3, n3)
            gather(d1, b2, n2)
            line_gather(home, n1)
        exchange(
            lambda: self.rb.at[pl.ds(at0, ROWS), :],
            lambda: self.fin.at[pl.ds(home, ROWS), :],
            w.peer("core"),
            lambda: None,
        )
        self.homes.append(at0)
        return steps

    def op(self, t, p):
        steps = self.steps[t]
        if p > 0:
            steps[p - 1][1]()
        if p < len(steps):
            steps[p][0]()


KINDS = "ABCABDABCABDABCABD"
START = tuple(t // 3 for t in range(18))
SMALL = 16


def block_of(refs, half, t):
    outer, inner = refs[:2]
    if t < 6:
        return outer.at[pl.ds(pl.multiple_of(half * 1536 + t * ROWS, ROWS), ROWS), :]
    if t < 12:
        i, j = (t - 6) % 3, (t - 6) // 3
        return inner.at[pl.ds(i * ROWS, ROWS), pl.ds(pl.multiple_of((half * 2 + j) * LANES, LANES), LANES)]
    return None


def attn_block(refs, half, t):
    ref = refs[2 + 2 * half + (t - 12) // 3]
    return ref.at[pl.ds((t - 12) % 3 * ROWS, ROWS), :]


class Branches:
    def __init__(self, core, first, second):
        self.core, self.first, self.second = core, first, second

    def start(self):
        for core, copy in ((0, self.first), (1, self.second)):
            @pl.when(self.core == core)
            def _(copy=copy):
                copy().start()

    def wait(self):
        self.first().wait()


def sum_kernel(extra_bits, *refs):
    ins, vectors, refs = refs[:6], refs[6:15], refs[15:]
    outs, small_out, refs = refs[:6], refs[6], refs[7:]
    acc, sib, fin, rb, small, small_rb, ssem, rsem, lsem, vsem = refs
    w = Wire(extra_bits)
    count = len(KINDS)

    def block_copy(arrays, own, t, buf, outward, sem):
        def copy(block):
            return pltpu.make_async_copy(buf, block, sem) if outward else pltpu.make_async_copy(block, buf, sem)

        if t < 12:
            return copy(block_of(arrays, w.core if own else 1 - w.core, t))
        low, high = attn_block(arrays, 0, t), attn_block(arrays, 1, t)
        return Branches(w.core, lambda: copy(low if own else high), lambda: copy(high if own else low))

    def load(t, who):
        buf = (acc, sib)[who].at[pl.ds(t * ROWS, ROWS), :]
        return block_copy(ins, who == 0, t, buf, False, lsem.at[2 * t + who])

    def store(t, who):
        source = rb.at[pl.ds(tasks.homes[t], ROWS), :] if who == 0 else fin.at[pl.ds(t * ROWS, ROWS), :]
        return block_copy(outs, who == 0, t, source, True, lsem.at[2 * t + who])

    for t in range(count):
        load(t, 1).start()
        load(t, 0).start()
    w.barrier()
    tasks = Tasks(w, KINDS, acc, sib, fin, rb, ssem, rsem)

    for at, ref in enumerate(vectors):
        for i in range(ref.shape[1] // LANES):
            small[0, at + i:at + i + 1, :] = ref[:, i * LANES:(i + 1) * LANES]
    small[0, 12:16, :] = jnp.zeros((4, LANES), jnp.float32)
    hops = ["core", "x", "y"] + list(range(2, 4 + extra_bits))

    def small_copy(k):
        return pltpu.make_async_remote_copy(
            src_ref=small.at[k], dst_ref=small_rb.at[k], send_sem=vsem.at[0, k], recv_sem=vsem.at[1, k],
            device_id=w.peer(hops[k]), device_id_type=MESH)

    def small_op(k):
        if k > 0:
            small_copy(k - 1).wait()
            small[k] = small[k - 1] + small_rb[k - 1]
        if k < len(hops):
            small_copy(k).start()

    ops = [(START[t] + p, t, p) for t in range(count) for p in range(len(tasks.steps[t]) + 1)]
    ops += [(k + 1, count, k) for k in range(len(hops) + 1)]
    for _, t, p in sorted(ops):
        if t == count:
            small_op(p)
            continue
        if p == 0:
            load(t, 1).wait()
        if p == 1:
            load(t, 0).wait()
        tasks.op(t, p)
        if p == len(tasks.steps[t]):
            store(t, 0).start()
            store(t, 1).start()
    small_out[...] = small[len(hops)]
    for t in range(count):
        store(t, 0).wait()
        store(t, 1).wait()


def sum_gradients(matrices, vectors):
    extra_bits = (lax.axis_size("batch") // 16).bit_length() - 1
    rows, sems = plan_sizes(KINDS, extra_bits)
    hops = 5 + extra_bits
    count = len(KINDS)
    hbm = pl.BlockSpec(memory_space=pl.ANY)
    vmem = pl.BlockSpec(memory_space=pltpu.VMEM)
    return pl.pallas_call(
        functools.partial(sum_kernel, extra_bits),
        out_shape=tuple(jax.ShapeDtypeStruct(m.shape, jnp.bfloat16) for m in matrices)
        + (jax.ShapeDtypeStruct((SMALL, LANES), jnp.float32),),
        in_specs=[hbm] * len(matrices) + [vmem] * len(vectors),
        out_specs=(hbm,) * len(matrices) + (vmem,),
        scratch_shapes=[
            pltpu.VMEM((count * ROWS, LANES), jnp.bfloat16),
            pltpu.VMEM((count * ROWS, LANES), jnp.bfloat16),
            pltpu.VMEM((count * ROWS, LANES), jnp.bfloat16),
            pltpu.VMEM((rows, LANES), jnp.bfloat16),
            pltpu.VMEM((hops + 1, SMALL, LANES), jnp.float32),
            pltpu.VMEM((hops, SMALL, LANES), jnp.float32),
            pltpu.SemaphoreType.DMA((sems,)),
            pltpu.SemaphoreType.DMA((sems,)),
            pltpu.SemaphoreType.DMA((2 * count,)),
            pltpu.SemaphoreType.DMA((2, hops)),
        ],
        compiler_params=pltpu.CompilerParams(collective_id=1, has_side_effects=True, vmem_limit_bytes=60 << 20),
    )(*matrices, *vectors)


def nt(a, b):
    return lax.dot_general(a, b, (((1,), (1,)), ((), ())), preferred_element_type=jnp.float32)


def nn(a, b):
    return lax.dot_general(a, b, (((1,), (0,)), ((), ())), preferred_element_type=jnp.float32)


def low_lanes(rows):
    return lax.broadcasted_iota(jnp.int32, (rows, 128), 1) < 64


def attend_pair(q, k, v, bias):
    low = low_lanes(k.shape[0])
    zero = jnp.zeros_like(k)
    vt = v.T
    parts, sums = [], []
    for head in range(2):
        own = jnp.where(low if head == 0 else ~low, k, zero)
        scores = nt(own, q) + bias
        top = jnp.max(scores, axis=0, keepdims=True)
        expo = jnp.exp(scores - top)
        total = jnp.sum(expo, axis=0, keepdims=True)
        parts.append(nn(vt[head * 64:head * 64 + 64], expo.astype(jnp.bfloat16)) * (1.0 / total))
        sums.append(top + jnp.log(total))
    return jnp.concatenate(parts, axis=0).T.astype(jnp.bfloat16), jnp.concatenate(sums, axis=0)


def attend_pair_back(q, k, v, dc, lse, bias):
    low = low_lanes(k.shape[0])
    zero = jnp.zeros_like(k)
    kt = k.T
    dq, dk, dv = [], [], []
    for head in range(2):
        mine = low if head == 0 else ~low
        probs = jnp.exp(nt(jnp.where(mine, k, zero), q) + (bias - lse[head:head + 1]))
        d_probs = nt(jnp.where(mine, v, zero), dc)
        inner = jnp.sum(probs * d_probs, axis=0, keepdims=True)
        d_scores = (probs * (d_probs - inner)).astype(jnp.bfloat16)
        dq.append(nn(kt[head * 64:head * 64 + 64], d_scores))
        dk.append(nn(d_scores, q))
        dv.append(nn(probs.astype(jnp.bfloat16), dc))
    d_query = (jnp.concatenate(dq, axis=0) * 0.125).T.astype(jnp.bfloat16)
    d_key = jnp.where(low, dk[0], dk[1]).astype(jnp.bfloat16)
    d_value = jnp.where(low, dv[0], dv[1]).astype(jnp.bfloat16)
    return d_query, d_key, d_value


def attend_kernel(q_ref, k_ref, v_ref, bias_ref, ctx_ref, lse_ref):
    bias = jnp.concatenate([bias_ref[...]] * (q_ref.shape[0] // 128), axis=1)
    ctx_ref[...], lse_ref[0, 0] = attend_pair(q_ref[...], k_ref[...], v_ref[...], bias)


def attend_back_kernel(q_ref, k_ref, v_ref, dc_ref, lse_ref, bias_ref, dq_ref, dk_ref, dv_ref):
    bias = jnp.concatenate([bias_ref[...]] * (q_ref.shape[0] // 128), axis=1)
    dq_ref[...], dk_ref[...], dv_ref[...] = attend_pair_back(
        q_ref[...], k_ref[...], v_ref[...], dc_ref[...], lse_ref[0, 0], bias)


def attend(q, k, v, bias, length):
    rows, width = q.shape
    seqs, pairs = rows // length, width // 128
    block = pl.BlockSpec((length, 128), lambda s, p: (s, p))
    mask = pl.BlockSpec((length, 128), lambda s, p: (s, 0))
    lse = pl.BlockSpec((1, 1, 2, length), lambda s, p: (s, p, 0, 0))
    return pl.pallas_call(
        attend_kernel,
        grid=(seqs, pairs),
        out_shape=(jax.ShapeDtypeStruct(q.shape, jnp.bfloat16), jax.ShapeDtypeStruct((seqs, pairs, 2, length), jnp.float32)),
        in_specs=[block, block, block, mask],
        out_specs=(block, lse),
    )(q, k, v, bias)


def attend_back(q, k, v, dc, lse, bias, length):
    rows, width = q.shape
    seqs, pairs = rows // length, width // 128
    block = pl.BlockSpec((length, 128), lambda s, p: (s, p))
    mask = pl.BlockSpec((length, 128), lambda s, p: (s, 0))
    lse_spec = pl.BlockSpec((1, 1, 2, length), lambda s, p: (s, p, 0, 0))
    return pl.pallas_call(
        attend_back_kernel,
        grid=(seqs, pairs),
        out_shape=tuple(jax.ShapeDtypeStruct(q.shape, jnp.bfloat16) for _ in range(3)),
        in_specs=[block, block, block, block, lse_spec, mask],
        out_specs=(block, block, block),
    )(q, k, v, dc, lse, bias)


epsilon = 1e-05


def to_partner(block):
    return lax.ppermute(block, "mod", [(0, 1), (1, 0)])


def take_side(array, axis, side):
    half = array.shape[axis] // 2
    return lax.dynamic_slice_in_dim(array, side * half, half, axis)


def gather_sequences(array, side):
    own = take_side(array, 0, side)
    other = to_partner(take_side(array, 0, 1 - side))
    both = jnp.where(side == 0, jnp.concatenate((own, other), axis=1), jnp.concatenate((other, own), axis=1))
    return both.reshape(-1, array.shape[2])


def return_rows(array, side):
    own = take_side(array, 1, side)
    other = to_partner(take_side(array, 1, 1 - side))
    return jnp.where(side == 0, jnp.concatenate((own, other)), jnp.concatenate((other, own)))


def linear(rows, weight_matrix):
    return lax.dot_general(rows, weight_matrix, (((1,), (0,)), ((), ())), preferred_element_type=jnp.float32)


def back_linear(gradient_rows, weight_matrix):
    return lax.dot_general(gradient_rows, weight_matrix, (((1,), (1,)), ((), ())), preferred_element_type=jnp.float32)


def weight_grad(layer_inputs, gradient_rows):
    return lax.dot_general(
        layer_inputs, gradient_rows, (((0,), (0,)), ((), ())), preferred_element_type=jnp.float32
    ).astype(jnp.bfloat16)


def row_total(values):
    return jnp.sum(values.astype(jnp.float32), axis=0, keepdims=True)


def layer_norm(rows):
    centre = rows - jnp.mean(rows, axis=-1, keepdims=True)
    factor = lax.rsqrt(jnp.mean(centre * centre, axis=-1, keepdims=True) + epsilon)
    return (centre * factor, factor)


def norm_back(gradient_rows, normed, factor):
    return factor * (
        gradient_rows
        - jnp.mean(gradient_rows, axis=-1, keepdims=True)
        - normed * jnp.mean(gradient_rows * normed, axis=-1, keepdims=True)
    )


def on_device(
    hidden_in,
    text_mask,
    region_count,
    w_query,
    b_query,
    w_key,
    w_value,
    b_value,
    w_attn_out,
    b_attn_out,
    gain_attn,
    shift_attn,
    w_inner,
    b_inner,
    w_outer,
    b_outer,
    gain_ffn,
    shift_ffn,
    cotangent,
):
    seq_count, half_len, width = hidden_in.shape
    length = 2 * half_len
    side = lax.axis_index("mod")
    f32 = jnp.float32
    rows_b = gather_sequences(hidden_in, side)
    upstream = gather_sequences(cotangent, side).astype(f32)
    mask = take_side(text_mask, 0, side) == 1
    regions = take_side(region_count, 0, side)
    slot_ok = lax.broadcasted_iota(jnp.int32, mask.shape, 1) < regions[:, None]
    bias = jnp.where(jnp.concatenate((mask, slot_ok), axis=1), f32(0.0), f32(-1000000000.0)).reshape(-1, 1)
    bias = jnp.broadcast_to(bias, (bias.shape[0], 128))

    query_b = ((linear(rows_b, w_query) + b_query.astype(f32)).astype(jnp.bfloat16) * jnp.bfloat16(0.125))
    key_b = linear(rows_b, w_key).astype(jnp.bfloat16)
    value_b = (linear(rows_b, w_value) + b_value.astype(f32)).astype(jnp.bfloat16)
    context_b, lse = attend(query_b, key_b, value_b, bias, length)
    branch = linear(context_b, w_attn_out) + b_attn_out.astype(f32)
    normed_one, factor_one = layer_norm(rows_b.astype(f32) + branch)
    middle = normed_one * gain_attn.astype(f32) + shift_attn.astype(f32)
    middle_b = middle.astype(jnp.bfloat16)
    pre_act = linear(middle_b, w_inner) + b_inner.astype(f32)
    activ, gelu_back = jax.vjp(lambda values: jax.nn.gelu(values, approximate=False), pre_act)
    activ_b = activ.astype(jnp.bfloat16)
    ffn_out = linear(activ_b, w_outer) + b_outer.astype(f32)
    normed_two, factor_two = layer_norm(middle + ffn_out)
    layer_out = (normed_two * gain_ffn.astype(f32) + shift_ffn.astype(f32)).astype(jnp.bfloat16)
    layer_out = return_rows(layer_out.reshape(seq_count // 2, length, width), side)
    grad_gain_ffn = row_total(upstream * normed_two)
    grad_shift_ffn = row_total(upstream)
    d_res_two = norm_back(upstream * gain_ffn.astype(f32), normed_two, factor_two)
    d_ffn_b = d_res_two.astype(jnp.bfloat16)
    grad_b_outer = row_total(d_ffn_b)
    grad_w_outer = weight_grad(activ_b, d_ffn_b)
    d_activ = back_linear(d_ffn_b, w_outer)
    d_pre_b = gelu_back(d_activ)[0].astype(jnp.bfloat16)
    grad_b_inner = row_total(d_pre_b)
    grad_w_inner = weight_grad(middle_b, d_pre_b)
    d_middle = d_res_two + back_linear(d_pre_b, w_inner)
    grad_gain_attn = row_total(d_middle * normed_one)
    grad_shift_attn = row_total(d_middle)
    d_res_one = norm_back(d_middle * gain_attn.astype(f32), normed_one, factor_one)
    d_branch_b = d_res_one.astype(jnp.bfloat16)
    grad_b_attn_out = row_total(d_branch_b)
    grad_w_attn_out = weight_grad(context_b, d_branch_b)
    d_context_b = back_linear(d_branch_b, w_attn_out).astype(jnp.bfloat16)
    d_query_b, d_key_b, d_value_b = attend_back(query_b, key_b, value_b, d_context_b, lse, bias, length)
    grad_b_query = row_total(d_query_b)
    grad_b_value = row_total(d_value_b)
    input_grad = (
        d_res_one
        + back_linear(d_query_b, w_query)
        + back_linear(d_key_b, w_key)
        + back_linear(d_value_b, w_value)
    ).astype(jnp.bfloat16)
    input_grad = return_rows(input_grad.reshape(seq_count // 2, length, width), side)
    sums = sum_gradients(
        (
            grad_w_outer,
            grad_w_inner,
            weight_grad(rows_b, d_query_b),
            weight_grad(rows_b, d_key_b),
            weight_grad(rows_b, d_value_b),
            grad_w_attn_out,
        ),
        (
            grad_b_query, grad_b_value, grad_b_attn_out, grad_gain_attn, grad_shift_attn, grad_b_outer,
            grad_gain_ffn, grad_shift_ffn, grad_b_inner,
        ),
    )
    s_outer, s_inner, s_query, s_key, s_value, s_attn_out, small = sums
    return (
        layer_out,
        input_grad,
        s_query.astype(f32),
        small[0],
        s_key.astype(f32),
        s_value.astype(f32),
        small[1],
        s_attn_out.astype(f32),
        small[2],
        small[3],
        small[4],
        s_inner.astype(f32),
        small[8:12].reshape(-1),
        s_outer.astype(f32),
        small[5],
        small[6],
        small[7],
    )


def solution(mesh):
    in_specs = (
        P("batch", "mod", None),
        P("batch", None),
        P("batch"),
        P(),
        P(),
        P(),
        P(),
        P(),
        P(),
        P(),
        P(),
        P(),
        P(),
        P(),
        P(),
        P(),
        P(),
        P(),
        P("batch", "mod", None),
    )
    out_specs = (
        P("batch", "mod", None),
        P("batch", "mod", None),
        P(),
        P(),
        P(),
        P(),
        P(),
        P(),
        P(),
        P(),
        P(),
        P(),
        P(),
        P(),
        P(),
        P(),
        P(),
    )
    return jax.shard_map(
        on_device, mesh=mesh, in_specs=in_specs, out_specs=out_specs, check_vma=False
    )
```

```python
import functools

import jax
import jax.numpy as jnp
from jax import lax
from jax.experimental import pallas as pl
from jax.experimental.pallas import tpu as pltpu
from jax.sharding import PartitionSpec as P

MESH = pl.DeviceIdType.MESH
ROWS = 256
LANES = 768


class Wire:
    def __init__(self, extra_bits):
        self.b = lax.axis_index("batch")
        self.m = lax.axis_index("mod")
        self.core = lax.rem(self.b, 2)
        self.y = lax.rem(self.b // 2, 2)
        self.z = lax.rem(self.b // 4, 4)
        self.extra_bits = extra_bits

    def flip(self, bit):
        own = lax.rem(self.b // (1 << bit), 2)
        return (self.b + (1 - 2 * own) * (1 << bit), self.m)

    def peer(self, dim):
        if dim == "x":
            return (self.b, 1 - self.m)
        if dim == "y":
            return self.flip(1)
        if dim == "core":
            return self.flip(0)
        if dim == "up":
            return (self.b + 4, self.m)
        if dim == "down":
            return (self.b - 4, self.m)
        return self.flip(dim)

    def coord(self, dim):
        return self.m if dim == "x" else self.y

    def barrier(self):
        bar = pltpu.get_barrier_semaphore()
        peers = [self.peer(d) for d in ("core", "x", "y")]
        peers += [self.flip(bit) for bit in range(2, 4 + self.extra_bits)]
        for who in peers:
            pl.semaphore_signal(bar, inc=1, device_id=who, device_id_type=MESH)
        mid_low, mid_high = self.z == 1, self.z == 2

        @pl.when(mid_low)
        def _():
            pl.semaphore_signal(bar, inc=1, device_id=self.peer("up"), device_id_type=MESH)

        @pl.when(mid_high)
        def _():
            pl.semaphore_signal(bar, inc=1, device_id=self.peer("down"), device_id_type=MESH)

        pl.semaphore_wait(bar, len(peers) + jnp.where(mid_low | mid_high, 1, 0))


def plan_sizes(kinds, extra_bits):
    rows = sems = 0
    for kind in kinds:
        n = ROWS
        rows += ROWS
        sems += 1
        order = "xyz" if kind == "A" else "yxz" if kind == "B" else "zxy" if kind == "C" else "zyx"
        for dim in order:
            if dim == "z":
                rows += 6 * (n // 4)
                n //= 4
            else:
                rows += n // 2
                n //= 2
        rows += extra_bits * n
        sems += 6 + 6 + 4 + extra_bits + 1
    return rows, sems


def add_rows(acc, at, rb, rb_at, n):
    step = min(n, 64)

    def body(i, carry):
        d = pl.multiple_of(at + i * step, 16)
        s = pl.multiple_of(rb_at + i * step, 16)
        total = acc[pl.ds(d, step), :].astype(jnp.float32) + rb[pl.ds(s, step), :].astype(jnp.float32)
        acc[pl.ds(d, step), :] = total.astype(jnp.bfloat16)
        return carry

    if n == step:
        body(0, 0)
    else:
        lax.fori_loop(0, n // step, body, 0)


class Tasks:
    def __init__(self, wire, kinds, part, rb, ssem, rsem, block):
        self.w, self.acc, self.rb, self.block = wire, part, rb, block
        self.ssem, self.rsem = ssem, rsem
        self.rb_at = 0
        self.sem_at = 0
        self.homes = []
        self.steps = [self.build(t, kind) for t, kind in enumerate(kinds)]

    def space(self, n):
        at = self.rb_at
        self.rb_at += n
        return at

    def copy(self, src, dst, who):
        k = self.sem_at
        self.sem_at += 1
        return lambda: pltpu.make_async_remote_copy(
            src_ref=src(), dst_ref=dst(), send_sem=self.ssem.at[k], recv_sem=self.rsem.at[k], device_id=who, device_id_type=MESH
        )

    def rows(self, at, n):
        return self.acc.at[pl.ds(pl.multiple_of(at, 16), n), :]

    def build(self, t, kind):
        w = self.w
        steps = []
        home = (w.core * len(KINDS) + t) * ROWS
        away = ((1 - w.core) * len(KINDS) + t) * ROWS
        at0 = self.space(ROWS)

        def done(at, n):
            return self.rb.at[pl.ds(pl.multiple_of(at + (at0 - home), 16), n), :]

        def keep(at, n):
            self.rb[pl.ds(pl.multiple_of(at + (at0 - home), 16), n), :] = self.acc[pl.ds(pl.multiple_of(at, 16), n), :]

        def exchange(src, dst, who, then):
            cp = self.copy(src, dst, who)

            def begin():
                cp().start()

            def finish():
                cp().wait()
                then()

            steps.append((begin, finish))

        def reduce(dim, base, n):
            half, a = n // 2, w.coord(dim)
            at = self.space(half)
            kept = base + a * half
            sent = base + (1 - a) * half
            exchange(
                lambda: self.rows(sent, half),
                lambda: self.rb.at[pl.ds(at, half), :],
                w.peer(dim),
                lambda: add_rows(self.acc, kept, self.rb, at, half),
            )
            return kept, half

        def gather(dim, base, n):
            exchange(lambda: done(base, n), lambda: done(base, n), w.peer(dim), lambda: None)

        def line_reduce(base, n):
            q, z, zz = n // 4, w.z, 3 - w.z
            for s in (1, 2, 3):
                up_at, down_at = self.space(q), self.space(q)
                up_sends, up_gets = (z < 3) & (s >= z + 1), (z >= 1) & (s >= z)
                down_sends, down_gets = (zz < 3) & (s >= zz + 1), (zz >= 1) & (s >= zz)
                up_src = base + jnp.clip(4 - s + z, 0, 3) * q
                down_src = base + jnp.clip(s + z - 4, 0, 3) * q
                up_add = base + jnp.clip(3 - s + z, 0, 3) * q
                down_add = base + jnp.clip(s - 3 + z, 0, 3) * q
                up = self.copy(lambda v=up_src: self.rows(v, q), lambda v=up_at: self.rb.at[pl.ds(v, q), :], w.peer("up"))
                down = self.copy(lambda v=down_src: self.rows(v, q), lambda v=down_at: self.rb.at[pl.ds(v, q), :], w.peer("down"))
                steps.append(line_step(up, down, up_sends, up_gets, down_sends, down_gets,
                                       lambda a=up_add, r=up_at: add_rows(self.acc, a, self.rb, r, q),
                                       lambda a=down_add, r=down_at: add_rows(self.acc, a, self.rb, r, q)))
            return base + z * q, q

        def line_gather(base, q):
            z = w.z
            for s in (1, 2, 3):
                up_sends, up_gets = (z < 3) & (z - (s - 1) >= 0), z - s >= 0
                down_sends, down_gets = (z > 0) & (z + (s - 1) <= 3), z + s <= 3
                up_src = base + jnp.clip(z - s + 1, 0, 3) * q
                down_src = base + jnp.clip(z + s - 1, 0, 3) * q
                up = self.copy(lambda v=up_src: done(v, q), lambda v=up_src: done(v, q), w.peer("up"))
                down = self.copy(lambda v=down_src: done(v, q), lambda v=down_src: done(v, q), w.peer("down"))
                steps.append(line_step(up, down, up_sends, up_gets, down_sends, down_gets, None, None))

        def line_step(up, down, up_sends, up_gets, down_sends, down_gets, up_then, down_then):
            def begin():
                @pl.when(up_sends)
                def _():
                    up().start()

                @pl.when(down_sends)
                def _():
                    down().start()

            def finish():
                for cp, gets, then in ((up, up_gets, up_then), (down, down_gets, down_then)):
                    @pl.when(gets)
                    def _(cp=cp, then=then):
                        cp().wait_recv()
                        if then is not None:
                            then()

                for cp, sends in ((up, up_sends), (down, down_sends)):
                    @pl.when(sends)
                    def _(cp=cp):
                        cp().wait_send()

            return begin, finish

        def then_keep(base, n):
            begin, finish = steps.pop()

            def finish_and_keep():
                finish()
                keep(base, n)

            steps.append((begin, finish_and_keep))

        def widen(base, n):
            for bit in range(4, 4 + w.extra_bits):
                at = self.space(n)
                exchange(
                    lambda: self.rows(base, n),
                    lambda at=at: self.rb.at[pl.ds(at, n), :],
                    w.peer(bit),
                    lambda at=at: add_rows(self.acc, base, self.rb, at, n),
                )

        exchange(
            lambda: self.rows(away, ROWS),
            lambda: self.rb.at[pl.ds(at0, ROWS), :],
            w.peer("core"),
            lambda: add_rows(self.acc, home, self.rb, at0, ROWS),
        )
        if kind in "AB":
            d1, d2 = ("x", "y") if kind == "A" else ("y", "x")
            b1, n1 = reduce(d1, home, ROWS)
            b2, n2 = reduce(d2, b1, n1)
            b3, n3 = line_reduce(b2, n2)
            widen(b3, n3)
            then_keep(b3, n3)
            line_gather(b2, n3)
            gather(d2, b2, n2)
            gather(d1, b1, n1)
        else:
            d1, d2 = ("x", "y") if kind == "C" else ("y", "x")
            b1, n1 = line_reduce(home, ROWS)
            b2, n2 = reduce(d1, b1, n1)
            b3, n3 = reduce(d2, b2, n2)
            widen(b3, n3)
            then_keep(b3, n3)
            gather(d2, b3, n3)
            gather(d1, b2, n2)
            line_gather(home, n1)
        k = self.sem_at
        self.sem_at += 1

        def last(block):
            return pltpu.make_async_remote_copy(
                src_ref=self.rb.at[pl.ds(at0, ROWS), :], dst_ref=block, send_sem=self.ssem.at[k], recv_sem=self.rsem.at[k],
                device_id=w.peer("core"), device_id_type=MESH)

        final = by_core(w.core, lambda half: last(self.block(half, t)), t)
        steps.append((lambda: final.start(), lambda: final.wait()))
        self.homes.append(at0)
        return steps

    def op(self, t, p):
        steps = self.steps[t]
        if p > 0:
            steps[p - 1][1]()
        if p < len(steps):
            steps[p][0]()


KINDS = "ABCABDABCABDABCABD"
START = tuple((0, 1, 2, 4, 8, 9)[t // 3] for t in range(18))
SMALL = 16
SMALL_START = 10
LAG = 1


def block_of(refs, half, t):
    if t < 6:
        return refs[0].at[pl.ds(pl.multiple_of(half * 1536 + t * ROWS, ROWS), ROWS), :]
    if t < 12:
        i, j = (t - 6) % 3, (t - 6) // 3
        return refs[1].at[pl.ds(i * ROWS, ROWS), pl.ds(pl.multiple_of((half * 2 + j) * LANES, LANES), LANES)]
    return refs[2 + 2 * half + (t - 12) // 3].at[pl.ds((t - 12) % 3 * ROWS, ROWS), :]


class Branches:
    def __init__(self, core, make):
        self.core, self.make = core, make

    def start(self):
        for core in range(2):
            @pl.when(self.core == core)
            def _(core=core):
                self.make(core).start()

    def wait(self):
        self.make(0).wait()


class Plain:
    def __init__(self, make):
        self.make = make

    def start(self):
        self.make().start()

    def wait(self):
        self.make().wait()


def by_core(core, make, t):
    return Plain(lambda: make(core)) if t < 12 else Branches(core, make)


def tn(a, b):
    return lax.dot_general(a, b, (((0,), (0,)), ((), ())), preferred_element_type=jnp.float32)


FULL = ("q", "k", "v", "ctx", "x", "mid", "dffn", "dmid", "normed", "wq", "wk", "wv", "wo")


def back_kernel(extra_bits, *refs):
    g_outer, w_outer, w_inner, slope, *refs = refs
    full_in, refs = dict(zip(FULL, refs)), refs[len(FULL):]
    factor, gain, lse, bias_ref, sum_outer, sum_gain, sum_shift, *refs = refs
    outs, small_out, grad_out, refs = refs[:6], refs[6], refs[7], refs[8:]
    v, refs = dict(zip(FULL, refs)), refs[len(FULL):]
    wou, win, gp, dp, dc, db, dq, dk, dv, ig, part, rb, small, small_rb, ssem, rsem, lsem, vsem, fsem, tsem, osem, isem = refs
    w = Wire(extra_bits)
    count = len(KINDS)
    f32 = jnp.float32
    rows = dp.shape[0]
    length = bias_ref.shape[0] // lse.shape[0]
    order = (0, 2, 1, 3)

    def load(half, t):
        to = part.at[pl.ds((half * count + t) * ROWS, ROWS), :]
        return pltpu.make_async_copy(g_outer.at[pl.ds(half * 1536 + t * ROWS, ROWS), :], to, lsem.at[half, t])

    def fetch(name):
        return pltpu.make_async_copy(full_in[name], v[name], fsem.at[FULL.index(name)])

    def tile(which, n):
        at, slot = order[n] * LANES, n % 2
        source, to = (
            (w_outer.at[pl.ds(at, LANES), :], wou),
            (w_inner.at[:, pl.ds(at, LANES)], win),
            (slope.at[:, pl.ds(at, LANES)], gp),
        )[which]
        return pltpu.make_async_copy(source, to.at[slot], tsem.at[which, n])

    for t in range(6):
        load(0, t).start()
        load(1, t).start()
        if t == 0:
            fetch("dffn").start()
            tile(0, 0).start()
            tile(2, 0).start()
            fetch("mid").start()
            tile(1, 0).start()
            fetch("dmid").start()
    for which in range(3):
        tile(which, 1).start()
    for name in ("normed", "wo", "ctx", "k", "q", "v", "x", "wq", "wk", "wv"):
        fetch(name).start()
    w.barrier()
    tasks = Tasks(w, KINDS, part, rb, ssem, rsem, lambda half, t: block_of(outs, half, t))

    def store(t):
        def make(half):
            return pltpu.make_async_copy(rb.at[pl.ds(tasks.homes[t], ROWS), :], block_of(outs, half, t), osem.at[t])

        return by_core(w.core, make, t)

    def grad_blocks(left, right, half, t):
        def body(i, carry):
            columns = pl.ds(pl.multiple_of(i * ROWS, ROWS), ROWS)
            to = pl.ds(pl.multiple_of((half * count + t + i) * ROWS, ROWS), ROWS)
            part[to, :] = tn(left[:, columns], right[...]).astype(jnp.bfloat16)
            return carry

        lax.fori_loop(0, LANES // ROWS, body, 0)

    def by_rows(step, body, carry=0):
        def wrapped(r, carry):
            return body(pl.ds(pl.multiple_of(r * step, step), step), carry)

        return lax.fori_loop(0, rows // step, wrapped, carry)

    none = jnp.zeros((1, LANES), f32)

    def d_pre(n):
        tile(0, n).wait()
        tile(2, n).wait()
        if n == 0:
            fetch("dffn").wait()

        def body(at, total):
            d = (nt(v["dffn"][at, :], wou[n % 2]) * gp[n % 2, at, :].astype(f32)).astype(jnp.bfloat16)
            dp[at, :] = d
            return total + jnp.sum(d.astype(f32), axis=0, keepdims=True)

        small[0, 8 + order[n]:9 + order[n], :] = by_rows(128, body, none)
        if n + 2 < 4:
            tile(0, n + 2).start()
            tile(2, n + 2).start()

    def inner_blocks(n):
        if n == 0:
            fetch("mid").wait()
        grad_blocks(v["mid"], dp, order[n] // 2, 6 + 3 * (order[n] % 2))

    def d_mid(n):
        tile(1, n).wait()
        if n == 0:
            fetch("dmid").wait()

        def body(at, carry):
            v["dmid"][at, :] += nt(dp[at, :], win[n % 2])
            return carry

        by_rows(128, body)
        if n + 2 < 4:
            tile(1, n + 2).start()

    def norm_step():
        fetch("normed").wait()

        def body(at, sums):
            d, normed = v["dmid"][at, :], v["normed"][at, :]
            e = d * gain[...]
            res = factor[at, :] * (
                e - jnp.mean(e, axis=-1, keepdims=True) - normed * jnp.mean(e * normed, axis=-1, keepdims=True)
            )
            low = res.astype(jnp.bfloat16)
            v["dmid"][at, :] = res
            db[at, :] = low
            return (
                sums[0] + jnp.sum(low.astype(f32), axis=0, keepdims=True),
                sums[1] + jnp.sum(d * normed, axis=0, keepdims=True),
                sums[2] + jnp.sum(d, axis=0, keepdims=True),
            )

        sums = by_rows(64, body, (none, none, none))
        for i in range(3):
            small[0, 2 + i:3 + i, :] = sums[i]

    def d_context():
        fetch("wo").wait()

        def body(i, carry):
            at = pl.ds(pl.multiple_of(i * 256, 256), 256)
            dc[:, at] = nt(db[...], v["wo"][at, :]).astype(jnp.bfloat16)
            return carry

        lax.fori_loop(0, LANES // 256, body, 0)

    def out_blocks():
        fetch("ctx").wait()
        grad_blocks(v["ctx"], db, 1, 15)

    def attention(seq, first, pairs):
        if seq == 0 and first == 0:
            for name in ("q", "k", "v"):
                fetch(name).wait()
        at = pl.ds(seq * length, length)
        bias = jnp.concatenate([bias_ref[at, :]] * (length // 128), axis=1)

        def body(p, carry):
            c = pl.ds(pl.multiple_of(p * 128, 128), 128)
            dq[at, c], dk[at, c], dv[at, c] = attend_pair_back(
                v["q"][at, c], v["k"][at, c], v["v"][at, c], dc[at, c], lse[seq, p], bias)
            return carry

        lax.fori_loop(first, first + pairs, body, 0)

    def total_rows(ref, row):
        def body(at, total):
            return total + jnp.sum(ref[at, :].astype(f32), axis=0, keepdims=True)

        small[0, row:row + 1, :] = by_rows(128, body, none)

    def value_blocks():
        grad_blocks(v["x"], dv, 1, 12)
        total_rows(dv, 1)

    def query_blocks():
        fetch("x").wait()
        grad_blocks(v["x"], dq, 0, 12)
        total_rows(dq, 0)

    def key_blocks():
        grad_blocks(v["x"], dk, 0, 15)

    def grad_copy(seq, away):
        source = ig.at[2 * seq + (1 - w.m if away else w.m)]
        to = grad_out.at[w.m * lse.shape[0] + seq]
        if not away:
            return pltpu.make_async_copy(source, to, isem.at[2, seq])
        return pltpu.make_async_remote_copy(
            src_ref=source, dst_ref=to, send_sem=isem.at[0, seq], recv_sem=isem.at[1, seq],
            device_id=w.peer("x"), device_id_type=MESH)

    def input_rows(seq):
        if seq == 0:
            for name in ("wq", "wk", "wv"):
                fetch(name).wait()

        def body(i, carry):
            at = pl.ds(pl.multiple_of(i * 128, 128), 128)
            total = v["dmid"][at, :] + nt(dq[at, :], v["wq"][...])
            total = total + nt(dk[at, :], v["wk"][...]) + nt(dv[at, :], v["wv"][...])
            ig[i] = total.astype(jnp.bfloat16)
            return carry

        lax.fori_loop(2 * seq, 2 * seq + 2, body, 0)
        grad_copy(seq, True).start()
        grad_copy(seq, False).start()

    small[0, 12:16, :] = jnp.zeros((4, LANES), f32)
    for row, ref in ((5, sum_outer), (6, sum_gain), (7, sum_shift)):
        small[0, row:row + 1, :] = ref[...]
    hops = ["core", "x", "y"] + list(range(2, 4 + extra_bits))

    def small_copy(k):
        return pltpu.make_async_remote_copy(
            src_ref=small.at[k], dst_ref=small_rb.at[k], send_sem=vsem.at[0, k], recv_sem=vsem.at[1, k],
            device_id=w.peer(hops[k]), device_id_type=MESH)

    def small_op(k):
        if k > 0:
            small_copy(k - 1).wait()
            small[k] = small[k - 1] + small_rb[k - 1]
        if k < len(hops):
            small_copy(k).start()

    seqs, pairs = lse.shape[:2]
    work = [[(d_pre, n), (inner_blocks, n), (d_mid, n)] for n in range(4)]
    work.append([(norm_step,), (d_context,), (out_blocks,)])
    attn = [(attention, seq, first, 2) for seq in range(seqs) for first in range(0, pairs, 2)]
    half = len(attn) // 2
    work += [attn[:half], attn[half:], [(query_blocks,), (value_blocks,), (key_blocks,)]]
    work.append([(input_rows, seq) for seq in range(seqs)])

    def comm(t, p):
        if t == count:
            small_op(p)
            return
        if p == 0 and t < 6:
            load(0, t).wait()
            load(1, t).wait()
        tasks.op(t, p)
        if p == len(tasks.steps[t]) - 1:
            store(t).start()

    ops = [(START[t] + p, t, p) for t in range(count) for p in range(len(tasks.steps[t]) + 1)]
    ops += [(SMALL_START + k, count, k) for k in range(len(hops) + 1)]
    for slot in range(max(op[0] for op in ops) + 1):
        now = sorted(op for op in ops if op[0] == slot)
        jobs = work[slot] if slot < len(work) else []
        marks = [(i * len(now)) // max(len(jobs), 1) + LAG for i in range(len(jobs))]
        for i, (_, t, p) in enumerate(now):
            for job, mark in zip(jobs, marks):
                if min(mark, len(now) - 1) == i:
                    job[0](*job[1:])
            comm(t, p)
    small_out[...] = small[len(hops)]
    for t in range(count):
        store(t).wait()
    for seq in range(seqs):
        grad_copy(seq, False).wait()
        grad_copy(seq, True).wait()


def backward(g_outer, w_outer, w_inner, slope, full, blocks, shape):
    extra_bits = (lax.axis_size("batch") // 16).bit_length() - 1
    space, sems = plan_sizes(KINDS, extra_bits)
    hops = 5 + extra_bits
    count = len(KINDS)
    low, f32 = jnp.bfloat16, jnp.float32
    hbm = pl.BlockSpec(memory_space=pl.ANY)
    vmem = pl.BlockSpec(memory_space=pltpu.VMEM)
    rows, width = full[0].shape
    grads = [g_outer.shape, w_inner.shape] + [(width, width)] * 4
    flat = pltpu.VMEM((rows, width), low)
    return pl.pallas_call(
        functools.partial(back_kernel, extra_bits),
        out_shape=tuple(jax.ShapeDtypeStruct(g, low) for g in grads)
        + (jax.ShapeDtypeStruct((SMALL, LANES), f32), jax.ShapeDtypeStruct(shape, low)),
        in_specs=[hbm] * (4 + len(full)) + [vmem] * len(blocks),
        out_specs=(hbm,) * len(grads) + (vmem, hbm),
        scratch_shapes=[pltpu.VMEM(m.shape, m.dtype) for m in full]
        + [
            pltpu.VMEM((2, LANES, LANES), low),
            pltpu.VMEM((2, LANES, LANES), low),
            pltpu.VMEM((2, rows, LANES), low),
            flat, flat, flat, flat, flat, flat,
            pltpu.VMEM((rows // 128, 128, width), low),
            pltpu.VMEM((2 * count * ROWS, LANES), low),
            pltpu.VMEM((space, LANES), low),
            pltpu.VMEM((hops + 1, SMALL, LANES), f32),
            pltpu.VMEM((hops, SMALL, LANES), f32),
            pltpu.SemaphoreType.DMA((sems,)),
            pltpu.SemaphoreType.DMA((sems,)),
            pltpu.SemaphoreType.DMA((2, 6)),
            pltpu.SemaphoreType.DMA((2, hops)),
            pltpu.SemaphoreType.DMA((len(full),)),
            pltpu.SemaphoreType.DMA((3, 4)),
            pltpu.SemaphoreType.DMA((count,)),
            pltpu.SemaphoreType.DMA((3, shape[0] // 2)),
        ],
        compiler_params=pltpu.CompilerParams(collective_id=1, has_side_effects=True, vmem_limit_bytes=62 << 20),
    )(g_outer, w_outer, w_inner, slope, *full, *blocks)


def nt(a, b):
    return lax.dot_general(a, b, (((1,), (1,)), ((), ())), preferred_element_type=jnp.float32)


def nn(a, b):
    return lax.dot_general(a, b, (((1,), (0,)), ((), ())), preferred_element_type=jnp.float32)


def low_lanes(rows):
    return lax.broadcasted_iota(jnp.int32, (rows, 128), 1) < 64


def attend_pair(q, k, v, bias):
    low = low_lanes(k.shape[0])
    zero = jnp.zeros_like(k)
    vt = v.T
    parts, sums = [], []
    for head in range(2):
        own = jnp.where(low if head == 0 else ~low, k, zero)
        scores = nt(own, q) + bias
        top = jnp.max(scores, axis=0, keepdims=True)
        expo = jnp.exp(scores - top)
        total = jnp.sum(expo, axis=0, keepdims=True)
        parts.append(nn(vt[head * 64:head * 64 + 64], expo.astype(jnp.bfloat16)) * (1.0 / total))
        sums.append(top + jnp.log(total))
    return jnp.concatenate(parts, axis=0).T.astype(jnp.bfloat16), jnp.concatenate(sums, axis=0)


def attend_pair_back(q, k, v, dc, lse, bias):
    low = low_lanes(k.shape[0])
    zero = jnp.zeros_like(k)
    kt = k.T
    dq, dk, dv = [], [], []
    for head in range(2):
        mine = low if head == 0 else ~low
        probs = jnp.exp(nt(jnp.where(mine, k, zero), q) + (bias - lse[head:head + 1]))
        d_probs = nt(jnp.where(mine, v, zero), dc)
        inner = jnp.sum(probs * d_probs, axis=0, keepdims=True)
        d_scores = (probs * (d_probs - inner)).astype(jnp.bfloat16)
        dq.append(nn(kt[head * 64:head * 64 + 64], d_scores))
        dk.append(nn(d_scores, q))
        dv.append(nn(probs.astype(jnp.bfloat16), dc))
    d_query = (jnp.concatenate(dq, axis=0) * 0.125).T.astype(jnp.bfloat16)
    d_key = jnp.where(low, dk[0], dk[1]).astype(jnp.bfloat16)
    d_value = jnp.where(low, dv[0], dv[1]).astype(jnp.bfloat16)
    return d_query, d_key, d_value


def attend_kernel(q_ref, k_ref, v_ref, bias_ref, ctx_ref, lse_ref):
    bias = jnp.concatenate([bias_ref[...]] * (q_ref.shape[0] // 128), axis=1)
    ctx_ref[...], lse_ref[0, 0] = attend_pair(q_ref[...], k_ref[...], v_ref[...], bias)


def attend(q, k, v, bias, length):
    rows, width = q.shape
    seqs, pairs = rows // length, width // 128
    block = pl.BlockSpec((length, 128), lambda s, p: (s, p))
    mask = pl.BlockSpec((length, 128), lambda s, p: (s, 0))
    lse = pl.BlockSpec((1, 1, 2, length), lambda s, p: (s, p, 0, 0))
    return pl.pallas_call(
        attend_kernel,
        grid=(seqs, pairs),
        out_shape=(jax.ShapeDtypeStruct(q.shape, jnp.bfloat16), jax.ShapeDtypeStruct((seqs, pairs, 2, length), jnp.float32)),
        in_specs=[block, block, block, mask],
        out_specs=(block, lse),
    )(q, k, v, bias)


epsilon = 1e-05


def to_partner(block):
    return lax.ppermute(block, "mod", [(0, 1), (1, 0)])


def take_side(array, axis, side):
    half = array.shape[axis] // 2
    return lax.dynamic_slice_in_dim(array, side * half, half, axis)


def gather_sequences(array, side):
    own = take_side(array, 0, side)
    other = to_partner(take_side(array, 0, 1 - side))
    both = jnp.where(side == 0, jnp.concatenate((own, other), axis=1), jnp.concatenate((other, own), axis=1))
    return both.reshape(-1, array.shape[2])


def return_rows(array, side):
    own = take_side(array, 1, side)
    other = to_partner(take_side(array, 1, 1 - side))
    return jnp.where(side == 0, jnp.concatenate((own, other)), jnp.concatenate((other, own)))


def linear(rows, weight_matrix):
    return lax.dot_general(rows, weight_matrix, (((1,), (0,)), ((), ())), preferred_element_type=jnp.float32)


def back_linear(gradient_rows, weight_matrix):
    return lax.dot_general(gradient_rows, weight_matrix, (((1,), (1,)), ((), ())), preferred_element_type=jnp.float32)


def weight_grad(layer_inputs, gradient_rows):
    return lax.dot_general(
        layer_inputs, gradient_rows, (((0,), (0,)), ((), ())), preferred_element_type=jnp.float32
    ).astype(jnp.bfloat16)


def row_total(values):
    return jnp.sum(values.astype(jnp.float32), axis=0, keepdims=True)


def layer_norm(rows):
    centre = rows - jnp.mean(rows, axis=-1, keepdims=True)
    factor = lax.rsqrt(jnp.mean(centre * centre, axis=-1, keepdims=True) + epsilon)
    return (centre * factor, factor)


def norm_back(gradient_rows, normed, factor):
    return factor * (
        gradient_rows
        - jnp.mean(gradient_rows, axis=-1, keepdims=True)
        - normed * jnp.mean(gradient_rows * normed, axis=-1, keepdims=True)
    )


def on_device(
    hidden_in,
    text_mask,
    region_count,
    w_query,
    b_query,
    w_key,
    w_value,
    b_value,
    w_attn_out,
    b_attn_out,
    gain_attn,
    shift_attn,
    w_inner,
    b_inner,
    w_outer,
    b_outer,
    gain_ffn,
    shift_ffn,
    cotangent,
):
    seq_count, half_len, width = hidden_in.shape
    length = 2 * half_len
    side = lax.axis_index("mod")
    f32 = jnp.float32
    rows_b = gather_sequences(hidden_in, side)
    upstream = gather_sequences(cotangent, side).astype(f32)
    mask = take_side(text_mask, 0, side) == 1
    regions = take_side(region_count, 0, side)
    slot_ok = lax.broadcasted_iota(jnp.int32, mask.shape, 1) < regions[:, None]
    bias = jnp.where(jnp.concatenate((mask, slot_ok), axis=1), f32(0.0), f32(-1000000000.0)).reshape(-1, 1)
    bias = jnp.broadcast_to(bias, (bias.shape[0], 128))

    query_b = ((linear(rows_b, w_query) + b_query.astype(f32)).astype(jnp.bfloat16) * jnp.bfloat16(0.125))
    key_b = linear(rows_b, w_key).astype(jnp.bfloat16)
    value_b = (linear(rows_b, w_value) + b_value.astype(f32)).astype(jnp.bfloat16)
    context_b, lse = attend(query_b, key_b, value_b, bias, length)
    branch = linear(context_b, w_attn_out) + b_attn_out.astype(f32)
    normed_one, factor_one = layer_norm(rows_b.astype(f32) + branch)
    middle = normed_one * gain_attn.astype(f32) + shift_attn.astype(f32)
    middle_b = middle.astype(jnp.bfloat16)
    pre_act = linear(middle_b, w_inner) + b_inner.astype(f32)
    below = 0.5 * (1.0 + lax.erf(pre_act * f32(0.7071067811865476)))
    slope_b = (below + pre_act * (jnp.exp(-0.5 * pre_act * pre_act) * f32(0.3989422804014327))).astype(jnp.bfloat16)
    activ_b = (pre_act * below).astype(jnp.bfloat16)
    ffn_out = linear(activ_b, w_outer) + b_outer.astype(f32)
    normed_two, factor_two = layer_norm(middle + ffn_out)
    layer_out = (normed_two * gain_ffn.astype(f32) + shift_ffn.astype(f32)).astype(jnp.bfloat16)
    layer_out = return_rows(layer_out.reshape(seq_count // 2, length, width), side)
    grad_gain_ffn = row_total(upstream * normed_two)
    grad_shift_ffn = row_total(upstream)
    d_res_two = norm_back(upstream * gain_ffn.astype(f32), normed_two, factor_two)
    d_ffn_b = d_res_two.astype(jnp.bfloat16)
    grad_b_outer = row_total(d_ffn_b)
    grad_w_outer = weight_grad(activ_b, d_ffn_b)
    s_outer, s_inner, s_query, s_key, s_value, s_attn_out, small, input_grad = backward(
        grad_w_outer, w_outer, w_inner, slope_b,
        (
            query_b, key_b, value_b, context_b, rows_b, middle_b, d_ffn_b, d_res_two, normed_one,
            w_query, w_key, w_value, w_attn_out,
        ),
        (factor_one, gain_attn.astype(f32).reshape(1, -1), lse, bias, grad_b_outer, grad_gain_ffn, grad_shift_ffn),
        hidden_in.shape,
    )
    return (
        layer_out,
        input_grad,
        s_query.astype(f32),
        small[0],
        s_key.astype(f32),
        s_value.astype(f32),
        small[1],
        s_attn_out.astype(f32),
        small[2],
        small[3],
        small[4],
        s_inner.astype(f32),
        small[8:12].reshape(-1),
        s_outer.astype(f32),
        small[5],
        small[6],
        small[7],
    )


def solution(mesh):
    in_specs = (
        P("batch", "mod", None),
        P("batch", None),
        P("batch"),
        P(),
        P(),
        P(),
        P(),
        P(),
        P(),
        P(),
        P(),
        P(),
        P(),
        P(),
        P(),
        P(),
        P(),
        P(),
        P("batch", "mod", None),
    )
    out_specs = (
        P("batch", "mod", None),
        P("batch", "mod", None),
        P(),
        P(),
        P(),
        P(),
        P(),
        P(),
        P(),
        P(),
        P(),
        P(),
        P(),
        P(),
        P(),
        P(),
        P(),
    )
    return jax.shard_map(
        on_device, mesh=mesh, in_specs=in_specs, out_specs=out_specs, check_vma=False
    )
```

```python
import functools

import jax
import jax.numpy as jnp
from jax import lax
from jax.experimental import pallas as pl
from jax.experimental.pallas import tpu as pltpu
from jax.sharding import PartitionSpec as P

MESH = pl.DeviceIdType.MESH
ROWS = 256
LANES = 768


class Wire:
    def __init__(self, extra_bits):
        self.b = lax.axis_index("batch")
        self.m = lax.axis_index("mod")
        self.core = lax.rem(self.b, 2)
        self.y = lax.rem(self.b // 2, 2)
        self.z = lax.rem(self.b // 4, 4)
        self.extra_bits = extra_bits

    def flip(self, bit):
        own = lax.rem(self.b // (1 << bit), 2)
        return (self.b + (1 - 2 * own) * (1 << bit), self.m)

    def peer(self, dim):
        if dim == "x":
            return (self.b, 1 - self.m)
        if dim == "y":
            return self.flip(1)
        if dim == "core":
            return self.flip(0)
        if dim == "up":
            return (self.b + 4, self.m)
        if dim == "down":
            return (self.b - 4, self.m)
        return self.flip(dim)

    def coord(self, dim):
        return self.m if dim == "x" else self.y

    def barrier(self):
        bar = pltpu.get_barrier_semaphore()
        peers = [self.peer(d) for d in ("core", "x", "y")]
        peers += [self.flip(bit) for bit in range(2, 4 + self.extra_bits)]
        for who in peers:
            pl.semaphore_signal(bar, inc=1, device_id=who, device_id_type=MESH)
        mid_low, mid_high = self.z == 1, self.z == 2

        @pl.when(mid_low)
        def _():
            pl.semaphore_signal(bar, inc=1, device_id=self.peer("up"), device_id_type=MESH)

        @pl.when(mid_high)
        def _():
            pl.semaphore_signal(bar, inc=1, device_id=self.peer("down"), device_id_type=MESH)

        pl.semaphore_wait(bar, len(peers) + jnp.where(mid_low | mid_high, 1, 0))


def plan_sizes(kinds, extra_bits):
    rows = sems = 0
    for kind in kinds:
        n = ROWS
        rows += ROWS
        sems += 1
        order = "xyz" if kind == "A" else "yxz" if kind == "B" else "zxy" if kind == "C" else "zyx"
        for dim in order:
            if dim == "z":
                rows += 6 * (n // 4)
                n //= 4
            else:
                rows += n // 2
                n //= 2
        rows += extra_bits * n
        sems += 6 + 6 + 4 + extra_bits + 1
    return rows, sems


def add_rows(acc, at, rb, rb_at, n):
    step = min(n, 64)

    def body(i, carry):
        d = pl.multiple_of(at + i * step, 16)
        s = pl.multiple_of(rb_at + i * step, 16)
        total = acc[pl.ds(d, step), :].astype(jnp.float32) + rb[pl.ds(s, step), :].astype(jnp.float32)
        acc[pl.ds(d, step), :] = total.astype(jnp.bfloat16)
        return carry

    if n == step:
        body(0, 0)
    else:
        lax.fori_loop(0, n // step, body, 0)


class Tasks:
    def __init__(self, wire, kinds, part, rb, ssem, rsem, block):
        self.w, self.acc, self.rb, self.block = wire, part, rb, block
        self.ssem, self.rsem = ssem, rsem
        self.rb_at = 0
        self.sem_at = 0
        self.homes = []
        self.steps = [self.build(t, kind) for t, kind in enumerate(kinds)]

    def space(self, n):
        at = self.rb_at
        self.rb_at += n
        return at

    def copy(self, src, dst, who):
        k = self.sem_at
        self.sem_at += 1
        return lambda: pltpu.make_async_remote_copy(
            src_ref=src(), dst_ref=dst(), send_sem=self.ssem.at[k], recv_sem=self.rsem.at[k], device_id=who, device_id_type=MESH
        )

    def rows(self, at, n):
        return self.acc.at[pl.ds(pl.multiple_of(at, 16), n), :]

    def build(self, t, kind):
        w = self.w
        steps = []
        home = (w.core * len(KINDS) + t) * ROWS
        away = ((1 - w.core) * len(KINDS) + t) * ROWS
        at0 = self.space(ROWS)

        def done(at, n):
            return self.rb.at[pl.ds(pl.multiple_of(at + (at0 - home), 16), n), :]

        def keep(at, n):
            self.rb[pl.ds(pl.multiple_of(at + (at0 - home), 16), n), :] = self.acc[pl.ds(pl.multiple_of(at, 16), n), :]

        def exchange(src, dst, who, then):
            cp = self.copy(src, dst, who)

            def begin():
                cp().start()

            def finish():
                cp().wait()
                then()

            steps.append((begin, finish))

        def reduce(dim, base, n):
            half, a = n // 2, w.coord(dim)
            at = self.space(half)
            kept = base + a * half
            sent = base + (1 - a) * half
            exchange(
                lambda: self.rows(sent, half),
                lambda: self.rb.at[pl.ds(at, half), :],
                w.peer(dim),
                lambda: add_rows(self.acc, kept, self.rb, at, half),
            )
            return kept, half

        def gather(dim, base, n):
            exchange(lambda: done(base, n), lambda: done(base, n), w.peer(dim), lambda: None)

        def line_reduce(base, n):
            q, z, zz = n // 4, w.z, 3 - w.z
            for s in (1, 2, 3):
                up_at, down_at = self.space(q), self.space(q)
                up_sends, up_gets = (z < 3) & (s >= z + 1), (z >= 1) & (s >= z)
                down_sends, down_gets = (zz < 3) & (s >= zz + 1), (zz >= 1) & (s >= zz)
                up_src = base + jnp.clip(4 - s + z, 0, 3) * q
                down_src = base + jnp.clip(s + z - 4, 0, 3) * q
                up_add = base + jnp.clip(3 - s + z, 0, 3) * q
                down_add = base + jnp.clip(s - 3 + z, 0, 3) * q
                up = self.copy(lambda v=up_src: self.rows(v, q), lambda v=up_at: self.rb.at[pl.ds(v, q), :], w.peer("up"))
                down = self.copy(lambda v=down_src: self.rows(v, q), lambda v=down_at: self.rb.at[pl.ds(v, q), :], w.peer("down"))
                steps.append(line_step(up, down, up_sends, up_gets, down_sends, down_gets,
                                       lambda a=up_add, r=up_at: add_rows(self.acc, a, self.rb, r, q),
                                       lambda a=down_add, r=down_at: add_rows(self.acc, a, self.rb, r, q)))
            return base + z * q, q

        def line_gather(base, q):
            z = w.z
            for s in (1, 2, 3):
                up_sends, up_gets = (z < 3) & (z - (s - 1) >= 0), z - s >= 0
                down_sends, down_gets = (z > 0) & (z + (s - 1) <= 3), z + s <= 3
                up_src = base + jnp.clip(z - s + 1, 0, 3) * q
                down_src = base + jnp.clip(z + s - 1, 0, 3) * q
                up = self.copy(lambda v=up_src: done(v, q), lambda v=up_src: done(v, q), w.peer("up"))
                down = self.copy(lambda v=down_src: done(v, q), lambda v=down_src: done(v, q), w.peer("down"))
                steps.append(line_step(up, down, up_sends, up_gets, down_sends, down_gets, None, None))

        def line_step(up, down, up_sends, up_gets, down_sends, down_gets, up_then, down_then):
            def begin():
                @pl.when(up_sends)
                def _():
                    up().start()

                @pl.when(down_sends)
                def _():
                    down().start()

            def finish():
                for cp, gets, then in ((up, up_gets, up_then), (down, down_gets, down_then)):
                    @pl.when(gets)
                    def _(cp=cp, then=then):
                        cp().wait_recv()
                        if then is not None:
                            then()

                for cp, sends in ((up, up_sends), (down, down_sends)):
                    @pl.when(sends)
                    def _(cp=cp):
                        cp().wait_send()

            return begin, finish

        def then_keep(base, n):
            begin, finish = steps.pop()

            def finish_and_keep():
                finish()
                keep(base, n)

            steps.append((begin, finish_and_keep))

        def widen(base, n):
            for bit in range(4, 4 + w.extra_bits):
                at = self.space(n)
                exchange(
                    lambda: self.rows(base, n),
                    lambda at=at: self.rb.at[pl.ds(at, n), :],
                    w.peer(bit),
                    lambda at=at: add_rows(self.acc, base, self.rb, at, n),
                )

        exchange(
            lambda: self.rows(away, ROWS),
            lambda: self.rb.at[pl.ds(at0, ROWS), :],
            w.peer("core"),
            lambda: add_rows(self.acc, home, self.rb, at0, ROWS),
        )
        if kind in "AB":
            d1, d2 = ("x", "y") if kind == "A" else ("y", "x")
            b1, n1 = reduce(d1, home, ROWS)
            b2, n2 = reduce(d2, b1, n1)
            b3, n3 = line_reduce(b2, n2)
            widen(b3, n3)
            then_keep(b3, n3)
            line_gather(b2, n3)
            gather(d2, b2, n2)
            gather(d1, b1, n1)
        else:
            d1, d2 = ("x", "y") if kind == "C" else ("y", "x")
            b1, n1 = line_reduce(home, ROWS)
            b2, n2 = reduce(d1, b1, n1)
            b3, n3 = reduce(d2, b2, n2)
            widen(b3, n3)
            then_keep(b3, n3)
            gather(d2, b3, n3)
            gather(d1, b2, n2)
            line_gather(home, n1)
        k = self.sem_at
        self.sem_at += 1

        def last(block):
            return pltpu.make_async_remote_copy(
                src_ref=self.rb.at[pl.ds(at0, ROWS), :], dst_ref=block, send_sem=self.ssem.at[k], recv_sem=self.rsem.at[k],
                device_id=w.peer("core"), device_id_type=MESH)

        final = by_core(w.core, lambda half: last(self.block(half, t)), t)
        steps.append((lambda: final.start(), lambda: final.wait()))
        self.homes.append(at0)
        return steps

    def op(self, t, p):
        steps = self.steps[t]
        if p > 0:
            steps[p - 1][1]()
        if p < len(steps):
            steps[p][0]()


KINDS = "ABCABDABCABDABCABD"
START = tuple((0, 1, 2, 3, 6, 6)[t // 3] for t in range(18))
SMALL = 16
SMALL_START = 8
LAG = 1


def block_of(refs, half, t):
    if t < 6:
        return refs[0].at[pl.ds(pl.multiple_of(half * 1536 + t * ROWS, ROWS), ROWS), :]
    if t < 12:
        i, j = (t - 6) % 3, (t - 6) // 3
        return refs[1].at[pl.ds(i * ROWS, ROWS), pl.ds(pl.multiple_of((half * 2 + j) * LANES, LANES), LANES)]
    return refs[2 + 2 * half + (t - 12) // 3].at[pl.ds((t - 12) % 3 * ROWS, ROWS), :]


class Branches:
    def __init__(self, core, make):
        self.core, self.make = core, make

    def start(self):
        for core in range(2):
            @pl.when(self.core == core)
            def _(core=core):
                self.make(core).start()

    def wait(self):
        self.make(0).wait()


class Plain:
    def __init__(self, make):
        self.make = make

    def start(self):
        self.make().start()

    def wait(self):
        self.make().wait()


def by_core(core, make, t):
    return Plain(lambda: make(core)) if t < 12 else Branches(core, make)


def tn(a, b):
    return lax.dot_general(a, b, (((0,), (0,)), ((), ())), preferred_element_type=jnp.float32)


FULL = ("q", "k", "v", "ctx", "x", "mid", "dffn", "dmid", "normed", "wq", "wk", "wv", "wo")


def back_kernel(extra_bits, *refs):
    g_outer, w_outer, w_inner, slope, *refs = refs
    full_in, refs = dict(zip(FULL, refs)), refs[len(FULL):]
    factor, gain, lse, bias_ref, sum_outer, sum_gain, sum_shift, *refs = refs
    outs, small_out, grad_out, refs = refs[:6], refs[6], refs[7], refs[8:]
    v, refs = dict(zip(FULL, refs)), refs[len(FULL):]
    wou, win, gp, dp, dc, db, dq, dk, dv, ig, part, rb, small, small_rb, ssem, rsem, lsem, vsem, fsem, tsem, osem, isem = refs
    w = Wire(extra_bits)
    count = len(KINDS)
    f32 = jnp.float32
    rows = dp.shape[0]
    length = bias_ref.shape[0] // lse.shape[0]
    order = (0, 2, 1, 3)

    def load(half, t):
        to = part.at[pl.ds((half * count + t) * ROWS, ROWS), :]
        return pltpu.make_async_copy(g_outer.at[pl.ds(half * 1536 + t * ROWS, ROWS), :], to, lsem.at[half, t])

    def fetch(name):
        return pltpu.make_async_copy(full_in[name], v[name], fsem.at[FULL.index(name)])

    def tile(which, n):
        at, slot = order[n] * LANES, n % 2
        source, to = (
            (w_outer.at[pl.ds(at, LANES), :], wou),
            (w_inner.at[:, pl.ds(at, LANES)], win),
            (slope.at[:, pl.ds(at, LANES)], gp),
        )[which]
        return pltpu.make_async_copy(source, to.at[slot], tsem.at[which, n])

    for t in range(6):
        load(0, t).start()
        load(1, t).start()
        if t == 0:
            fetch("dffn").start()
            tile(0, 0).start()
            tile(2, 0).start()
            fetch("mid").start()
            tile(1, 0).start()
            fetch("dmid").start()
    for which in range(3):
        tile(which, 1).start()
    for name in ("normed", "wo", "ctx", "k", "q", "v", "x", "wq", "wk", "wv"):
        fetch(name).start()
    w.barrier()
    tasks = Tasks(w, KINDS, part, rb, ssem, rsem, lambda half, t: block_of(outs, half, t))

    def store(t):
        def make(half):
            return pltpu.make_async_copy(rb.at[pl.ds(tasks.homes[t], ROWS), :], block_of(outs, half, t), osem.at[t])

        return by_core(w.core, make, t)

    def grad_blocks(left, right, half, t):
        to = pl.ds((half * count + t) * ROWS, left.shape[1])
        part[to, :] = tn(left[...], right[...]).astype(jnp.bfloat16)

    def by_rows(step, body, carry=0):
        def wrapped(r, carry):
            return body(pl.ds(pl.multiple_of(r * step, step), step), carry)

        return lax.fori_loop(0, rows // step, wrapped, carry)

    none = jnp.zeros((1, LANES), f32)

    def d_pre(n):
        tile(0, n).wait()
        tile(2, n).wait()
        if n == 0:
            fetch("dffn").wait()

        d = (nt(v["dffn"][...], wou[n % 2]) * gp[n % 2].astype(f32)).astype(jnp.bfloat16)
        dp[...] = d
        small[0, 8 + order[n]:9 + order[n], :] = jnp.sum(d.astype(f32), axis=0, keepdims=True)
        if n + 2 < 4:
            tile(0, n + 2).start()
            tile(2, n + 2).start()

    def inner_blocks(n):
        if n == 0:
            fetch("mid").wait()
        grad_blocks(v["mid"], dp, order[n] // 2, 6 + 3 * (order[n] % 2))

    def d_mid(n):
        tile(1, n).wait()
        if n == 0:
            fetch("dmid").wait()

        v["dmid"][...] += nt(dp[...], win[n % 2])
        if n + 2 < 4:
            tile(1, n + 2).start()

    def norm_step():
        fetch("normed").wait()

        def body(at, sums):
            d, normed = v["dmid"][at, :], v["normed"][at, :]
            e = d * gain[...]
            res = factor[at, :] * (
                e - jnp.mean(e, axis=-1, keepdims=True) - normed * jnp.mean(e * normed, axis=-1, keepdims=True)
            )
            low = res.astype(jnp.bfloat16)
            v["dmid"][at, :] = res
            db[at, :] = low
            return (
                sums[0] + jnp.sum(low.astype(f32), axis=0, keepdims=True),
                sums[1] + jnp.sum(d * normed, axis=0, keepdims=True),
                sums[2] + jnp.sum(d, axis=0, keepdims=True),
            )

        sums = by_rows(128, body, (none, none, none))
        for i in range(3):
            small[0, 2 + i:3 + i, :] = sums[i]

    def d_context():
        fetch("wo").wait()

        dc[...] = nt(db[...], v["wo"][...]).astype(jnp.bfloat16)

    def out_blocks():
        fetch("ctx").wait()
        grad_blocks(v["ctx"], db, 1, 15)

    def attention(seq, first, pairs):
        if seq == 0 and first == 0:
            for name in ("q", "k", "v"):
                fetch(name).wait()
        at = pl.ds(seq * length, length)
        bias = jnp.concatenate([bias_ref[at, :]] * (length // 128), axis=1)

        columns = [pl.ds(p * 128, 128) for p in range(first, first + pairs)]
        found = attend_back(
            [(v["q"][at, c], v["k"][at, c], v["v"][at, c], dc[at, c], lse[seq, first + i]) for i, c in enumerate(columns)],
            bias)
        for c, (d_query, d_key, d_value) in zip(columns, found):
            dq[at, c], dk[at, c], dv[at, c] = d_query, d_key, d_value

    def total_rows(ref, row):
        def body(at, total):
            return total + jnp.sum(ref[at, :].astype(f32), axis=0, keepdims=True)

        small[0, row:row + 1, :] = by_rows(128, body, none)

    def value_blocks():
        grad_blocks(v["x"], dv, 1, 12)
        total_rows(dv, 1)

    def query_blocks():
        fetch("x").wait()
        grad_blocks(v["x"], dq, 0, 12)
        total_rows(dq, 0)

    def key_blocks():
        grad_blocks(v["x"], dk, 0, 15)

    def grad_copy(seq, away):
        source = ig.at[2 * seq + (1 - w.m if away else w.m)]
        to = grad_out.at[w.m * lse.shape[0] + seq]
        if not away:
            return pltpu.make_async_copy(source, to, isem.at[2, seq])
        return pltpu.make_async_remote_copy(
            src_ref=source, dst_ref=to, send_sem=isem.at[0, seq], recv_sem=isem.at[1, seq],
            device_id=w.peer("x"), device_id_type=MESH)

    def input_rows(seq):
        if seq == 0:
            for name in ("wq", "wk", "wv"):
                fetch(name).wait()

        at = pl.ds(seq * length, length)
        total = v["dmid"][at, :] + nt(dq[at, :], v["wq"][...])
        total = total + nt(dk[at, :], v["wk"][...]) + nt(dv[at, :], v["wv"][...])
        for i in range(length // 128):
            ig[2 * seq + i] = total[i * 128:i * 128 + 128].astype(jnp.bfloat16)
        grad_copy(seq, True).start()
        grad_copy(seq, False).start()

    small[0, 12:16, :] = jnp.zeros((4, LANES), f32)
    for row, ref in ((5, sum_outer), (6, sum_gain), (7, sum_shift)):
        small[0, row:row + 1, :] = ref[...]
    hops = ["core", "x", "y"] + list(range(2, 4 + extra_bits))

    def small_copy(k):
        return pltpu.make_async_remote_copy(
            src_ref=small.at[k], dst_ref=small_rb.at[k], send_sem=vsem.at[0, k], recv_sem=vsem.at[1, k],
            device_id=w.peer(hops[k]), device_id_type=MESH)

    def small_op(k):
        if k > 0:
            small_copy(k - 1).wait()
            small[k] = small[k - 1] + small_rb[k - 1]
        if k < len(hops):
            small_copy(k).start()

    seqs, pairs = lse.shape[:2]
    ffn = [job for n in range(4) for job in ((d_pre, n), (inner_blocks, n), (d_mid, n))]
    attn = [(attention, seq, first, 3) for seq in range(seqs) for first in range(0, pairs, 3)]
    work = [ffn[:3], ffn[3:7], ffn[7:], [(norm_step,), (d_context,), (out_blocks,)] + attn[:1]]
    work += [attn[1:], [(query_blocks,), (value_blocks,), (key_blocks,)]]
    work.append([(input_rows, seq) for seq in range(seqs)])

    def comm(t, p):
        if t == count:
            small_op(p)
            return
        if p == 0 and t < 6:
            load(0, t).wait()
            load(1, t).wait()
        tasks.op(t, p)
        if p == len(tasks.steps[t]) - 1:
            store(t).start()

    ops = [(START[t] + p, t, p) for t in range(count) for p in range(len(tasks.steps[t]) + 1)]
    ops += [(SMALL_START + k, count, k) for k in range(len(hops) + 1)]
    for slot in range(max(op[0] for op in ops) + 1):
        now = sorted(op for op in ops if op[0] == slot)
        jobs = work[slot] if slot < len(work) else []
        marks = [(i * len(now)) // max(len(jobs), 1) + LAG for i in range(len(jobs))]
        for i, (_, t, p) in enumerate(now):
            for job, mark in zip(jobs, marks):
                if min(mark, len(now) - 1) == i:
                    job[0](*job[1:])
            comm(t, p)
    small_out[...] = small[len(hops)]
    for t in range(count):
        store(t).wait()
    for seq in range(seqs):
        grad_copy(seq, False).wait()
        grad_copy(seq, True).wait()


def backward(g_outer, w_outer, w_inner, slope, full, blocks, shape):
    extra_bits = (lax.axis_size("batch") // 16).bit_length() - 1
    space, sems = plan_sizes(KINDS, extra_bits)
    hops = 5 + extra_bits
    count = len(KINDS)
    low, f32 = jnp.bfloat16, jnp.float32
    hbm = pl.BlockSpec(memory_space=pl.ANY)
    vmem = pl.BlockSpec(memory_space=pltpu.VMEM)
    rows, width = full[0].shape
    grads = [g_outer.shape, w_inner.shape] + [(width, width)] * 4
    flat = pltpu.VMEM((rows, width), low)
    return pl.pallas_call(
        functools.partial(back_kernel, extra_bits),
        out_shape=tuple(jax.ShapeDtypeStruct(g, low) for g in grads)
        + (jax.ShapeDtypeStruct((SMALL, LANES), f32), jax.ShapeDtypeStruct(shape, low)),
        in_specs=[hbm] * (4 + len(full)) + [vmem] * len(blocks),
        out_specs=(hbm,) * len(grads) + (vmem, hbm),
        scratch_shapes=[pltpu.VMEM(m.shape, m.dtype) for m in full]
        + [
            pltpu.VMEM((2, LANES, LANES), low),
            pltpu.VMEM((2, LANES, LANES), low),
            pltpu.VMEM((2, rows, LANES), low),
            flat, flat, flat, flat, flat, flat,
            pltpu.VMEM((rows // 128, 128, width), low),
            pltpu.VMEM((2 * count * ROWS, LANES), low),
            pltpu.VMEM((space, LANES), low),
            pltpu.VMEM((hops + 1, SMALL, LANES), f32),
            pltpu.VMEM((hops, SMALL, LANES), f32),
            pltpu.SemaphoreType.DMA((sems,)),
            pltpu.SemaphoreType.DMA((sems,)),
            pltpu.SemaphoreType.DMA((2, 6)),
            pltpu.SemaphoreType.DMA((2, hops)),
            pltpu.SemaphoreType.DMA((len(full),)),
            pltpu.SemaphoreType.DMA((3, 4)),
            pltpu.SemaphoreType.DMA((count,)),
            pltpu.SemaphoreType.DMA((3, shape[0] // 2)),
        ],
        compiler_params=pltpu.CompilerParams(collective_id=1, has_side_effects=True, vmem_limit_bytes=62 << 20),
    )(g_outer, w_outer, w_inner, slope, *full, *blocks)


def nt(a, b):
    return lax.dot_general(a, b, (((1,), (1,)), ((), ())), preferred_element_type=jnp.float32)


def nn(a, b):
    return lax.dot_general(a, b, (((1,), (0,)), ((), ())), preferred_element_type=jnp.float32)


def low_lanes(rows):
    return lax.broadcasted_iota(jnp.int32, (rows, 128), 1) < 64


def heads_of(pairs):
    return [(i, head) for i in range(len(pairs)) for head in range(2)]


def own_lanes(block, head):
    low = low_lanes(block.shape[0])
    return jnp.where(low if head == 0 else ~low, block, jnp.zeros_like(block))


def attend(pairs, bias):
    heads = heads_of(pairs)
    scores = [nt(own_lanes(pairs[i][1], head), pairs[i][0]) + bias for i, head in heads]
    tops = [jnp.max(s, axis=0, keepdims=True) for s in scores]
    expo = [jnp.exp(s - top) for s, top in zip(scores, tops)]
    totals = [jnp.sum(e, axis=0, keepdims=True) for e in expo]
    vt = [pair[2].T for pair in pairs]
    context = [
        nn(vt[i][head * 64:head * 64 + 64], e.astype(jnp.bfloat16)) * (1.0 / total)
        for e, total, (i, head) in zip(expo, totals, heads)
    ]
    logs = [top + jnp.log(total) for top, total in zip(tops, totals)]
    return [
        (jnp.concatenate(context[2 * i:2 * i + 2], axis=0).T.astype(jnp.bfloat16), jnp.concatenate(logs[2 * i:2 * i + 2], axis=0))
        for i in range(len(pairs))
    ]


def attend_back(pairs, bias):
    heads = heads_of(pairs)
    kt = [pair[1].T for pair in pairs]
    scores = [nt(own_lanes(pairs[i][1], head), pairs[i][0]) for i, head in heads]
    d_probs = [nt(own_lanes(pairs[i][2], head), pairs[i][3]) for i, head in heads]
    probs = [jnp.exp(s + (bias - pairs[i][4][head:head + 1])) for s, (i, head) in zip(scores, heads)]
    inner = [jnp.sum(p * d, axis=0, keepdims=True) for p, d in zip(probs, d_probs)]
    d_scores = [(p * (d - one)).astype(jnp.bfloat16) for p, d, one in zip(probs, d_probs, inner)]
    probs_low = [p.astype(jnp.bfloat16) for p in probs]
    dq = [nn(kt[i][head * 64:head * 64 + 64], d) for d, (i, head) in zip(d_scores, heads)]
    dk = [nn(d, pairs[i][0]) for d, (i, head) in zip(d_scores, heads)]
    dv = [nn(p, pairs[i][3]) for p, (i, head) in zip(probs_low, heads)]
    low = low_lanes(pairs[0][0].shape[0])
    return [
        (
            (jnp.concatenate(dq[2 * i:2 * i + 2], axis=0) * 0.125).T.astype(jnp.bfloat16),
            jnp.where(low, dk[2 * i], dk[2 * i + 1]).astype(jnp.bfloat16),
            jnp.where(low, dv[2 * i], dv[2 * i + 1]).astype(jnp.bfloat16),
        )
        for i in range(len(pairs))
    ]


def forward_kernel(q_ref, k_ref, v_ref, bias_ref, ctx_ref, lse_ref):
    length, width = q_ref.shape
    bias = jnp.concatenate([bias_ref[...]] * (length // 128), axis=1)

    def body(step, carry):
        columns = [pl.ds(pl.multiple_of((step * 3 + i) * 128, 128), 128) for i in range(3)]
        found = attend([(q_ref[:, c], k_ref[:, c], v_ref[:, c]) for c in columns], bias)
        for i, (context, logs) in enumerate(found):
            ctx_ref[:, columns[i]] = context
            lse_ref[0, step * 3 + i] = logs
        return carry

    lax.fori_loop(0, width // 384, body, 0)


def attention_forward(q, k, v, bias, length):
    rows, width = q.shape
    seqs, pairs = rows // length, width // 128
    block = pl.BlockSpec((length, width), lambda s: (s, 0))
    return pl.pallas_call(
        forward_kernel,
        grid=(seqs,),
        out_shape=(jax.ShapeDtypeStruct(q.shape, jnp.bfloat16), jax.ShapeDtypeStruct((seqs, pairs, 2, length), jnp.float32)),
        in_specs=[block, block, block, pl.BlockSpec((length, 128), lambda s: (s, 0))],
        out_specs=(block, pl.BlockSpec((1, pairs, 2, length), lambda s: (s, 0, 0, 0))),
    )(q, k, v, bias)


epsilon = 1e-05


def to_partner(block):
    return lax.ppermute(block, "mod", [(0, 1), (1, 0)])


def take_side(array, axis, side):
    half = array.shape[axis] // 2
    return lax.dynamic_slice_in_dim(array, side * half, half, axis)


def gather_sequences(array, side):
    own = take_side(array, 0, side)
    other = to_partner(take_side(array, 0, 1 - side))
    both = jnp.where(side == 0, jnp.concatenate((own, other), axis=1), jnp.concatenate((other, own), axis=1))
    return both.reshape(-1, array.shape[2])


def return_rows(array, side):
    own = take_side(array, 1, side)
    other = to_partner(take_side(array, 1, 1 - side))
    return jnp.where(side == 0, jnp.concatenate((own, other)), jnp.concatenate((other, own)))


def linear(rows, weight_matrix):
    return lax.dot_general(rows, weight_matrix, (((1,), (0,)), ((), ())), preferred_element_type=jnp.float32)


def back_linear(gradient_rows, weight_matrix):
    return lax.dot_general(gradient_rows, weight_matrix, (((1,), (1,)), ((), ())), preferred_element_type=jnp.float32)


def weight_grad(layer_inputs, gradient_rows):
    return lax.dot_general(
        layer_inputs, gradient_rows, (((0,), (0,)), ((), ())), preferred_element_type=jnp.float32
    ).astype(jnp.bfloat16)


def row_total(values):
    return jnp.sum(values.astype(jnp.float32), axis=0, keepdims=True)


def layer_norm(rows):
    centre = rows - jnp.mean(rows, axis=-1, keepdims=True)
    factor = lax.rsqrt(jnp.mean(centre * centre, axis=-1, keepdims=True) + epsilon)
    return (centre * factor, factor)


def norm_back(gradient_rows, normed, factor):
    return factor * (
        gradient_rows
        - jnp.mean(gradient_rows, axis=-1, keepdims=True)
        - normed * jnp.mean(gradient_rows * normed, axis=-1, keepdims=True)
    )


def on_device(
    hidden_in,
    text_mask,
    region_count,
    w_query,
    b_query,
    w_key,
    w_value,
    b_value,
    w_attn_out,
    b_attn_out,
    gain_attn,
    shift_attn,
    w_inner,
    b_inner,
    w_outer,
    b_outer,
    gain_ffn,
    shift_ffn,
    cotangent,
):
    seq_count, half_len, width = hidden_in.shape
    length = 2 * half_len
    side = lax.axis_index("mod")
    f32 = jnp.float32
    rows_b = gather_sequences(hidden_in, side)
    upstream = gather_sequences(cotangent, side).astype(f32)
    mask = take_side(text_mask, 0, side) == 1
    regions = take_side(region_count, 0, side)
    slot_ok = lax.broadcasted_iota(jnp.int32, mask.shape, 1) < regions[:, None]
    bias = jnp.where(jnp.concatenate((mask, slot_ok), axis=1), f32(0.0), f32(-1000000000.0)).reshape(-1, 1)
    bias = jnp.broadcast_to(bias, (bias.shape[0], 128))

    query_b = ((linear(rows_b, w_query) + b_query.astype(f32)).astype(jnp.bfloat16) * jnp.bfloat16(0.125))
    key_b = linear(rows_b, w_key).astype(jnp.bfloat16)
    value_b = (linear(rows_b, w_value) + b_value.astype(f32)).astype(jnp.bfloat16)
    context_b, lse = attention_forward(query_b, key_b, value_b, bias, length)
    branch = linear(context_b, w_attn_out) + b_attn_out.astype(f32)
    normed_one, factor_one = layer_norm(rows_b.astype(f32) + branch)
    middle = normed_one * gain_attn.astype(f32) + shift_attn.astype(f32)
    middle_b = middle.astype(jnp.bfloat16)
    pre_act = linear(middle_b, w_inner) + b_inner.astype(f32)
    below = 0.5 * (1.0 + lax.erf(pre_act * f32(0.7071067811865476)))
    slope_b = (below + pre_act * (jnp.exp(-0.5 * pre_act * pre_act) * f32(0.3989422804014327))).astype(jnp.bfloat16)
    activ_b = (pre_act * below).astype(jnp.bfloat16)
    ffn_out = linear(activ_b, w_outer) + b_outer.astype(f32)
    normed_two, factor_two = layer_norm(middle + ffn_out)
    layer_out = (normed_two * gain_ffn.astype(f32) + shift_ffn.astype(f32)).astype(jnp.bfloat16)
    layer_out = return_rows(layer_out.reshape(seq_count // 2, length, width), side)
    grad_gain_ffn = row_total(upstream * normed_two)
    grad_shift_ffn = row_total(upstream)
    d_res_two = norm_back(upstream * gain_ffn.astype(f32), normed_two, factor_two)
    d_ffn_b = d_res_two.astype(jnp.bfloat16)
    grad_b_outer = row_total(d_ffn_b)
    grad_w_outer = weight_grad(activ_b, d_ffn_b)
    s_outer, s_inner, s_query, s_key, s_value, s_attn_out, small, input_grad = backward(
        grad_w_outer, w_outer, w_inner, slope_b,
        (
            query_b, key_b, value_b, context_b, rows_b, middle_b, d_ffn_b, d_res_two, normed_one,
            w_query, w_key, w_value, w_attn_out,
        ),
        (factor_one, gain_attn.astype(f32).reshape(1, -1), lse, bias, grad_b_outer, grad_gain_ffn, grad_shift_ffn),
        hidden_in.shape,
    )
    return (
        layer_out,
        input_grad,
        s_query.astype(f32),
        small[0],
        s_key.astype(f32),
        s_value.astype(f32),
        small[1],
        s_attn_out.astype(f32),
        small[2],
        small[3],
        small[4],
        s_inner.astype(f32),
        small[8:12].reshape(-1),
        s_outer.astype(f32),
        small[5],
        small[6],
        small[7],
    )


def solution(mesh):
    in_specs = (
        P("batch", "mod", None),
        P("batch", None),
        P("batch"),
        P(),
        P(),
        P(),
        P(),
        P(),
        P(),
        P(),
        P(),
        P(),
        P(),
        P(),
        P(),
        P(),
        P(),
        P(),
        P("batch", "mod", None),
    )
    out_specs = (
        P("batch", "mod", None),
        P("batch", "mod", None),
        P(),
        P(),
        P(),
        P(),
        P(),
        P(),
        P(),
        P(),
        P(),
        P(),
        P(),
        P(),
        P(),
        P(),
        P(),
    )
    return jax.shard_map(
        on_device, mesh=mesh, in_specs=in_specs, out_specs=out_specs, check_vma=False
    )
```

```python
import functools

import jax
import jax.numpy as jnp
from jax import lax
from jax.experimental import pallas as pl
from jax.experimental.pallas import tpu as pltpu
from jax.sharding import PartitionSpec as P

MESH = pl.DeviceIdType.MESH
ROWS = 256
LANES = 768


class Wire:
    def __init__(self, extra_bits):
        self.b = lax.axis_index("batch")
        self.m = lax.axis_index("mod")
        self.core = lax.rem(self.b, 2)
        self.y = lax.rem(self.b // 2, 2)
        self.z = lax.rem(self.b // 4, 4)
        self.extra_bits = extra_bits

    def flip(self, bit):
        own = lax.rem(self.b // (1 << bit), 2)
        return (self.b + (1 - 2 * own) * (1 << bit), self.m)

    def peer(self, dim):
        if dim == "x":
            return (self.b, 1 - self.m)
        if dim == "y":
            return self.flip(1)
        if dim == "core":
            return self.flip(0)
        if dim == "up":
            return (self.b + 4, self.m)
        if dim == "down":
            return (self.b - 4, self.m)
        return self.flip(dim)

    def coord(self, dim):
        return self.m if dim == "x" else self.y

    def barrier(self):
        bar = pltpu.get_barrier_semaphore()
        peers = [self.peer(d) for d in ("core", "x", "y")]
        peers += [self.flip(bit) for bit in range(2, 4 + self.extra_bits)]
        for who in peers:
            pl.semaphore_signal(bar, inc=1, device_id=who, device_id_type=MESH)
        mid_low, mid_high = self.z == 1, self.z == 2

        @pl.when(mid_low)
        def _():
            pl.semaphore_signal(bar, inc=1, device_id=self.peer("up"), device_id_type=MESH)

        @pl.when(mid_high)
        def _():
            pl.semaphore_signal(bar, inc=1, device_id=self.peer("down"), device_id_type=MESH)

        pl.semaphore_wait(bar, len(peers) + jnp.where(mid_low | mid_high, 1, 0))


def plan_sizes(kinds, extra_bits):
    rows = sems = 0
    for kind in kinds:
        n = ROWS
        rows += ROWS
        sems += 1
        order = "xyz" if kind == "A" else "yxz" if kind == "B" else "zxy" if kind == "C" else "zyx"
        for dim in order:
            if dim == "z":
                rows += 6 * (n // 4)
                n //= 4
            else:
                rows += n // 2
                n //= 2
        rows += extra_bits * n
        sems += 6 + 6 + 4 + extra_bits + 1
    return rows, sems


def add_rows(acc, at, rb, rb_at, n):
    step = 64 if n > 64 else min(n, 32)

    def body(i, carry):
        d = pl.multiple_of(at + i * step, 16)
        s = pl.multiple_of(rb_at + i * step, 16)
        total = acc[pl.ds(d, step), :].astype(jnp.float32) + rb[pl.ds(s, step), :].astype(jnp.float32)
        acc[pl.ds(d, step), :] = total.astype(jnp.bfloat16)
        return carry

    if n == step:
        body(0, 0)
    else:
        lax.fori_loop(0, n // step, body, 0)


class Tasks:
    def __init__(self, wire, kinds, part, rb, ssem, rsem, block):
        self.w, self.acc, self.rb, self.block = wire, part, rb, block
        self.ssem, self.rsem = ssem, rsem
        self.rb_at = 0
        self.sem_at = 0
        self.homes = []
        self.steps = [self.build(t, kind) for t, kind in enumerate(kinds)]

    def space(self, n):
        at = self.rb_at
        self.rb_at += n
        return at

    def copy(self, src, dst, who):
        k = self.sem_at
        self.sem_at += 1
        return lambda: pltpu.make_async_remote_copy(
            src_ref=src(), dst_ref=dst(), send_sem=self.ssem.at[k], recv_sem=self.rsem.at[k], device_id=who, device_id_type=MESH
        )

    def rows(self, at, n):
        return self.acc.at[pl.ds(pl.multiple_of(at, 16), n), :]

    def build(self, t, kind):
        w = self.w
        steps = []
        home = (w.core * len(KINDS) + t) * ROWS
        away = ((1 - w.core) * len(KINDS) + t) * ROWS
        at0 = self.space(ROWS)

        def done(at, n):
            return self.rb.at[pl.ds(pl.multiple_of(at + (at0 - home), 16), n), :]

        def keep(at, n):
            self.rb[pl.ds(pl.multiple_of(at + (at0 - home), 16), n), :] = self.acc[pl.ds(pl.multiple_of(at, 16), n), :]

        def exchange(src, dst, who, then):
            cp = self.copy(src, dst, who)

            def begin():
                cp().start()

            def finish():
                cp().wait()
                then()

            steps.append((begin, finish))

        def reduce(dim, base, n):
            half, a = n // 2, w.coord(dim)
            at = self.space(half)
            kept = base + a * half
            sent = base + (1 - a) * half
            exchange(
                lambda: self.rows(sent, half),
                lambda: self.rb.at[pl.ds(at, half), :],
                w.peer(dim),
                lambda: add_rows(self.acc, kept, self.rb, at, half),
            )
            return kept, half

        def gather(dim, base, n):
            exchange(lambda: done(base, n), lambda: done(base, n), w.peer(dim), lambda: None)

        def line_reduce(base, n):
            q, z, zz = n // 4, w.z, 3 - w.z
            for s in (1, 2, 3):
                up_at, down_at = self.space(q), self.space(q)
                up_sends, up_gets = (z < 3) & (s >= z + 1), (z >= 1) & (s >= z)
                down_sends, down_gets = (zz < 3) & (s >= zz + 1), (zz >= 1) & (s >= zz)
                up_src = base + jnp.clip(4 - s + z, 0, 3) * q
                down_src = base + jnp.clip(s + z - 4, 0, 3) * q
                up_add = base + jnp.clip(3 - s + z, 0, 3) * q
                down_add = base + jnp.clip(s - 3 + z, 0, 3) * q
                up = self.copy(lambda v=up_src: self.rows(v, q), lambda v=up_at: self.rb.at[pl.ds(v, q), :], w.peer("up"))
                down = self.copy(lambda v=down_src: self.rows(v, q), lambda v=down_at: self.rb.at[pl.ds(v, q), :], w.peer("down"))
                steps.append(line_step(up, down, up_sends, up_gets, down_sends, down_gets,
                                       lambda a=up_add, r=up_at: add_rows(self.acc, a, self.rb, r, q),
                                       lambda a=down_add, r=down_at: add_rows(self.acc, a, self.rb, r, q)))
            return base + z * q, q

        def line_gather(base, q):
            z = w.z
            for s in (1, 2, 3):
                up_sends, up_gets = (z < 3) & (z - (s - 1) >= 0), z - s >= 0
                down_sends, down_gets = (z > 0) & (z + (s - 1) <= 3), z + s <= 3
                up_src = base + jnp.clip(z - s + 1, 0, 3) * q
                down_src = base + jnp.clip(z + s - 1, 0, 3) * q
                up = self.copy(lambda v=up_src: done(v, q), lambda v=up_src: done(v, q), w.peer("up"))
                down = self.copy(lambda v=down_src: done(v, q), lambda v=down_src: done(v, q), w.peer("down"))
                steps.append(line_step(up, down, up_sends, up_gets, down_sends, down_gets, None, None))

        def line_step(up, down, up_sends, up_gets, down_sends, down_gets, up_then, down_then):
            def begin():
                @pl.when(up_sends)
                def _():
                    up().start()

                @pl.when(down_sends)
                def _():
                    down().start()

            def finish():
                for cp, gets, then in ((up, up_gets, up_then), (down, down_gets, down_then)):
                    @pl.when(gets)
                    def _(cp=cp, then=then):
                        cp().wait_recv()
                        if then is not None:
                            then()

                for cp, sends in ((up, up_sends), (down, down_sends)):
                    @pl.when(sends)
                    def _(cp=cp):
                        cp().wait_send()

            return begin, finish

        def then_keep(base, n):
            begin, finish = steps.pop()

            def finish_and_keep():
                finish()
                keep(base, n)

            steps.append((begin, finish_and_keep))

        def widen(base, n):
            for bit in range(4, 4 + w.extra_bits):
                at = self.space(n)
                exchange(
                    lambda: self.rows(base, n),
                    lambda at=at: self.rb.at[pl.ds(at, n), :],
                    w.peer(bit),
                    lambda at=at: add_rows(self.acc, base, self.rb, at, n),
                )

        exchange(
            lambda: self.rows(away, ROWS),
            lambda: self.rb.at[pl.ds(at0, ROWS), :],
            w.peer("core"),
            lambda: add_rows(self.acc, home, self.rb, at0, ROWS),
        )
        if kind in "AB":
            d1, d2 = ("x", "y") if kind == "A" else ("y", "x")
            b1, n1 = reduce(d1, home, ROWS)
            b2, n2 = reduce(d2, b1, n1)
            b3, n3 = line_reduce(b2, n2)
            widen(b3, n3)
            then_keep(b3, n3)
            line_gather(b2, n3)
            gather(d2, b2, n2)
            gather(d1, b1, n1)
        else:
            d1, d2 = ("x", "y") if kind == "C" else ("y", "x")
            b1, n1 = line_reduce(home, ROWS)
            b2, n2 = reduce(d1, b1, n1)
            b3, n3 = reduce(d2, b2, n2)
            widen(b3, n3)
            then_keep(b3, n3)
            gather(d2, b3, n3)
            gather(d1, b2, n2)
            line_gather(home, n1)
        k = self.sem_at
        self.sem_at += 1

        def last(block):
            return pltpu.make_async_remote_copy(
                src_ref=self.rb.at[pl.ds(at0, ROWS), :], dst_ref=block, send_sem=self.ssem.at[k], recv_sem=self.rsem.at[k],
                device_id=w.peer("core"), device_id_type=MESH)

        final = by_core(w.core, lambda half: last(self.block(half, t)), t)
        steps.append((lambda: final.start(), lambda: final.wait()))
        self.homes.append(at0)
        return steps

    def op(self, t, p):
        steps = self.steps[t]
        if p > 0:
            steps[p - 1][1]()
        if p < len(steps):
            steps[p][0]()


KINDS = "ABCABDABCABDABCABD"
ORDER = (
    1, 4, 0, 3, 2, -1, 5, -1, 1, 0, 3, 2, 5, -1, 4, -1, -1, 2, 7, -1, 0, 6, 1, 8, 5, -1, 7, 6, 2, -1, 3, 8, 4, -1, 0, 1,
    -1, 5, 2, -1, 0, 9, 6, 11, 10, 7, 1, 8, -1, 4, 9, 0, 2, 5, 3, 11, 1, -1, 10, -1, 5, 0, 6, 4, 3, -1, 8, 5, 9, 6, 0, 7,
    4, 2, 1, -1, 10, 2, 5, 3, 8, 6, 0, 4, 1, 11, -1, 10, 7, 1, 5, 0, 9, 2, 6, 8, -1, -1, 1, 9, 10, 12, 13, 8, 7, 14, 11, 0,
    3, 4, -1, 1, 8, 2, 15, 5, 17, 13, 7, 14, 9, 6, 3, 16, 11, 12, 17, 10, 8, 15, 2, 16, -1, 14, 17, 3, 13, 4, 1, 6, 5, 0, 12, 7,
    2, 9, 10, 11, 3, 4, 15, 16, 14, 13, 6, 8, 0, 17, 5, 11, 12, 7, 4, 3, 13, 9, 1, 14, 12, 10, 16, 15, 8, 16, 11, 6, 17, 5, 15, 13,
    12, 3, 9, 7, 10, 16, 15, 13, 14, 11, 17, 2, 9, 12, 10, 16, 13, 14, 8, 15, 4, 6, 7, 3, 17, 12, 9, 11, 14, 16, 8, 13, 17, 4, 10, 12,
    12, 15, 13, 11, 15, 16, 7, 9, 14, 17, 11, 16, 6, 15, 9, 10, 14, 13, 12, 17, 16, 15, 10, 14, 14, 17, 13, 12, 17, 15, 16, 13, 11, 12, 14, 17,
    7, 15, 16,
)
SMALL = 16


def block_of(refs, half, t):
    if t < 6:
        return refs[0].at[pl.ds(pl.multiple_of(half * 1536 + t * ROWS, ROWS), ROWS), :]
    if t < 12:
        i, j = (t - 6) % 3, (t - 6) // 3
        return refs[1].at[pl.ds(i * ROWS, ROWS), pl.ds(pl.multiple_of((half * 2 + j) * LANES, LANES), LANES)]
    return refs[2 + 2 * half + (t - 12) // 3].at[pl.ds((t - 12) % 3 * ROWS, ROWS), :]


class Branches:
    def __init__(self, core, make):
        self.core, self.make = core, make

    def start(self):
        for core in range(2):
            @pl.when(self.core == core)
            def _(core=core):
                self.make(core).start()

    def wait(self):
        self.make(0).wait()


class Plain:
    def __init__(self, make):
        self.make = make

    def start(self):
        self.make().start()

    def wait(self):
        self.make().wait()


def by_core(core, make, t):
    return Plain(lambda: make(core)) if t < 12 else Branches(core, make)


def tn(a, b):
    return lax.dot_general(a, b, (((0,), (0,)), ((), ())), preferred_element_type=jnp.float32)


FULL = ("q", "k", "v", "ctx", "x", "mid", "dffn", "dmid", "normed", "wq", "wk", "wv", "wo")


def back_kernel(extra_bits, *refs):
    g_outer, w_outer, w_inner, slope, *refs = refs
    full_in, refs = dict(zip(FULL, refs)), refs[len(FULL):]
    factor, gain, lse, bias_ref, sum_outer, sum_gain, sum_shift, *refs = refs
    outs, small_out, grad_out, refs = refs[:6], refs[6], refs[7], refs[8:]
    v, refs = dict(zip(FULL, refs)), refs[len(FULL):]
    wou, win, gp, dp, dc, db, dq, dk, dv, ig, part, rb, small, small_rb, ssem, rsem, lsem, vsem, fsem, tsem, osem, isem = refs
    w = Wire(extra_bits)
    count = len(KINDS)
    f32 = jnp.float32
    rows = dp.shape[0]
    length = bias_ref.shape[0] // lse.shape[0]
    order = (0, 2, 1, 3)

    def load(half, t):
        to = part.at[pl.ds((half * count + t) * ROWS, ROWS), :]
        return pltpu.make_async_copy(g_outer.at[pl.ds(half * 1536 + t * ROWS, ROWS), :], to, lsem.at[half, t])

    def fetch(name):
        return pltpu.make_async_copy(full_in[name], v[name], fsem.at[FULL.index(name)])

    def tile(which, n):
        at, slot = order[n] * LANES, n % 2
        source, to = (
            (w_outer.at[pl.ds(at, LANES), :], wou),
            (w_inner.at[:, pl.ds(at, LANES)], win),
            (slope.at[:, pl.ds(at, LANES)], gp),
        )[which]
        return pltpu.make_async_copy(source, to.at[slot], tsem.at[which, n])

    for t in range(6):
        load(0, t).start()
        load(1, t).start()
        if t == 0:
            fetch("dffn").start()
            tile(0, 0).start()
            tile(2, 0).start()
            fetch("mid").start()
            tile(1, 0).start()
            fetch("dmid").start()
    for which in range(3):
        tile(which, 1).start()
    for name in ("normed", "wo", "ctx", "k", "q", "v", "x", "wq", "wk", "wv"):
        fetch(name).start()
    w.barrier()
    tasks = Tasks(w, KINDS, part, rb, ssem, rsem, lambda half, t: block_of(outs, half, t))

    def store(t):
        def make(half):
            return pltpu.make_async_copy(rb.at[pl.ds(tasks.homes[t], ROWS), :], block_of(outs, half, t), osem.at[t])

        return by_core(w.core, make, t)

    def grad_blocks(left, right, half, t):
        to = pl.ds((half * count + t) * ROWS, left.shape[1])
        part[to, :] = tn(left[...], right[...]).astype(jnp.bfloat16)

    def by_rows(step, body, carry=0):
        def wrapped(r, carry):
            return body(pl.ds(pl.multiple_of(r * step, step), step), carry)

        return lax.fori_loop(0, rows // step, wrapped, carry)

    none = jnp.zeros((1, LANES), f32)

    def d_pre(n):
        tile(0, n).wait()
        tile(2, n).wait()
        if n == 0:
            fetch("dffn").wait()

        def body(at, total):
            d = (nt(v["dffn"][at, :], wou[n % 2]) * gp[n % 2, at, :].astype(f32)).astype(jnp.bfloat16)
            dp[at, :] = d
            return total + jnp.sum(d.astype(f32), axis=0, keepdims=True)

        small[0, 8 + order[n]:9 + order[n], :] = by_rows(256, body, none)
        if n + 2 < 4:
            tile(0, n + 2).start()
            tile(2, n + 2).start()

    def inner_blocks(n):
        if n == 0:
            fetch("mid").wait()
        grad_blocks(v["mid"], dp, order[n] // 2, 6 + 3 * (order[n] % 2))

    def d_mid(n):
        tile(1, n).wait()
        if n == 0:
            fetch("dmid").wait()

        def body(at, carry):
            v["dmid"][at, :] += nt(dp[at, :], win[n % 2])
            return carry

        by_rows(256, body)
        if n + 2 < 4:
            tile(1, n + 2).start()

    def norm_step():
        fetch("normed").wait()

        def body(at, sums):
            d, normed = v["dmid"][at, :], v["normed"][at, :]
            e = d * gain[...]
            res = factor[at, :] * (
                e - jnp.mean(e, axis=-1, keepdims=True) - normed * jnp.mean(e * normed, axis=-1, keepdims=True)
            )
            low = res.astype(jnp.bfloat16)
            v["dmid"][at, :] = res
            db[at, :] = low
            return (
                sums[0] + jnp.sum(low.astype(f32), axis=0, keepdims=True),
                sums[1] + jnp.sum(d * normed, axis=0, keepdims=True),
                sums[2] + jnp.sum(d, axis=0, keepdims=True),
            )

        sums = by_rows(128, body, (none, none, none))
        for i in range(3):
            small[0, 2 + i:3 + i, :] = sums[i]

    def d_context():
        fetch("wo").wait()

        dc[...] = nt(db[...], v["wo"][...]).astype(jnp.bfloat16)

    def out_blocks():
        fetch("ctx").wait()
        grad_blocks(v["ctx"], db, 1, 15)

    def attention(seq, count):
        if seq == 0:
            for name in ("q", "k", "v"):
                fetch(name).wait()
        at = pl.ds(seq * length, length)
        bias = jnp.concatenate([bias_ref[at, :]] * (length // 128), axis=1)

        def body(step, carry):
            first = step * count
            columns = [pl.ds(pl.multiple_of((first + i) * 128, 128), 128) for i in range(count)]
            found = attend_back(
                [(v["q"][at, c], v["k"][at, c], v["v"][at, c], dc[at, c], lse[seq, first + i]) for i, c in enumerate(columns)],
                bias)
            for c, (d_query, d_key, d_value) in zip(columns, found):
                dq[at, c], dk[at, c], dv[at, c] = d_query, d_key, d_value
            return carry

        lax.fori_loop(0, lse.shape[1] // count, body, 0)

    def total_rows(ref, row):
        def body(at, total):
            return total + jnp.sum(ref[at, :].astype(f32), axis=0, keepdims=True)

        small[0, row:row + 1, :] = by_rows(128, body, none)

    def value_blocks():
        grad_blocks(v["x"], dv, 1, 12)
        total_rows(dv, 1)

    def query_blocks():
        fetch("x").wait()
        grad_blocks(v["x"], dq, 0, 12)
        total_rows(dq, 0)

    def key_blocks():
        grad_blocks(v["x"], dk, 0, 15)

    def grad_copy(seq, away):
        source = ig.at[2 * seq + (1 - w.m if away else w.m)]
        to = grad_out.at[w.m * lse.shape[0] + seq]
        if not away:
            return pltpu.make_async_copy(source, to, isem.at[2, seq])
        return pltpu.make_async_remote_copy(
            src_ref=source, dst_ref=to, send_sem=isem.at[0, seq], recv_sem=isem.at[1, seq],
            device_id=w.peer("x"), device_id_type=MESH)

    def input_rows():
        for name in ("wq", "wk", "wv"):
            fetch(name).wait()

        def body(seq, carry):
            at = pl.ds(pl.multiple_of(seq * length, length), length)
            total = v["dmid"][at, :] + nt(dq[at, :], v["wq"][...])
            total = total + nt(dk[at, :], v["wk"][...]) + nt(dv[at, :], v["wv"][...])
            for i in range(length // 128):
                ig[2 * seq + i] = total[i * 128:i * 128 + 128].astype(jnp.bfloat16)
            return carry

        lax.fori_loop(0, lse.shape[0], body, 0)
        for seq in range(lse.shape[0]):
            grad_copy(seq, True).start()
            grad_copy(seq, False).start()

    small[0, 12:16, :] = jnp.zeros((4, LANES), f32)
    for row, ref in ((5, sum_outer), (6, sum_gain), (7, sum_shift)):
        small[0, row:row + 1, :] = ref[...]
    hops = ["core", "x", "y"] + list(range(2, 4 + extra_bits))

    def small_copy(k):
        return pltpu.make_async_remote_copy(
            src_ref=small.at[k], dst_ref=small_rb.at[k], send_sem=vsem.at[0, k], recv_sem=vsem.at[1, k],
            device_id=w.peer(hops[k]), device_id_type=MESH)

    def small_op(k):
        if k > 0:
            small_copy(k - 1).wait()
            small[k] = small[k - 1] + small_rb[k - 1]
        if k < len(hops):
            small_copy(k).start()

    seqs = lse.shape[0]
    work = [job for n in range(4) for job in ((d_pre, n), (inner_blocks, n), (d_mid, n))]
    work += [(norm_step,), (d_context,), (out_blocks,)] + [(attention, seq, 3) for seq in range(seqs)]
    work += [(query_blocks,), (value_blocks,), (key_blocks,), (input_rows,)]

    def comm(t, p):
        if t == count:
            small_op(p)
            return
        if p == 0 and t < 6:
            load(0, t).wait()
            load(1, t).wait()
        tasks.op(t, p)
        if p == len(tasks.steps[t]) - 1:
            store(t).start()

    at, vectors, since = [0] * count, 0, 0
    for t in ORDER:
        if t < 0:
            job = work.pop(0)
            job[0](*job[1:])
            continue
        comm(t, at[t])
        at[t] += 1
        since += 1
        if len(work) < 2 and since >= 6 and vectors <= len(hops):
            comm(count, vectors)
            vectors, since = vectors + 1, 0
    for k in range(vectors, len(hops) + 1):
        comm(count, k)
    for _ in range(extra_bits):
        for t in range(count):
            comm(t, at[t])
            at[t] += 1
    small_out[...] = small[len(hops)]
    for t in range(count):
        store(t).wait()
    for seq in range(seqs):
        grad_copy(seq, False).wait()
        grad_copy(seq, True).wait()


def backward(g_outer, w_outer, w_inner, slope, full, blocks, shape):
    extra_bits = (lax.axis_size("batch") // 16).bit_length() - 1
    space, sems = plan_sizes(KINDS, extra_bits)
    hops = 5 + extra_bits
    count = len(KINDS)
    low, f32 = jnp.bfloat16, jnp.float32
    hbm = pl.BlockSpec(memory_space=pl.ANY)
    vmem = pl.BlockSpec(memory_space=pltpu.VMEM)
    rows, width = full[0].shape
    grads = [g_outer.shape, w_inner.shape] + [(width, width)] * 4
    flat = pltpu.VMEM((rows, width), low)
    return pl.pallas_call(
        functools.partial(back_kernel, extra_bits),
        out_shape=tuple(jax.ShapeDtypeStruct(g, low) for g in grads)
        + (jax.ShapeDtypeStruct((SMALL, LANES), f32), jax.ShapeDtypeStruct(shape, low)),
        in_specs=[hbm] * (4 + len(full)) + [vmem] * len(blocks),
        out_specs=(hbm,) * len(grads) + (vmem, hbm),
        scratch_shapes=[pltpu.VMEM(m.shape, m.dtype) for m in full]
        + [
            pltpu.VMEM((2, LANES, LANES), low),
            pltpu.VMEM((2, LANES, LANES), low),
            pltpu.VMEM((2, rows, LANES), low),
            flat, flat, flat, flat, flat, flat,
            pltpu.VMEM((rows // 128, 128, width), low),
            pltpu.VMEM((2 * count * ROWS, LANES), low),
            pltpu.VMEM((space, LANES), low),
            pltpu.VMEM((hops + 1, SMALL, LANES), f32),
            pltpu.VMEM((hops, SMALL, LANES), f32),
            pltpu.SemaphoreType.DMA((sems,)),
            pltpu.SemaphoreType.DMA((sems,)),
            pltpu.SemaphoreType.DMA((2, 6)),
            pltpu.SemaphoreType.DMA((2, hops)),
            pltpu.SemaphoreType.DMA((len(full),)),
            pltpu.SemaphoreType.DMA((3, 4)),
            pltpu.SemaphoreType.DMA((count,)),
            pltpu.SemaphoreType.DMA((3, shape[0] // 2)),
        ],
        compiler_params=pltpu.CompilerParams(collective_id=1, has_side_effects=True, vmem_limit_bytes=62 << 20),
    )(g_outer, w_outer, w_inner, slope, *full, *blocks)


def nt(a, b):
    return lax.dot_general(a, b, (((1,), (1,)), ((), ())), preferred_element_type=jnp.float32)


def nn(a, b):
    return lax.dot_general(a, b, (((1,), (0,)), ((), ())), preferred_element_type=jnp.float32)


def low_lanes(rows):
    return lax.broadcasted_iota(jnp.int32, (rows, 128), 1) < 64


def heads_of(pairs):
    return [(i, head) for i in range(len(pairs)) for head in range(2)]


def own_lanes(block, head):
    low = low_lanes(block.shape[0])
    return jnp.where(low if head == 0 else ~low, block, jnp.zeros_like(block))


def attend(pairs, bias):
    heads = heads_of(pairs)
    scores = [nt(own_lanes(pairs[i][1], head), pairs[i][0]) + bias for i, head in heads]
    tops = [jnp.max(s, axis=0, keepdims=True) for s in scores]
    expo = [jnp.exp(s - top) for s, top in zip(scores, tops)]
    totals = [jnp.sum(e, axis=0, keepdims=True) for e in expo]
    vt = [pair[2].T for pair in pairs]
    context = [
        nn(vt[i][head * 64:head * 64 + 64], e.astype(jnp.bfloat16)) * (1.0 / total)
        for e, total, (i, head) in zip(expo, totals, heads)
    ]
    logs = [top + jnp.log(total) for top, total in zip(tops, totals)]
    return [
        (jnp.concatenate(context[2 * i:2 * i + 2], axis=0).T.astype(jnp.bfloat16), jnp.concatenate(logs[2 * i:2 * i + 2], axis=0))
        for i in range(len(pairs))
    ]


def attend_back(pairs, bias):
    heads = heads_of(pairs)
    kt = [pair[1].T for pair in pairs]
    scores = [nt(own_lanes(pairs[i][1], head), pairs[i][0]) for i, head in heads]
    d_probs = [nt(own_lanes(pairs[i][2], head), pairs[i][3]) for i, head in heads]
    probs = [jnp.exp(s + (bias - pairs[i][4][head:head + 1])) for s, (i, head) in zip(scores, heads)]
    inner = [jnp.sum(p * d, axis=0, keepdims=True) for p, d in zip(probs, d_probs)]
    d_scores = [(p * (d - one)).astype(jnp.bfloat16) for p, d, one in zip(probs, d_probs, inner)]
    probs_low = [p.astype(jnp.bfloat16) for p in probs]
    dq = [nn(kt[i][head * 64:head * 64 + 64], d) for d, (i, head) in zip(d_scores, heads)]
    dk = [nn(d, pairs[i][0]) for d, (i, head) in zip(d_scores, heads)]
    dv = [nn(p, pairs[i][3]) for p, (i, head) in zip(probs_low, heads)]
    low = low_lanes(pairs[0][0].shape[0])
    return [
        (
            (jnp.concatenate(dq[2 * i:2 * i + 2], axis=0) * 0.125).T.astype(jnp.bfloat16),
            jnp.where(low, dk[2 * i], dk[2 * i + 1]).astype(jnp.bfloat16),
            jnp.where(low, dv[2 * i], dv[2 * i + 1]).astype(jnp.bfloat16),
        )
        for i in range(len(pairs))
    ]


def forward_kernel(q_ref, k_ref, v_ref, bias_ref, ctx_ref, lse_ref):
    length, width = q_ref.shape
    bias = jnp.concatenate([bias_ref[...]] * (length // 128), axis=1)

    def body(step, carry):
        columns = [pl.ds(pl.multiple_of((step * 3 + i) * 128, 128), 128) for i in range(3)]
        found = attend([(q_ref[:, c], k_ref[:, c], v_ref[:, c]) for c in columns], bias)
        for i, (context, logs) in enumerate(found):
            ctx_ref[:, columns[i]] = context
            lse_ref[0, step * 3 + i] = logs
        return carry

    lax.fori_loop(0, width // 384, body, 0)


def attention_forward(q, k, v, bias, length):
    rows, width = q.shape
    seqs, pairs = rows // length, width // 128
    block = pl.BlockSpec((length, width), lambda s: (s, 0))
    return pl.pallas_call(
        forward_kernel,
        grid=(seqs,),
        out_shape=(jax.ShapeDtypeStruct(q.shape, jnp.bfloat16), jax.ShapeDtypeStruct((seqs, pairs, 2, length), jnp.float32)),
        in_specs=[block, block, block, pl.BlockSpec((length, 128), lambda s: (s, 0))],
        out_specs=(block, pl.BlockSpec((1, pairs, 2, length), lambda s: (s, 0, 0, 0))),
    )(q, k, v, bias)


def widen_kernel(*refs):
    for source, to in zip(refs[:len(refs) // 2], refs[len(refs) // 2:]):
        to[...] = source[...].astype(jnp.float32)


def to_float32(arrays):
    steps = 12
    blocks = [pl.BlockSpec((a.shape[0] // steps, a.shape[1]), lambda i: (i, 0)) for a in arrays]
    return pl.pallas_call(
        widen_kernel,
        grid=(steps,),
        out_shape=tuple(jax.ShapeDtypeStruct(a.shape, jnp.float32) for a in arrays),
        in_specs=blocks,
        out_specs=tuple(blocks),
    )(*arrays)


epsilon = 1e-05


def to_partner(block):
    return lax.ppermute(block, "mod", [(0, 1), (1, 0)])


def take_side(array, axis, side):
    half = array.shape[axis] // 2
    return lax.dynamic_slice_in_dim(array, side * half, half, axis)


def gather_sequences(array, side):
    own = take_side(array, 0, side)
    other = to_partner(take_side(array, 0, 1 - side))
    both = jnp.where(side == 0, jnp.concatenate((own, other), axis=1), jnp.concatenate((other, own), axis=1))
    return both.reshape(-1, array.shape[2])


def return_rows(array, side):
    own = take_side(array, 1, side)
    other = to_partner(take_side(array, 1, 1 - side))
    return jnp.where(side == 0, jnp.concatenate((own, other)), jnp.concatenate((other, own)))


def linear(rows, weight_matrix):
    return lax.dot_general(rows, weight_matrix, (((1,), (0,)), ((), ())), preferred_element_type=jnp.float32)


def back_linear(gradient_rows, weight_matrix):
    return lax.dot_general(gradient_rows, weight_matrix, (((1,), (1,)), ((), ())), preferred_element_type=jnp.float32)


def weight_grad(layer_inputs, gradient_rows):
    return lax.dot_general(
        layer_inputs, gradient_rows, (((0,), (0,)), ((), ())), preferred_element_type=jnp.float32
    ).astype(jnp.bfloat16)


def row_total(values):
    return jnp.sum(values.astype(jnp.float32), axis=0, keepdims=True)


def layer_norm(rows):
    centre = rows - jnp.mean(rows, axis=-1, keepdims=True)
    factor = lax.rsqrt(jnp.mean(centre * centre, axis=-1, keepdims=True) + epsilon)
    return (centre * factor, factor)


def norm_back(gradient_rows, normed, factor):
    return factor * (
        gradient_rows
        - jnp.mean(gradient_rows, axis=-1, keepdims=True)
        - normed * jnp.mean(gradient_rows * normed, axis=-1, keepdims=True)
    )


def on_device(
    hidden_in,
    text_mask,
    region_count,
    w_query,
    b_query,
    w_key,
    w_value,
    b_value,
    w_attn_out,
    b_attn_out,
    gain_attn,
    shift_attn,
    w_inner,
    b_inner,
    w_outer,
    b_outer,
    gain_ffn,
    shift_ffn,
    cotangent,
):
    seq_count, half_len, width = hidden_in.shape
    length = 2 * half_len
    side = lax.axis_index("mod")
    f32 = jnp.float32
    rows_b = gather_sequences(hidden_in, side)
    upstream = gather_sequences(cotangent, side).astype(f32)
    mask = take_side(text_mask, 0, side) == 1
    regions = take_side(region_count, 0, side)
    slot_ok = lax.broadcasted_iota(jnp.int32, mask.shape, 1) < regions[:, None]
    bias = jnp.where(jnp.concatenate((mask, slot_ok), axis=1), f32(0.0), f32(-1000000000.0)).reshape(-1, 1)
    bias = jnp.broadcast_to(bias, (bias.shape[0], 128))

    query_b = ((linear(rows_b, w_query) + b_query.astype(f32)).astype(jnp.bfloat16) * jnp.bfloat16(0.125))
    key_b = linear(rows_b, w_key).astype(jnp.bfloat16)
    value_b = (linear(rows_b, w_value) + b_value.astype(f32)).astype(jnp.bfloat16)
    context_b, lse = attention_forward(query_b, key_b, value_b, bias, length)
    branch = linear(context_b, w_attn_out) + b_attn_out.astype(f32)
    normed_one, factor_one = layer_norm(rows_b.astype(f32) + branch)
    middle = normed_one * gain_attn.astype(f32) + shift_attn.astype(f32)
    middle_b = middle.astype(jnp.bfloat16)
    pre_act = linear(middle_b, w_inner) + b_inner.astype(f32)
    below = 0.5 * (1.0 + lax.erf(pre_act * f32(0.7071067811865476)))
    slope_b = (below + pre_act * (jnp.exp(-0.5 * pre_act * pre_act) * f32(0.3989422804014327))).astype(jnp.bfloat16)
    activ_b = (pre_act * below).astype(jnp.bfloat16)
    ffn_out = linear(activ_b, w_outer) + b_outer.astype(f32)
    normed_two, factor_two = layer_norm(middle + ffn_out)
    layer_out = (normed_two * gain_ffn.astype(f32) + shift_ffn.astype(f32)).astype(jnp.bfloat16)
    layer_out = return_rows(layer_out.reshape(seq_count // 2, length, width), side)
    grad_gain_ffn = row_total(upstream * normed_two)
    grad_shift_ffn = row_total(upstream)
    d_res_two = norm_back(upstream * gain_ffn.astype(f32), normed_two, factor_two)
    d_ffn_b = d_res_two.astype(jnp.bfloat16)
    grad_b_outer = row_total(d_ffn_b)
    grad_w_outer = weight_grad(activ_b, d_ffn_b)
    s_outer, s_inner, s_query, s_key, s_value, s_attn_out, small, input_grad = backward(
        grad_w_outer, w_outer, w_inner, slope_b,
        (
            query_b, key_b, value_b, context_b, rows_b, middle_b, d_ffn_b, d_res_two, normed_one,
            w_query, w_key, w_value, w_attn_out,
        ),
        (factor_one, gain_attn.astype(f32).reshape(1, -1), lse, bias, grad_b_outer, grad_gain_ffn, grad_shift_ffn),
        hidden_in.shape,
    )
    s_outer, s_inner, s_query, s_key, s_value, s_attn_out = to_float32(
        (s_outer, s_inner, s_query, s_key, s_value, s_attn_out)
    )
    return (
        layer_out,
        input_grad,
        s_query,
        small[0],
        s_key,
        s_value,
        small[1],
        s_attn_out,
        small[2],
        small[3],
        small[4],
        s_inner,
        small[8:12].reshape(-1),
        s_outer,
        small[5],
        small[6],
        small[7],
    )


def solution(mesh):
    in_specs = (
        P("batch", "mod", None),
        P("batch", None),
        P("batch"),
        P(),
        P(),
        P(),
        P(),
        P(),
        P(),
        P(),
        P(),
        P(),
        P(),
        P(),
        P(),
        P(),
        P(),
        P(),
        P("batch", "mod", None),
    )
    out_specs = (
        P("batch", "mod", None),
        P("batch", "mod", None),
        P(),
        P(),
        P(),
        P(),
        P(),
        P(),
        P(),
        P(),
        P(),
        P(),
        P(),
        P(),
        P(),
        P(),
        P(),
    )
    return jax.shard_map(
        on_device, mesh=mesh, in_specs=in_specs, out_specs=out_specs, check_vma=False
    )
```

```python
import functools

import jax
import jax.numpy as jnp
from jax import lax
from jax.experimental import pallas as pl
from jax.experimental.pallas import tpu as pltpu
from jax.sharding import PartitionSpec as P

MESH = pl.DeviceIdType.MESH
ROWS = 256
LANES = 768


class Wire:
    def __init__(self, extra_bits):
        self.b = lax.axis_index("batch")
        self.m = lax.axis_index("mod")
        self.core = lax.rem(self.b, 2)
        self.y = lax.rem(self.b // 2, 2)
        self.z = lax.rem(self.b // 4, 4)
        self.extra_bits = extra_bits

    def flip(self, bit):
        own = lax.rem(self.b // (1 << bit), 2)
        return (self.b + (1 - 2 * own) * (1 << bit), self.m)

    def peer(self, dim):
        if dim == "x":
            return (self.b, 1 - self.m)
        if dim == "y":
            return self.flip(1)
        if dim == "core":
            return self.flip(0)
        if dim == "up":
            return (self.b + 4, self.m)
        if dim == "down":
            return (self.b - 4, self.m)
        return self.flip(dim)

    def coord(self, dim):
        return self.m if dim == "x" else self.y

    def barrier(self):
        bar = pltpu.get_barrier_semaphore()
        peers = [self.peer(d) for d in ("core", "x", "y")]
        peers += [self.flip(bit) for bit in range(2, 4 + self.extra_bits)]
        for who in peers:
            pl.semaphore_signal(bar, inc=1, device_id=who, device_id_type=MESH)
        mid_low, mid_high = self.z == 1, self.z == 2

        @pl.when(mid_low)
        def _():
            pl.semaphore_signal(bar, inc=1, device_id=self.peer("up"), device_id_type=MESH)

        @pl.when(mid_high)
        def _():
            pl.semaphore_signal(bar, inc=1, device_id=self.peer("down"), device_id_type=MESH)

        pl.semaphore_wait(bar, len(peers) + jnp.where(mid_low | mid_high, 1, 0))


def plan_sizes(kinds, extra_bits):
    rows = sems = 0
    for kind in kinds:
        n = ROWS
        rows += ROWS
        sems += 1
        order = "xyz" if kind == "A" else "yxz" if kind == "B" else "zxy" if kind == "C" else "zyx"
        for dim in order:
            if dim == "z":
                rows += 6 * (n // 4)
                n //= 4
            else:
                rows += n // 2
                n //= 2
        rows += extra_bits * n
        sems += 6 + 6 + 4 + extra_bits + 1
    return rows, sems


def add_rows(acc, at, rb, rb_at, n):
    step = 64 if n > 64 else min(n, 32)

    def body(i, carry):
        d = pl.multiple_of(at + i * step, 16)
        s = pl.multiple_of(rb_at + i * step, 16)
        total = acc[pl.ds(d, step), :].astype(jnp.float32) + rb[pl.ds(s, step), :].astype(jnp.float32)
        acc[pl.ds(d, step), :] = total.astype(jnp.bfloat16)
        return carry

    if n == step:
        body(0, 0)
    else:
        lax.fori_loop(0, n // step, body, 0)


class Tasks:
    def __init__(self, wire, kinds, part, rb, ssem, rsem, block):
        self.w, self.acc, self.rb, self.block = wire, part, rb, block
        self.ssem, self.rsem = ssem, rsem
        self.rb_at = 0
        self.sem_at = 0
        self.homes = []
        self.steps = [self.build(t, kind) for t, kind in enumerate(kinds)]

    def space(self, n):
        at = self.rb_at
        self.rb_at += n
        return at

    def copy(self, src, dst, who):
        k = self.sem_at
        self.sem_at += 1
        return lambda: pltpu.make_async_remote_copy(
            src_ref=src(), dst_ref=dst(), send_sem=self.ssem.at[k], recv_sem=self.rsem.at[k], device_id=who, device_id_type=MESH
        )

    def rows(self, at, n):
        return self.acc.at[pl.ds(pl.multiple_of(at, 16), n), :]

    def build(self, t, kind):
        w = self.w
        steps = []
        home = (w.core * len(KINDS) + t) * ROWS
        away = ((1 - w.core) * len(KINDS) + t) * ROWS
        at0 = self.space(ROWS)

        def done(at, n):
            return self.rb.at[pl.ds(pl.multiple_of(at + (at0 - home), 16), n), :]

        def keep(at, n):
            self.rb[pl.ds(pl.multiple_of(at + (at0 - home), 16), n), :] = self.acc[pl.ds(pl.multiple_of(at, 16), n), :]

        def exchange(src, dst, who, then):
            cp = self.copy(src, dst, who)

            def begin():
                cp().start()

            def finish():
                cp().wait()
                then()

            steps.append((begin, finish))

        def reduce(dim, base, n):
            half, a = n // 2, w.coord(dim)
            at = self.space(half)
            kept = base + a * half
            sent = base + (1 - a) * half
            exchange(
                lambda: self.rows(sent, half),
                lambda: self.rb.at[pl.ds(at, half), :],
                w.peer(dim),
                lambda: add_rows(self.acc, kept, self.rb, at, half),
            )
            return kept, half

        def gather(dim, base, n):
            exchange(lambda: done(base, n), lambda: done(base, n), w.peer(dim), lambda: None)

        def line_reduce(base, n):
            q, z, zz = n // 4, w.z, 3 - w.z
            for s in (1, 2, 3):
                up_at, down_at = self.space(q), self.space(q)
                up_sends, up_gets = (z < 3) & (s >= z + 1), (z >= 1) & (s >= z)
                down_sends, down_gets = (zz < 3) & (s >= zz + 1), (zz >= 1) & (s >= zz)
                up_src = base + jnp.clip(4 - s + z, 0, 3) * q
                down_src = base + jnp.clip(s + z - 4, 0, 3) * q
                up_add = base + jnp.clip(3 - s + z, 0, 3) * q
                down_add = base + jnp.clip(s - 3 + z, 0, 3) * q
                up = self.copy(lambda v=up_src: self.rows(v, q), lambda v=up_at: self.rb.at[pl.ds(v, q), :], w.peer("up"))
                down = self.copy(lambda v=down_src: self.rows(v, q), lambda v=down_at: self.rb.at[pl.ds(v, q), :], w.peer("down"))
                steps.append(line_step(up, down, up_sends, up_gets, down_sends, down_gets,
                                       lambda a=up_add, r=up_at: add_rows(self.acc, a, self.rb, r, q),
                                       lambda a=down_add, r=down_at: add_rows(self.acc, a, self.rb, r, q)))
            return base + z * q, q

        def line_gather(base, q):
            z = w.z
            for s in (1, 2, 3):
                up_sends, up_gets = (z < 3) & (z - (s - 1) >= 0), z - s >= 0
                down_sends, down_gets = (z > 0) & (z + (s - 1) <= 3), z + s <= 3
                up_src = base + jnp.clip(z - s + 1, 0, 3) * q
                down_src = base + jnp.clip(z + s - 1, 0, 3) * q
                up = self.copy(lambda v=up_src: done(v, q), lambda v=up_src: done(v, q), w.peer("up"))
                down = self.copy(lambda v=down_src: done(v, q), lambda v=down_src: done(v, q), w.peer("down"))
                steps.append(line_step(up, down, up_sends, up_gets, down_sends, down_gets, None, None))

        def line_step(up, down, up_sends, up_gets, down_sends, down_gets, up_then, down_then):
            def begin():
                @pl.when(up_sends)
                def _():
                    up().start()

                @pl.when(down_sends)
                def _():
                    down().start()

            def finish():
                for cp, gets, then in ((up, up_gets, up_then), (down, down_gets, down_then)):
                    @pl.when(gets)
                    def _(cp=cp, then=then):
                        cp().wait_recv()
                        if then is not None:
                            then()

                for cp, sends in ((up, up_sends), (down, down_sends)):
                    @pl.when(sends)
                    def _(cp=cp):
                        cp().wait_send()

            return begin, finish

        def then_keep(base, n):
            begin, finish = steps.pop()

            def finish_and_keep():
                finish()
                keep(base, n)

            steps.append((begin, finish_and_keep))

        def widen(base, n):
            for bit in range(4, 4 + w.extra_bits):
                at = self.space(n)
                exchange(
                    lambda: self.rows(base, n),
                    lambda at=at: self.rb.at[pl.ds(at, n), :],
                    w.peer(bit),
                    lambda at=at: add_rows(self.acc, base, self.rb, at, n),
                )

        exchange(
            lambda: self.rows(away, ROWS),
            lambda: self.rb.at[pl.ds(at0, ROWS), :],
            w.peer("core"),
            lambda: add_rows(self.acc, home, self.rb, at0, ROWS),
        )
        if kind in "AB":
            d1, d2 = ("x", "y") if kind == "A" else ("y", "x")
            b1, n1 = reduce(d1, home, ROWS)
            b2, n2 = reduce(d2, b1, n1)
            b3, n3 = line_reduce(b2, n2)
            widen(b3, n3)
            then_keep(b3, n3)
            line_gather(b2, n3)
            gather(d2, b2, n2)
            gather(d1, b1, n1)
        else:
            d1, d2 = ("x", "y") if kind == "C" else ("y", "x")
            b1, n1 = line_reduce(home, ROWS)
            b2, n2 = reduce(d1, b1, n1)
            b3, n3 = reduce(d2, b2, n2)
            widen(b3, n3)
            then_keep(b3, n3)
            gather(d2, b3, n3)
            gather(d1, b2, n2)
            line_gather(home, n1)
        k = self.sem_at
        self.sem_at += 1

        def last(block):
            return pltpu.make_async_remote_copy(
                src_ref=self.rb.at[pl.ds(at0, ROWS), :], dst_ref=block, send_sem=self.ssem.at[k], recv_sem=self.rsem.at[k],
                device_id=w.peer("core"), device_id_type=MESH)

        final = by_core(w.core, lambda half: last(self.block(half, t)), t)
        steps.append((lambda: final.start(), lambda: final.wait()))
        self.homes.append(at0)
        return steps

    def op(self, t, p):
        steps = self.steps[t]
        if p > 0:
            steps[p - 1][1]()
        if p < len(steps):
            steps[p][0]()


KINDS = "ABCABDABCABDABCABD"
ORDER = (
    1, 4, 0, 3, 2, -1, 5, -1, 1, 0, 3, 2, 5, -1, 4, -1, -1, 2, 7, -1, 0, 6, 1, 8, 5, -1, 7, 6, 2, -1, 3, 8, 4, -1, 0, 1,
    -1, 5, 2, -1, 0, 9, 6, 11, 10, 7, 1, 8, -1, 4, 9, 0, 2, 5, 3, 11, 1, -1, 10, -1, 5, 0, 6, 4, 3, -1, 8, 5, 9, 6, 0, 7,
    4, 2, 1, -1, 10, 2, 5, 3, 8, 6, 0, 4, 1, 11, -1, 10, 7, 1, 5, 0, 9, 2, 6, 8, -1, -1, 1, 9, 10, 12, 13, 8, 7, 14, 11, 0,
    3, 4, -1, 1, 8, 2, 15, 5, 17, 13, 7, 14, 9, 6, 3, 16, 11, 12, 17, 10, 8, 15, 2, 16, -1, 14, 17, 3, 13, 4, 1, 6, 5, 0, 12, 7,
    2, 9, 10, 11, 3, 4, 15, 16, 14, 13, 6, 8, 0, 17, 5, 11, 12, 7, 4, 3, 13, 9, 1, 14, 12, 10, 16, 15, 8, 16, 11, 6, 17, 5, 15, 13,
    12, 3, 9, 7, 10, 16, 15, 13, 14, 11, 17, 2, 9, 12, 10, 16, 13, 14, 8, 15, 4, 6, 7, 3, 17, 12, 9, 11, 14, 16, 8, 13, 17, 4, 10, 12,
    12, 15, 13, 11, 15, 16, 7, 9, 14, 17, 11, 16, 6, 15, 9, 10, 14, 13, 12, 17, 16, 15, 10, 14, 14, 17, 13, 12, 17, 15, 16, 13, 11, 12, 14, 17,
    7, 15, 16,
)
SMALL = 16


def block_of(refs, half, t):
    if t < 6:
        return refs[0].at[pl.ds(pl.multiple_of(half * 1536 + t * ROWS, ROWS), ROWS), :]
    if t < 12:
        i, j = (t - 6) % 3, (t - 6) // 3
        return refs[1].at[pl.ds(i * ROWS, ROWS), pl.ds(pl.multiple_of((half * 2 + j) * LANES, LANES), LANES)]
    return refs[2 + 2 * half + (t - 12) // 3].at[pl.ds((t - 12) % 3 * ROWS, ROWS), :]


class Branches:
    def __init__(self, core, make):
        self.core, self.make = core, make

    def start(self):
        for core in range(2):
            @pl.when(self.core == core)
            def _(core=core):
                self.make(core).start()

    def wait(self):
        self.make(0).wait()


class Plain:
    def __init__(self, make):
        self.make = make

    def start(self):
        self.make().start()

    def wait(self):
        self.make().wait()


def by_core(core, make, t):
    return Plain(lambda: make(core)) if t < 12 else Branches(core, make)


def tn(a, b):
    return lax.dot_general(a, b, (((0,), (0,)), ((), ())), preferred_element_type=jnp.float32)


FULL = ("q", "k", "v", "ctx", "x", "mid", "dffn", "dmid", "normed", "wq", "wk", "wv", "wo")


def back_kernel(extra_bits, *refs):
    g_outer, w_outer, w_inner, slope, *refs = refs
    full_in, refs = dict(zip(FULL, refs)), refs[len(FULL):]
    factor, gain, lse, bias_ref, sum_outer, sum_gain, sum_shift, *refs = refs
    outs, small_out, grad_out, refs = refs[:6], refs[6], refs[7], refs[8:]
    v, refs = dict(zip(FULL, refs)), refs[len(FULL):]
    wou, win, gp, dp, dc, db, dq, dk, dv, ig, part, rb, small, small_rb, ssem, rsem, lsem, vsem, fsem, tsem, osem, isem = refs
    w = Wire(extra_bits)
    count = len(KINDS)
    f32 = jnp.float32
    rows = dp.shape[0]
    length = bias_ref.shape[0] // lse.shape[0]
    order = (0, 2, 1, 3)

    def load(half, t):
        to = part.at[pl.ds((half * count + t) * ROWS, ROWS), :]
        return pltpu.make_async_copy(g_outer.at[pl.ds(half * 1536 + t * ROWS, ROWS), :], to, lsem.at[half, t])

    def fetch(name):
        return pltpu.make_async_copy(full_in[name], v[name], fsem.at[FULL.index(name)])

    def tile(which, n):
        at, slot = order[n] * LANES, n % 2
        source, to = (
            (w_outer.at[pl.ds(at, LANES), :], wou),
            (w_inner.at[:, pl.ds(at, LANES)], win),
            (slope.at[:, pl.ds(at, LANES)], gp),
        )[which]
        return pltpu.make_async_copy(source, to.at[slot], tsem.at[which, n])

    for t in range(6):
        load(0, t).start()
        load(1, t).start()
        if t == 0:
            fetch("dffn").start()
            tile(0, 0).start()
            tile(2, 0).start()
            fetch("mid").start()
            tile(1, 0).start()
            fetch("dmid").start()
    for which in range(3):
        tile(which, 1).start()
    for name in ("normed", "wo", "ctx", "k", "q", "v", "x", "wq", "wk", "wv"):
        fetch(name).start()
    w.barrier()
    tasks = Tasks(w, KINDS, part, rb, ssem, rsem, lambda half, t: block_of(outs, half, t))

    def store(t):
        def make(half):
            return pltpu.make_async_copy(rb.at[pl.ds(tasks.homes[t], ROWS), :], block_of(outs, half, t), osem.at[t])

        return by_core(w.core, make, t)

    def grad_blocks(left, right, half, t):
        to = pl.ds((half * count + t) * ROWS, left.shape[1])
        part[to, :] = tn(left[...], right[...]).astype(jnp.bfloat16)

    def by_rows(step, body, carry=0):
        def wrapped(r, carry):
            return body(pl.ds(pl.multiple_of(r * step, step), step), carry)

        return lax.fori_loop(0, rows // step, wrapped, carry)

    none = jnp.zeros((1, LANES), f32)

    def d_pre(n):
        tile(0, n).wait()
        tile(2, n).wait()
        if n == 0:
            fetch("dffn").wait()

        def body(at, total):
            d = (nt(v["dffn"][at, :], wou[n % 2]) * gp[n % 2, at, :].astype(f32)).astype(jnp.bfloat16)
            dp[at, :] = d
            return total + jnp.sum(d.astype(f32), axis=0, keepdims=True)

        small[0, 8 + order[n]:9 + order[n], :] = by_rows(256, body, none)
        if n + 2 < 4:
            tile(0, n + 2).start()
            tile(2, n + 2).start()

    def inner_blocks(n):
        if n == 0:
            fetch("mid").wait()
        grad_blocks(v["mid"], dp, order[n] // 2, 6 + 3 * (order[n] % 2))

    def d_mid(n):
        tile(1, n).wait()
        if n == 0:
            fetch("dmid").wait()

        def body(at, carry):
            v["dmid"][at, :] += nt(dp[at, :], win[n % 2])
            return carry

        by_rows(256, body)
        if n + 2 < 4:
            tile(1, n + 2).start()

    def norm_step():
        fetch("normed").wait()

        def body(at, sums):
            d, normed = v["dmid"][at, :], v["normed"][at, :]
            e = d * gain[...]
            res = factor[at, :] * (
                e - jnp.mean(e, axis=-1, keepdims=True) - normed * jnp.mean(e * normed, axis=-1, keepdims=True)
            )
            low = res.astype(jnp.bfloat16)
            v["dmid"][at, :] = res
            db[at, :] = low
            return (
                sums[0] + jnp.sum(low.astype(f32), axis=0, keepdims=True),
                sums[1] + jnp.sum(d * normed, axis=0, keepdims=True),
                sums[2] + jnp.sum(d, axis=0, keepdims=True),
            )

        sums = by_rows(128, body, (none, none, none))
        for i in range(3):
            small[0, 2 + i:3 + i, :] = sums[i]

    def d_context():
        fetch("wo").wait()

        dc[...] = nt(db[...], v["wo"][...]).astype(jnp.bfloat16)

    def out_blocks():
        fetch("ctx").wait()
        grad_blocks(v["ctx"], db, 1, 15)

    def attention(seq, count):
        if seq == 0:
            for name in ("q", "k", "v"):
                fetch(name).wait()
        at = pl.ds(seq * length, length)
        bias = jnp.concatenate([bias_ref[at, :]] * (length // 128), axis=1)

        def body(step, carry):
            first = step * count
            columns = [pl.ds(pl.multiple_of((first + i) * 128, 128), 128) for i in range(count)]
            found = attend_back(
                [(v["q"][at, c], v["k"][at, c], v["v"][at, c], dc[at, c], lse[seq, first + i]) for i, c in enumerate(columns)],
                bias)
            for c, (d_query, d_key, d_value) in zip(columns, found):
                dq[at, c], dk[at, c], dv[at, c] = d_query, d_key, d_value
            return carry

        lax.fori_loop(0, lse.shape[1] // count, body, 0)

    def total_rows(ref, row):
        def body(at, total):
            return total + jnp.sum(ref[at, :].astype(f32), axis=0, keepdims=True)

        small[0, row:row + 1, :] = by_rows(128, body, none)

    def value_blocks():
        grad_blocks(v["x"], dv, 1, 12)
        total_rows(dv, 1)

    def query_blocks():
        fetch("x").wait()
        grad_blocks(v["x"], dq, 0, 12)
        total_rows(dq, 0)

    def key_blocks():
        grad_blocks(v["x"], dk, 0, 15)

    def grad_copy(seq, away):
        source = ig.at[2 * seq + (1 - w.m if away else w.m)]
        to = grad_out.at[w.m * lse.shape[0] + seq]
        if not away:
            return pltpu.make_async_copy(source, to, isem.at[2, seq])
        return pltpu.make_async_remote_copy(
            src_ref=source, dst_ref=to, send_sem=isem.at[0, seq], recv_sem=isem.at[1, seq],
            device_id=w.peer("x"), device_id_type=MESH)

    def input_rows():
        for name in ("wq", "wk", "wv"):
            fetch(name).wait()

        def body(seq, carry):
            at = pl.ds(pl.multiple_of(seq * length, length), length)
            total = v["dmid"][at, :] + nt(dq[at, :], v["wq"][...])
            total = total + nt(dk[at, :], v["wk"][...]) + nt(dv[at, :], v["wv"][...])
            for i in range(length // 128):
                ig[2 * seq + i] = total[i * 128:i * 128 + 128].astype(jnp.bfloat16)
            return carry

        lax.fori_loop(0, lse.shape[0], body, 0)
        for seq in range(lse.shape[0]):
            grad_copy(seq, True).start()
            grad_copy(seq, False).start()

    small[0, 12:16, :] = jnp.zeros((4, LANES), f32)
    for row, ref in ((5, sum_outer), (6, sum_gain), (7, sum_shift)):
        small[0, row:row + 1, :] = ref[...]
    hops = ["core", "x", "y"] + list(range(2, 4 + extra_bits))

    def small_copy(k):
        return pltpu.make_async_remote_copy(
            src_ref=small.at[k], dst_ref=small_rb.at[k], send_sem=vsem.at[0, k], recv_sem=vsem.at[1, k],
            device_id=w.peer(hops[k]), device_id_type=MESH)

    def small_op(k):
        if k > 0:
            small_copy(k - 1).wait()
            small[k] = small[k - 1] + small_rb[k - 1]
        if k < len(hops):
            small_copy(k).start()

    seqs = lse.shape[0]
    work = [job for n in range(4) for job in ((d_pre, n), (inner_blocks, n), (d_mid, n))]
    work += [(norm_step,), (d_context,), (out_blocks,)] + [(attention, seq, 3) for seq in range(seqs)]
    work += [(query_blocks,), (value_blocks,), (key_blocks,), (input_rows,)]

    def comm(t, p):
        if t == count:
            small_op(p)
            return
        if p == 0 and t < 6:
            load(0, t).wait()
            load(1, t).wait()
        tasks.op(t, p)
        if p == len(tasks.steps[t]) - 1:
            store(t).start()

    at, vectors, since = [0] * count, 0, 0
    for t in ORDER:
        if t < 0:
            job = work.pop(0)
            job[0](*job[1:])
            continue
        comm(t, at[t])
        at[t] += 1
        since += 1
        if len(work) < 2 and since >= 6 and vectors <= len(hops):
            comm(count, vectors)
            vectors, since = vectors + 1, 0
    for k in range(vectors, len(hops) + 1):
        comm(count, k)
    for _ in range(extra_bits):
        for t in range(count):
            comm(t, at[t])
            at[t] += 1
    small_out[...] = small[len(hops)]
    for t in range(count):
        store(t).wait()
    for seq in range(seqs):
        grad_copy(seq, False).wait()
        grad_copy(seq, True).wait()


def backward(g_outer, w_outer, w_inner, slope, full, blocks, shape):
    extra_bits = (lax.axis_size("batch") // 16).bit_length() - 1
    space, sems = plan_sizes(KINDS, extra_bits)
    hops = 5 + extra_bits
    count = len(KINDS)
    low, f32 = jnp.bfloat16, jnp.float32
    hbm = pl.BlockSpec(memory_space=pl.ANY)
    vmem = pl.BlockSpec(memory_space=pltpu.VMEM)
    rows, width = full[0].shape
    grads = [g_outer.shape, w_inner.shape] + [(width, width)] * 4
    flat = pltpu.VMEM((rows, width), low)
    return pl.pallas_call(
        functools.partial(back_kernel, extra_bits),
        out_shape=tuple(jax.ShapeDtypeStruct(g, low) for g in grads)
        + (jax.ShapeDtypeStruct((SMALL, LANES), f32), jax.ShapeDtypeStruct(shape, low)),
        in_specs=[hbm] * (4 + len(full)) + [vmem] * len(blocks),
        out_specs=(hbm,) * len(grads) + (vmem, hbm),
        scratch_shapes=[pltpu.VMEM(m.shape, m.dtype) for m in full]
        + [
            pltpu.VMEM((2, LANES, LANES), low),
            pltpu.VMEM((2, LANES, LANES), low),
            pltpu.VMEM((2, rows, LANES), low),
            flat, flat, flat, flat, flat, flat,
            pltpu.VMEM((rows // 128, 128, width), low),
            pltpu.VMEM((2 * count * ROWS, LANES), low),
            pltpu.VMEM((space, LANES), low),
            pltpu.VMEM((hops + 1, SMALL, LANES), f32),
            pltpu.VMEM((hops, SMALL, LANES), f32),
            pltpu.SemaphoreType.DMA((sems,)),
            pltpu.SemaphoreType.DMA((sems,)),
            pltpu.SemaphoreType.DMA((2, 6)),
            pltpu.SemaphoreType.DMA((2, hops)),
            pltpu.SemaphoreType.DMA((len(full),)),
            pltpu.SemaphoreType.DMA((3, 4)),
            pltpu.SemaphoreType.DMA((count,)),
            pltpu.SemaphoreType.DMA((3, shape[0] // 2)),
        ],
        compiler_params=pltpu.CompilerParams(collective_id=1, has_side_effects=True, vmem_limit_bytes=62 << 20),
    )(g_outer, w_outer, w_inner, slope, *full, *blocks)


def nt(a, b):
    return lax.dot_general(a, b, (((1,), (1,)), ((), ())), preferred_element_type=jnp.float32)


def nn(a, b):
    return lax.dot_general(a, b, (((1,), (0,)), ((), ())), preferred_element_type=jnp.float32)


def low_lanes(rows):
    return lax.broadcasted_iota(jnp.int32, (rows, 128), 1) < 64


def heads_of(pairs):
    return [(i, head) for i in range(len(pairs)) for head in range(2)]


def own_lanes(block, head):
    low = low_lanes(block.shape[0])
    return jnp.where(low if head == 0 else ~low, block, jnp.zeros_like(block))


def attend(pairs, bias):
    heads = heads_of(pairs)
    scores = [nt(own_lanes(pairs[i][1], head), pairs[i][0]) + bias for i, head in heads]
    tops = [jnp.max(s, axis=0, keepdims=True) for s in scores]
    expo = [jnp.exp(s - top) for s, top in zip(scores, tops)]
    totals = [jnp.sum(e, axis=0, keepdims=True) for e in expo]
    vt = [pair[2].T for pair in pairs]
    context = [
        nn(vt[i][head * 64:head * 64 + 64], e.astype(jnp.bfloat16)) * (1.0 / total)
        for e, total, (i, head) in zip(expo, totals, heads)
    ]
    logs = [top + jnp.log(total) for top, total in zip(tops, totals)]
    return [
        (jnp.concatenate(context[2 * i:2 * i + 2], axis=0).T.astype(jnp.bfloat16), jnp.concatenate(logs[2 * i:2 * i + 2], axis=0))
        for i in range(len(pairs))
    ]


def attend_back(pairs, bias):
    heads = heads_of(pairs)
    kt = [pair[1].T for pair in pairs]
    scores = [nt(own_lanes(pairs[i][1], head), pairs[i][0]) for i, head in heads]
    d_probs = [nt(own_lanes(pairs[i][2], head), pairs[i][3]) for i, head in heads]
    probs = [jnp.exp(s + (bias - pairs[i][4][head:head + 1])) for s, (i, head) in zip(scores, heads)]
    inner = [jnp.sum(p * d, axis=0, keepdims=True) for p, d in zip(probs, d_probs)]
    d_scores = [(p * (d - one)).astype(jnp.bfloat16) for p, d, one in zip(probs, d_probs, inner)]
    probs_low = [p.astype(jnp.bfloat16) for p in probs]
    dq = [nn(kt[i][head * 64:head * 64 + 64], d) for d, (i, head) in zip(d_scores, heads)]
    dk = [nn(d, pairs[i][0]) for d, (i, head) in zip(d_scores, heads)]
    dv = [nn(p, pairs[i][3]) for p, (i, head) in zip(probs_low, heads)]
    low = low_lanes(pairs[0][0].shape[0])
    return [
        (
            (jnp.concatenate(dq[2 * i:2 * i + 2], axis=0) * 0.125).T.astype(jnp.bfloat16),
            jnp.where(low, dk[2 * i], dk[2 * i + 1]).astype(jnp.bfloat16),
            jnp.where(low, dv[2 * i], dv[2 * i + 1]).astype(jnp.bfloat16),
        )
        for i in range(len(pairs))
    ]


def forward_kernel(q_ref, k_ref, v_ref, bias_ref, ctx_ref, lse_ref):
    length, width = q_ref.shape
    bias = jnp.concatenate([bias_ref[...]] * (length // 128), axis=1)

    def body(step, carry):
        columns = [pl.ds(pl.multiple_of((step * 3 + i) * 128, 128), 128) for i in range(3)]
        found = attend([(q_ref[:, c], k_ref[:, c], v_ref[:, c]) for c in columns], bias)
        for i, (context, logs) in enumerate(found):
            ctx_ref[:, columns[i]] = context
            lse_ref[0, step * 3 + i] = logs
        return carry

    lax.fori_loop(0, width // 384, body, 0)


def attention_forward(q, k, v, bias, length):
    rows, width = q.shape
    seqs, pairs = rows // length, width // 128
    block = pl.BlockSpec((length, width), lambda s: (s, 0))
    return pl.pallas_call(
        forward_kernel,
        grid=(seqs,),
        out_shape=(jax.ShapeDtypeStruct(q.shape, jnp.bfloat16), jax.ShapeDtypeStruct((seqs, pairs, 2, length), jnp.float32)),
        in_specs=[block, block, block, pl.BlockSpec((length, 128), lambda s: (s, 0))],
        out_specs=(block, pl.BlockSpec((1, pairs, 2, length), lambda s: (s, 0, 0, 0))),
    )(q, k, v, bias)


def widen_kernel(*refs):
    for source, to in zip(refs[:len(refs) // 2], refs[len(refs) // 2:]):
        to[...] = source[...].astype(jnp.float32)


def to_float32(arrays):
    steps = 12
    blocks = [pl.BlockSpec((a.shape[0] // steps, a.shape[1]), lambda i: (i, 0)) for a in arrays]
    return pl.pallas_call(
        widen_kernel,
        grid=(steps,),
        out_shape=tuple(jax.ShapeDtypeStruct(a.shape, jnp.float32) for a in arrays),
        in_specs=blocks,
        out_specs=tuple(blocks),
    )(*arrays)


epsilon = 1e-05


def to_partner(block):
    return lax.ppermute(block, "mod", [(0, 1), (1, 0)])


def take_side(array, axis, side):
    half = array.shape[axis] // 2
    return lax.dynamic_slice_in_dim(array, side * half, half, axis)


def gather_sequences(array, side, away):
    own = take_side(array, 0, side)
    other = to_partner(away)
    both = jnp.where(side == 0, jnp.concatenate((own, other), axis=1), jnp.concatenate((other, own), axis=1))
    return both.reshape(-1, array.shape[2])


def return_rows(array, side):
    own = take_side(array, 1, side)
    other = to_partner(take_side(array, 1, 1 - side))
    return jnp.where(side == 0, jnp.concatenate((own, other)), jnp.concatenate((other, own)))


def linear(rows, weight_matrix):
    return lax.dot_general(rows, weight_matrix, (((1,), (0,)), ((), ())), preferred_element_type=jnp.float32)


def back_linear(gradient_rows, weight_matrix):
    return lax.dot_general(gradient_rows, weight_matrix, (((1,), (1,)), ((), ())), preferred_element_type=jnp.float32)


def weight_grad(layer_inputs, gradient_rows):
    return lax.dot_general(
        layer_inputs, gradient_rows, (((0,), (0,)), ((), ())), preferred_element_type=jnp.float32
    ).astype(jnp.bfloat16)


def row_total(values):
    return jnp.sum(values.astype(jnp.float32), axis=0, keepdims=True)


def layer_norm(rows):
    centre = rows - jnp.mean(rows, axis=-1, keepdims=True)
    factor = lax.rsqrt(jnp.mean(centre * centre, axis=-1, keepdims=True) + epsilon)
    return (centre * factor, factor)


def norm_back(gradient_rows, normed, factor):
    return factor * (
        gradient_rows
        - jnp.mean(gradient_rows, axis=-1, keepdims=True)
        - normed * jnp.mean(gradient_rows * normed, axis=-1, keepdims=True)
    )


def on_device(
    hidden_in,
    text_mask,
    region_count,
    w_query,
    b_query,
    w_key,
    w_value,
    b_value,
    w_attn_out,
    b_attn_out,
    gain_attn,
    shift_attn,
    w_inner,
    b_inner,
    w_outer,
    b_outer,
    gain_ffn,
    shift_ffn,
    cotangent,
):
    seq_count, half_len, width = hidden_in.shape
    length = 2 * half_len
    side = lax.axis_index("mod")
    f32 = jnp.float32
    rows_b = gather_sequences(hidden_in, side, take_side(hidden_in, 0, 1 - side))
    rows_b, away = lax.optimization_barrier((rows_b, take_side(cotangent, 0, 1 - side)))
    upstream = gather_sequences(cotangent, side, away).astype(f32)
    mask = take_side(text_mask, 0, side) == 1
    regions = take_side(region_count, 0, side)
    slot_ok = lax.broadcasted_iota(jnp.int32, mask.shape, 1) < regions[:, None]
    bias = jnp.where(jnp.concatenate((mask, slot_ok), axis=1), f32(0.0), f32(-1000000000.0)).reshape(-1, 1)
    bias = jnp.broadcast_to(bias, (bias.shape[0], 128))

    query_b = ((linear(rows_b, w_query) + b_query.astype(f32)).astype(jnp.bfloat16) * jnp.bfloat16(0.125))
    key_b = linear(rows_b, w_key).astype(jnp.bfloat16)
    value_b = (linear(rows_b, w_value) + b_value.astype(f32)).astype(jnp.bfloat16)
    context_b, lse = attention_forward(query_b, key_b, value_b, bias, length)
    branch = linear(context_b, w_attn_out) + b_attn_out.astype(f32)
    normed_one, factor_one = layer_norm(rows_b.astype(f32) + branch)
    middle = normed_one * gain_attn.astype(f32) + shift_attn.astype(f32)
    middle_b = middle.astype(jnp.bfloat16)
    pre_act = linear(middle_b, w_inner) + b_inner.astype(f32)
    below = 0.5 * (1.0 + lax.erf(pre_act * f32(0.7071067811865476)))
    slope_b = (below + pre_act * (jnp.exp(-0.5 * pre_act * pre_act) * f32(0.3989422804014327))).astype(jnp.bfloat16)
    activ_b = (pre_act * below).astype(jnp.bfloat16)
    ffn_out = linear(activ_b, w_outer) + b_outer.astype(f32)
    normed_two, factor_two = layer_norm(middle + ffn_out)
    layer_out = (normed_two * gain_ffn.astype(f32) + shift_ffn.astype(f32)).astype(jnp.bfloat16)
    layer_out = return_rows(layer_out.reshape(seq_count // 2, length, width), side)
    grad_gain_ffn = row_total(upstream * normed_two)
    grad_shift_ffn = row_total(upstream)
    d_res_two = norm_back(upstream * gain_ffn.astype(f32), normed_two, factor_two)
    d_ffn_b = d_res_two.astype(jnp.bfloat16)
    grad_b_outer = row_total(d_ffn_b)
    grad_w_outer = weight_grad(activ_b, d_ffn_b)
    s_outer, s_inner, s_query, s_key, s_value, s_attn_out, small, input_grad = backward(
        grad_w_outer, w_outer, w_inner, slope_b,
        (
            query_b, key_b, value_b, context_b, rows_b, middle_b, d_ffn_b, d_res_two, normed_one,
            w_query, w_key, w_value, w_attn_out,
        ),
        (factor_one, gain_attn.astype(f32).reshape(1, -1), lse, bias, grad_b_outer, grad_gain_ffn, grad_shift_ffn),
        hidden_in.shape,
    )
    s_outer, s_inner, s_query, s_key, s_value, s_attn_out = to_float32(
        (s_outer, s_inner, s_query, s_key, s_value, s_attn_out)
    )
    return (
        layer_out,
        input_grad,
        s_query,
        small[0],
        s_key,
        s_value,
        small[1],
        s_attn_out,
        small[2],
        small[3],
        small[4],
        s_inner,
        small[8:12].reshape(-1),
        s_outer,
        small[5],
        small[6],
        small[7],
    )


def solution(mesh):
    in_specs = (
        P("batch", "mod", None),
        P("batch", None),
        P("batch"),
        P(),
        P(),
        P(),
        P(),
        P(),
        P(),
        P(),
        P(),
        P(),
        P(),
        P(),
        P(),
        P(),
        P(),
        P(),
        P("batch", "mod", None),
    )
    out_specs = (
        P("batch", "mod", None),
        P("batch", "mod", None),
        P(),
        P(),
        P(),
        P(),
        P(),
        P(),
        P(),
        P(),
        P(),
        P(),
        P(),
        P(),
        P(),
        P(),
        P(),
    )
    return jax.shard_map(
        on_device, mesh=mesh, in_specs=in_specs, out_specs=out_specs, check_vma=False
    )
```

```python
import functools

import jax
import jax.numpy as jnp
from jax import lax
from jax.experimental import pallas as pl
from jax.experimental.pallas import tpu as pltpu
from jax.sharding import PartitionSpec as P

MESH = pl.DeviceIdType.MESH
ROWS = 256
LANES = 768


class Wire:
    def __init__(self, extra_bits):
        self.b = lax.axis_index("batch")
        self.m = lax.axis_index("mod")
        self.core = lax.rem(self.b, 2)
        self.y = lax.rem(self.b // 2, 2)
        self.z = lax.rem(self.b // 4, 4)
        self.extra_bits = extra_bits

    def flip(self, bit):
        own = lax.rem(self.b // (1 << bit), 2)
        return (self.b + (1 - 2 * own) * (1 << bit), self.m)

    def peer(self, dim):
        if dim == "x":
            return (self.b, 1 - self.m)
        if dim == "y":
            return self.flip(1)
        if dim == "core":
            return self.flip(0)
        if dim == "up":
            return (self.b + 4, self.m)
        if dim == "down":
            return (self.b - 4, self.m)
        return self.flip(dim)

    def coord(self, dim):
        return self.m if dim == "x" else self.y

    def barrier(self):
        bar = pltpu.get_barrier_semaphore()
        peers = [self.peer(d) for d in ("core", "x", "y")]
        peers += [self.flip(bit) for bit in range(2, 4 + self.extra_bits)]
        for who in peers:
            pl.semaphore_signal(bar, inc=1, device_id=who, device_id_type=MESH)
        mid_low, mid_high = self.z == 1, self.z == 2

        @pl.when(mid_low)
        def _():
            pl.semaphore_signal(bar, inc=1, device_id=self.peer("up"), device_id_type=MESH)

        @pl.when(mid_high)
        def _():
            pl.semaphore_signal(bar, inc=1, device_id=self.peer("down"), device_id_type=MESH)

        pl.semaphore_wait(bar, len(peers) + jnp.where(mid_low | mid_high, 1, 0))


def plan_sizes(kinds, extra_bits):
    rows = sems = 0
    for kind in kinds:
        n = ROWS
        rows += ROWS
        sems += 1
        order = "xyz" if kind == "A" else "yxz" if kind == "B" else "zxy" if kind == "C" else "zyx"
        for dim in order:
            if dim == "z":
                rows += 6 * (n // 4)
                n //= 4
            else:
                rows += n // 2
                n //= 2
        rows += extra_bits * n
        sems += 6 + 6 + 4 + extra_bits + 1
    return rows, sems


def add_rows(acc, at, rb, rb_at, n):
    step = 64 if n > 64 else min(n, 32)

    def body(i, carry):
        d = pl.multiple_of(at + i * step, 16)
        s = pl.multiple_of(rb_at + i * step, 16)
        total = acc[pl.ds(d, step), :].astype(jnp.float32) + rb[pl.ds(s, step), :].astype(jnp.float32)
        acc[pl.ds(d, step), :] = total.astype(jnp.bfloat16)
        return carry

    if n == step:
        body(0, 0)
    else:
        lax.fori_loop(0, n // step, body, 0)


class Tasks:
    def __init__(self, wire, kinds, part, rb, ssem, rsem, block):
        self.w, self.acc, self.rb, self.block = wire, part, rb, block
        self.ssem, self.rsem = ssem, rsem
        self.rb_at = 0
        self.sem_at = 0
        self.homes = []
        self.steps = [self.build(t, kind) for t, kind in enumerate(kinds)]

    def space(self, n):
        at = self.rb_at
        self.rb_at += n
        return at

    def copy(self, src, dst, who):
        k = self.sem_at
        self.sem_at += 1
        return lambda: pltpu.make_async_remote_copy(
            src_ref=src(), dst_ref=dst(), send_sem=self.ssem.at[k], recv_sem=self.rsem.at[k], device_id=who, device_id_type=MESH
        )

    def rows(self, at, n):
        return self.acc.at[pl.ds(pl.multiple_of(at, 16), n), :]

    def build(self, t, kind):
        w = self.w
        steps = []
        home = (w.core * len(KINDS) + t) * ROWS
        away = ((1 - w.core) * len(KINDS) + t) * ROWS
        at0 = self.space(ROWS)

        def done(at, n):
            return self.rb.at[pl.ds(pl.multiple_of(at + (at0 - home), 16), n), :]

        def keep(at, n):
            self.rb[pl.ds(pl.multiple_of(at + (at0 - home), 16), n), :] = self.acc[pl.ds(pl.multiple_of(at, 16), n), :]

        def exchange(src, dst, who, then):
            cp = self.copy(src, dst, who)

            def begin():
                cp().start()

            def finish():
                cp().wait()
                then()

            steps.append((begin, finish))

        def reduce(dim, base, n):
            half, a = n // 2, w.coord(dim)
            at = self.space(half)
            kept = base + a * half
            sent = base + (1 - a) * half
            exchange(
                lambda: self.rows(sent, half),
                lambda: self.rb.at[pl.ds(at, half), :],
                w.peer(dim),
                lambda: add_rows(self.acc, kept, self.rb, at, half),
            )
            return kept, half

        def gather(dim, base, n):
            exchange(lambda: done(base, n), lambda: done(base, n), w.peer(dim), lambda: None)

        def line_reduce(base, n):
            q, z, zz = n // 4, w.z, 3 - w.z
            for s in (1, 2, 3):
                up_at, down_at = self.space(q), self.space(q)
                up_sends, up_gets = (z < 3) & (s >= z + 1), (z >= 1) & (s >= z)
                down_sends, down_gets = (zz < 3) & (s >= zz + 1), (zz >= 1) & (s >= zz)
                up_src = base + jnp.clip(4 - s + z, 0, 3) * q
                down_src = base + jnp.clip(s + z - 4, 0, 3) * q
                up_add = base + jnp.clip(3 - s + z, 0, 3) * q
                down_add = base + jnp.clip(s - 3 + z, 0, 3) * q
                up = self.copy(lambda v=up_src: self.rows(v, q), lambda v=up_at: self.rb.at[pl.ds(v, q), :], w.peer("up"))
                down = self.copy(lambda v=down_src: self.rows(v, q), lambda v=down_at: self.rb.at[pl.ds(v, q), :], w.peer("down"))
                steps.append(line_step(up, down, up_sends, up_gets, down_sends, down_gets,
                                       lambda a=up_add, r=up_at: add_rows(self.acc, a, self.rb, r, q),
                                       lambda a=down_add, r=down_at: add_rows(self.acc, a, self.rb, r, q)))
            return base + z * q, q

        def line_gather(base, q):
            z = w.z
            for s in (1, 2, 3):
                up_sends, up_gets = (z < 3) & (z - (s - 1) >= 0), z - s >= 0
                down_sends, down_gets = (z > 0) & (z + (s - 1) <= 3), z + s <= 3
                up_src = base + jnp.clip(z - s + 1, 0, 3) * q
                down_src = base + jnp.clip(z + s - 1, 0, 3) * q
                up = self.copy(lambda v=up_src: done(v, q), lambda v=up_src: done(v, q), w.peer("up"))
                down = self.copy(lambda v=down_src: done(v, q), lambda v=down_src: done(v, q), w.peer("down"))
                steps.append(line_step(up, down, up_sends, up_gets, down_sends, down_gets, None, None))

        def line_step(up, down, up_sends, up_gets, down_sends, down_gets, up_then, down_then):
            def begin():
                @pl.when(up_sends)
                def _():
                    up().start()

                @pl.when(down_sends)
                def _():
                    down().start()

            def finish():
                for cp, gets, then in ((up, up_gets, up_then), (down, down_gets, down_then)):
                    @pl.when(gets)
                    def _(cp=cp, then=then):
                        cp().wait_recv()
                        if then is not None:
                            then()

                for cp, sends in ((up, up_sends), (down, down_sends)):
                    @pl.when(sends)
                    def _(cp=cp):
                        cp().wait_send()

            return begin, finish

        def then_keep(base, n):
            begin, finish = steps.pop()

            def finish_and_keep():
                finish()
                keep(base, n)

            steps.append((begin, finish_and_keep))

        def widen(base, n):
            for bit in range(4, 4 + w.extra_bits):
                at = self.space(n)
                exchange(
                    lambda: self.rows(base, n),
                    lambda at=at: self.rb.at[pl.ds(at, n), :],
                    w.peer(bit),
                    lambda at=at: add_rows(self.acc, base, self.rb, at, n),
                )

        exchange(
            lambda: self.rows(away, ROWS),
            lambda: self.rb.at[pl.ds(at0, ROWS), :],
            w.peer("core"),
            lambda: add_rows(self.acc, home, self.rb, at0, ROWS),
        )
        if kind in "AB":
            d1, d2 = ("x", "y") if kind == "A" else ("y", "x")
            b1, n1 = reduce(d1, home, ROWS)
            b2, n2 = reduce(d2, b1, n1)
            b3, n3 = line_reduce(b2, n2)
            widen(b3, n3)
            then_keep(b3, n3)
            line_gather(b2, n3)
            gather(d2, b2, n2)
            gather(d1, b1, n1)
        else:
            d1, d2 = ("x", "y") if kind == "C" else ("y", "x")
            b1, n1 = line_reduce(home, ROWS)
            b2, n2 = reduce(d1, b1, n1)
            b3, n3 = reduce(d2, b2, n2)
            widen(b3, n3)
            then_keep(b3, n3)
            gather(d2, b3, n3)
            gather(d1, b2, n2)
            line_gather(home, n1)
        k = self.sem_at
        self.sem_at += 1

        def last(block):
            return pltpu.make_async_remote_copy(
                src_ref=self.rb.at[pl.ds(at0, ROWS), :], dst_ref=block, send_sem=self.ssem.at[k], recv_sem=self.rsem.at[k],
                device_id=w.peer("core"), device_id_type=MESH)

        final = by_core(w.core, lambda half: last(self.block(half, t)), t)
        steps.append((lambda: final.start(), lambda: final.wait()))
        self.homes.append(at0)
        return steps

    def op(self, t, p):
        steps = self.steps[t]
        if p > 0:
            steps[p - 1][1]()
        if p < len(steps):
            steps[p][0]()


KINDS = "ABCABDABCABDABCABD"
ORDER = (
    1, 4, 0, 3, 2, -1, 5, -1, 1, 0, 3, 2, 5, -1, 4, -1, -1, 2, 7, -1, 0, 6, 1, 8, 5, -1, 7, 6, 2, -1, 3, 8, 4, -1, 0, 1,
    -1, 5, 2, -1, 0, 9, 6, 11, 10, 7, 1, 8, -1, 4, 9, 0, 2, 5, 3, 11, 1, -1, 10, -1, 5, 0, 6, 4, 3, -1, 8, 5, 9, 6, 0, 7,
    4, 2, 1, -1, 10, 2, 5, 3, 8, 6, 0, 4, 1, 11, -1, 10, 7, 1, 5, 0, 9, 2, 6, 8, -1, -1, 1, 9, 10, 12, 13, 8, 7, 14, 11, 0,
    3, 4, -1, 1, 8, 2, 15, 5, 17, 13, 7, 14, 9, 6, 3, 16, 11, 12, 17, 10, 8, 15, 2, 16, -1, 14, 17, 3, 13, 4, 1, 6, 5, 0, 12, 7,
    2, 9, 10, 11, 3, 4, 15, 16, 14, 13, 6, 8, 0, 17, 5, 11, 12, 7, 4, 3, 13, 9, 1, 14, 12, 10, 16, 15, 8, 16, 11, 6, 17, 5, 15, 13,
    12, 3, 9, 7, 10, 16, 15, 13, 14, 11, 17, 2, 9, 12, 10, 16, 13, 14, 8, 15, 4, 6, 7, 3, 17, 12, 9, 11, 14, 16, 8, 13, 17, 4, 10, 12,
    12, 15, 13, 11, 15, 16, 7, 9, 14, 17, 11, 16, 6, 15, 9, 10, 14, 13, 12, 17, 16, 15, 10, 14, 14, 17, 13, 12, 17, 15, 16, 13, 11, 12, 14, 17,
    7, 15, 16,
)
SMALL = 16


def block_of(refs, half, t):
    if t < 6:
        return refs[0].at[pl.ds(pl.multiple_of(half * 1536 + t * ROWS, ROWS), ROWS), :]
    if t < 12:
        i, j = (t - 6) % 3, (t - 6) // 3
        return refs[1].at[pl.ds(i * ROWS, ROWS), pl.ds(pl.multiple_of((half * 2 + j) * LANES, LANES), LANES)]
    return refs[2 + 2 * half + (t - 12) // 3].at[pl.ds((t - 12) % 3 * ROWS, ROWS), :]


class Branches:
    def __init__(self, core, make):
        self.core, self.make = core, make

    def start(self):
        for core in range(2):
            @pl.when(self.core == core)
            def _(core=core):
                self.make(core).start()

    def wait(self):
        self.make(0).wait()


class Plain:
    def __init__(self, make):
        self.make = make

    def start(self):
        self.make().start()

    def wait(self):
        self.make().wait()


def by_core(core, make, t):
    return Plain(lambda: make(core)) if t < 12 else Branches(core, make)


def tn(a, b):
    return lax.dot_general(a, b, (((0,), (0,)), ((), ())), preferred_element_type=jnp.float32)


FULL = ("q", "k", "v", "ctx", "x", "mid", "dffn", "dmid", "normed", "wq", "wk", "wv", "wo")


def back_kernel(extra_bits, *refs):
    g_outer, w_outer, w_inner, slope, *refs = refs
    full_in, refs = dict(zip(FULL, refs)), refs[len(FULL):]
    factor, gain, lse, bias_ref, sum_outer, sum_gain, sum_shift, *refs = refs
    outs, small_out, grad_out, refs = refs[:6], refs[6], refs[7], refs[8:]
    v, refs = dict(zip(FULL, refs)), refs[len(FULL):]
    wou, win, gp, dp, dc, db, dq, dk, dv, ig, part, rb, small, small_rb, ssem, rsem, lsem, vsem, fsem, tsem, osem, isem = refs
    w = Wire(extra_bits)
    count = len(KINDS)
    f32 = jnp.float32
    rows = dp.shape[0]
    length = bias_ref.shape[0] // lse.shape[0]
    order = (0, 2, 1, 3)

    def load(half, t):
        to = part.at[pl.ds((half * count + t) * ROWS, ROWS), :]
        return pltpu.make_async_copy(g_outer.at[pl.ds(half * 1536 + t * ROWS, ROWS), :], to, lsem.at[half, t])

    def fetch(name):
        return pltpu.make_async_copy(full_in[name], v[name], fsem.at[FULL.index(name)])

    def tile(which, n):
        at, slot = order[n] * LANES, n % 2
        source, to = (
            (w_outer.at[pl.ds(at, LANES), :], wou),
            (w_inner.at[:, pl.ds(at, LANES)], win),
            (slope.at[:, pl.ds(at, LANES)], gp),
        )[which]
        return pltpu.make_async_copy(source, to.at[slot], tsem.at[which, n])

    for t in range(6):
        load(0, t).start()
        load(1, t).start()
        if t == 0:
            fetch("dffn").start()
            tile(0, 0).start()
            tile(2, 0).start()
            fetch("mid").start()
            tile(1, 0).start()
            fetch("dmid").start()
    for which in range(3):
        tile(which, 1).start()
    for name in ("normed", "wo", "ctx", "k", "q", "v", "x", "wq", "wk", "wv"):
        fetch(name).start()
    w.barrier()
    tasks = Tasks(w, KINDS, part, rb, ssem, rsem, lambda half, t: block_of(outs, half, t))

    def store(t):
        def make(half):
            return pltpu.make_async_copy(rb.at[pl.ds(tasks.homes[t], ROWS), :], block_of(outs, half, t), osem.at[t])

        return by_core(w.core, make, t)

    def grad_blocks(left, right, half, t):
        to = pl.ds((half * count + t) * ROWS, left.shape[1])
        part[to, :] = tn(left[...], right[...]).astype(jnp.bfloat16)

    def by_rows(step, body, carry=0):
        def wrapped(r, carry):
            return body(pl.ds(pl.multiple_of(r * step, step), step), carry)

        return lax.fori_loop(0, rows // step, wrapped, carry)

    none = jnp.zeros((1, LANES), f32)

    def d_pre(n):
        tile(0, n).wait()
        tile(2, n).wait()
        if n == 0:
            fetch("dffn").wait()

        def body(at, total):
            d = (nt(v["dffn"][at, :], wou[n % 2]) * gp[n % 2, at, :].astype(f32)).astype(jnp.bfloat16)
            dp[at, :] = d
            return total + jnp.sum(d.astype(f32), axis=0, keepdims=True)

        small[0, 8 + order[n]:9 + order[n], :] = by_rows(256, body, none)
        if n + 2 < 4:
            tile(0, n + 2).start()
            tile(2, n + 2).start()

    def inner_blocks(n):
        if n == 0:
            fetch("mid").wait()
        grad_blocks(v["mid"], dp, order[n] // 2, 6 + 3 * (order[n] % 2))

    def d_mid(n):
        tile(1, n).wait()
        if n == 0:
            fetch("dmid").wait()

        def body(at, carry):
            v["dmid"][at, :] += nt(dp[at, :], win[n % 2])
            return carry

        by_rows(256, body)
        if n + 2 < 4:
            tile(1, n + 2).start()

    def norm_step():
        fetch("normed").wait()

        def body(at, sums):
            d, normed = v["dmid"][at, :], v["normed"][at, :]
            e = d * gain[...]
            res = factor[at, :] * (
                e - jnp.mean(e, axis=-1, keepdims=True) - normed * jnp.mean(e * normed, axis=-1, keepdims=True)
            )
            low = res.astype(jnp.bfloat16)
            v["dmid"][at, :] = res
            db[at, :] = low
            return (
                sums[0] + jnp.sum(low.astype(f32), axis=0, keepdims=True),
                sums[1] + jnp.sum(d * normed, axis=0, keepdims=True),
                sums[2] + jnp.sum(d, axis=0, keepdims=True),
            )

        sums = by_rows(128, body, (none, none, none))
        for i in range(3):
            small[0, 2 + i:3 + i, :] = sums[i]

    def d_context():
        fetch("wo").wait()

        dc[...] = nt(db[...], v["wo"][...]).astype(jnp.bfloat16)

    def out_blocks():
        fetch("ctx").wait()
        grad_blocks(v["ctx"], db, 1, 15)

    def attention(seq, count):
        if seq == 0:
            for name in ("q", "k", "v"):
                fetch(name).wait()
        at = pl.ds(seq * length, length)
        bias = jnp.concatenate([bias_ref[at, :]] * (length // 128), axis=1)

        def body(step, carry):
            first = step * count
            columns = [pl.ds(pl.multiple_of((first + i) * 128, 128), 128) for i in range(count)]
            found = attend_back(
                [(v["q"][at, c], v["k"][at, c], v["v"][at, c], dc[at, c], lse[seq, first + i]) for i, c in enumerate(columns)],
                bias)
            for c, (d_query, d_key, d_value) in zip(columns, found):
                dq[at, c], dk[at, c], dv[at, c] = d_query, d_key, d_value
            return carry

        lax.fori_loop(0, lse.shape[1] // count, body, 0)

    def total_rows(ref, row):
        def body(at, total):
            return total + jnp.sum(ref[at, :].astype(f32), axis=0, keepdims=True)

        small[0, row:row + 1, :] = by_rows(128, body, none)

    def value_blocks():
        grad_blocks(v["x"], dv, 1, 12)
        total_rows(dv, 1)

    def query_blocks():
        fetch("x").wait()
        grad_blocks(v["x"], dq, 0, 12)
        total_rows(dq, 0)

    def key_blocks():
        grad_blocks(v["x"], dk, 0, 15)

    def grad_copy(seq, away):
        source = ig.at[2 * seq + (1 - w.m if away else w.m)]
        to = grad_out.at[w.m * lse.shape[0] + seq]
        if not away:
            return pltpu.make_async_copy(source, to, isem.at[2, seq])
        return pltpu.make_async_remote_copy(
            src_ref=source, dst_ref=to, send_sem=isem.at[0, seq], recv_sem=isem.at[1, seq],
            device_id=w.peer("x"), device_id_type=MESH)

    def input_rows():
        for name in ("wq", "wk", "wv"):
            fetch(name).wait()

        def body(seq, carry):
            at = pl.ds(pl.multiple_of(seq * length, length), length)
            total = v["dmid"][at, :] + nt(dq[at, :], v["wq"][...])
            total = total + nt(dk[at, :], v["wk"][...]) + nt(dv[at, :], v["wv"][...])
            for i in range(length // 128):
                ig[2 * seq + i] = total[i * 128:i * 128 + 128].astype(jnp.bfloat16)
            return carry

        lax.fori_loop(0, lse.shape[0], body, 0)
        for seq in range(lse.shape[0]):
            grad_copy(seq, True).start()
            grad_copy(seq, False).start()

    small[0, 12:16, :] = jnp.zeros((4, LANES), f32)
    for row, ref in ((5, sum_outer), (6, sum_gain), (7, sum_shift)):
        small[0, row:row + 1, :] = ref[...]
    hops = ["core", "x", "y"] + list(range(2, 4 + extra_bits))

    def small_copy(k):
        return pltpu.make_async_remote_copy(
            src_ref=small.at[k], dst_ref=small_rb.at[k], send_sem=vsem.at[0, k], recv_sem=vsem.at[1, k],
            device_id=w.peer(hops[k]), device_id_type=MESH)

    def small_op(k):
        if k > 0:
            small_copy(k - 1).wait()
            small[k] = small[k - 1] + small_rb[k - 1]
        if k < len(hops):
            small_copy(k).start()

    seqs = lse.shape[0]
    work = [job for n in range(4) for job in ((d_pre, n), (inner_blocks, n), (d_mid, n))]
    work += [(norm_step,), (d_context,), (out_blocks,)] + [(attention, seq, 3) for seq in range(seqs)]
    work += [(query_blocks,), (value_blocks,), (key_blocks,), (input_rows,)]

    def comm(t, p):
        if t == count:
            small_op(p)
            return
        if p == 0 and t < 6:
            load(0, t).wait()
            load(1, t).wait()
        tasks.op(t, p)
        if p == len(tasks.steps[t]) - 1:
            store(t).start()

    at, vectors, since = [0] * count, 0, 0
    for t in ORDER:
        if t < 0:
            job = work.pop(0)
            job[0](*job[1:])
            continue
        comm(t, at[t])
        at[t] += 1
        since += 1
        if len(work) < 2 and since >= 6 and vectors <= len(hops):
            comm(count, vectors)
            vectors, since = vectors + 1, 0
    for k in range(vectors, len(hops) + 1):
        comm(count, k)
    for _ in range(extra_bits):
        for t in range(count):
            comm(t, at[t])
            at[t] += 1
    small_out[...] = small[len(hops)]
    for t in range(count):
        store(t).wait()
    for seq in range(seqs):
        grad_copy(seq, False).wait()
        grad_copy(seq, True).wait()


def backward(g_outer, w_outer, w_inner, slope, full, blocks, shape):
    extra_bits = (lax.axis_size("batch") // 16).bit_length() - 1
    space, sems = plan_sizes(KINDS, extra_bits)
    hops = 5 + extra_bits
    count = len(KINDS)
    low, f32 = jnp.bfloat16, jnp.float32
    hbm = pl.BlockSpec(memory_space=pl.ANY)
    vmem = pl.BlockSpec(memory_space=pltpu.VMEM)
    rows, width = full[0].shape
    grads = [g_outer.shape, w_inner.shape] + [(width, width)] * 4
    flat = pltpu.VMEM((rows, width), low)
    return pl.pallas_call(
        functools.partial(back_kernel, extra_bits),
        out_shape=tuple(jax.ShapeDtypeStruct(g, low) for g in grads)
        + (jax.ShapeDtypeStruct((SMALL, LANES), f32), jax.ShapeDtypeStruct(shape, low)),
        in_specs=[hbm] * (4 + len(full)) + [vmem] * len(blocks),
        out_specs=(hbm,) * len(grads) + (vmem, hbm),
        scratch_shapes=[pltpu.VMEM(m.shape, m.dtype) for m in full]
        + [
            pltpu.VMEM((2, LANES, LANES), low),
            pltpu.VMEM((2, LANES, LANES), low),
            pltpu.VMEM((2, rows, LANES), low),
            flat, flat, flat, flat, flat, flat,
            pltpu.VMEM((rows // 128, 128, width), low),
            pltpu.VMEM((2 * count * ROWS, LANES), low),
            pltpu.VMEM((space, LANES), low),
            pltpu.VMEM((hops + 1, SMALL, LANES), f32),
            pltpu.VMEM((hops, SMALL, LANES), f32),
            pltpu.SemaphoreType.DMA((sems,)),
            pltpu.SemaphoreType.DMA((sems,)),
            pltpu.SemaphoreType.DMA((2, 6)),
            pltpu.SemaphoreType.DMA((2, hops)),
            pltpu.SemaphoreType.DMA((len(full),)),
            pltpu.SemaphoreType.DMA((3, 4)),
            pltpu.SemaphoreType.DMA((count,)),
            pltpu.SemaphoreType.DMA((3, shape[0] // 2)),
        ],
        compiler_params=pltpu.CompilerParams(collective_id=1, has_side_effects=True, vmem_limit_bytes=62 << 20),
    )(g_outer, w_outer, w_inner, slope, *full, *blocks)


def nt(a, b):
    return lax.dot_general(a, b, (((1,), (1,)), ((), ())), preferred_element_type=jnp.float32)


def nn(a, b):
    return lax.dot_general(a, b, (((1,), (0,)), ((), ())), preferred_element_type=jnp.float32)


def low_lanes(rows):
    return lax.broadcasted_iota(jnp.int32, (rows, 128), 1) < 64


def heads_of(pairs):
    return [(i, head) for i in range(len(pairs)) for head in range(2)]


def own_lanes(block, head):
    low = low_lanes(block.shape[0])
    return jnp.where(low if head == 0 else ~low, block, jnp.zeros_like(block))


def attend(pairs, bias):
    heads = heads_of(pairs)
    scores = [nt(own_lanes(pairs[i][1], head), pairs[i][0]) + bias for i, head in heads]
    tops = [jnp.max(s, axis=0, keepdims=True) for s in scores]
    expo = [jnp.exp(s - top) for s, top in zip(scores, tops)]
    totals = [jnp.sum(e, axis=0, keepdims=True) for e in expo]
    vt = [pair[2].T for pair in pairs]
    context = [
        nn(vt[i][head * 64:head * 64 + 64], e.astype(jnp.bfloat16)) * (1.0 / total)
        for e, total, (i, head) in zip(expo, totals, heads)
    ]
    logs = [top + jnp.log(total) for top, total in zip(tops, totals)]
    return [
        (jnp.concatenate(context[2 * i:2 * i + 2], axis=0).T.astype(jnp.bfloat16), jnp.concatenate(logs[2 * i:2 * i + 2], axis=0))
        for i in range(len(pairs))
    ]


def attend_back(pairs, bias):
    heads = heads_of(pairs)
    kt = [pair[1].T for pair in pairs]
    scores = [nt(own_lanes(pairs[i][1], head), pairs[i][0]) for i, head in heads]
    d_probs = [nt(own_lanes(pairs[i][2], head), pairs[i][3]) for i, head in heads]
    probs = [jnp.exp(s + (bias - pairs[i][4][head:head + 1])) for s, (i, head) in zip(scores, heads)]
    inner = [jnp.sum(p * d, axis=0, keepdims=True) for p, d in zip(probs, d_probs)]
    d_scores = [(p * (d - one)).astype(jnp.bfloat16) for p, d, one in zip(probs, d_probs, inner)]
    probs_low = [p.astype(jnp.bfloat16) for p in probs]
    dq = [nn(kt[i][head * 64:head * 64 + 64], d) for d, (i, head) in zip(d_scores, heads)]
    dk = [nn(d, pairs[i][0]) for d, (i, head) in zip(d_scores, heads)]
    dv = [nn(p, pairs[i][3]) for p, (i, head) in zip(probs_low, heads)]
    low = low_lanes(pairs[0][0].shape[0])
    return [
        (
            (jnp.concatenate(dq[2 * i:2 * i + 2], axis=0) * 0.125).T.astype(jnp.bfloat16),
            jnp.where(low, dk[2 * i], dk[2 * i + 1]).astype(jnp.bfloat16),
            jnp.where(low, dv[2 * i], dv[2 * i + 1]).astype(jnp.bfloat16),
        )
        for i in range(len(pairs))
    ]


def forward_kernel(q_ref, k_ref, v_ref, bias_ref, ctx_ref, lse_ref):
    length, width = q_ref.shape
    bias = jnp.concatenate([bias_ref[...]] * (length // 128), axis=1)

    def body(step, carry):
        columns = [pl.ds(pl.multiple_of((step * 3 + i) * 128, 128), 128) for i in range(3)]
        found = attend([(q_ref[:, c], k_ref[:, c], v_ref[:, c]) for c in columns], bias)
        for i, (context, logs) in enumerate(found):
            ctx_ref[:, columns[i]] = context
            lse_ref[0, step * 3 + i] = logs
        return carry

    lax.fori_loop(0, width // 384, body, 0)


def attention_forward(q, k, v, bias, length):
    rows, width = q.shape
    seqs, pairs = rows // length, width // 128
    block = pl.BlockSpec((length, width), lambda s: (s, 0))
    return pl.pallas_call(
        forward_kernel,
        grid=(seqs,),
        out_shape=(jax.ShapeDtypeStruct(q.shape, jnp.bfloat16), jax.ShapeDtypeStruct((seqs, pairs, 2, length), jnp.float32)),
        in_specs=[block, block, block, pl.BlockSpec((length, 128), lambda s: (s, 0))],
        out_specs=(block, pl.BlockSpec((1, pairs, 2, length), lambda s: (s, 0, 0, 0))),
    )(q, k, v, bias)


def widen_kernel(*refs):
    for source, to in zip(refs[:len(refs) // 2], refs[len(refs) // 2:]):
        to[...] = source[...].astype(jnp.float32)


def to_float32(arrays):
    steps = 24
    blocks = [pl.BlockSpec((a.shape[0] // steps, a.shape[1]), lambda i: (i, 0)) for a in arrays]
    return pl.pallas_call(
        widen_kernel,
        grid=(steps,),
        out_shape=tuple(jax.ShapeDtypeStruct(a.shape, jnp.float32) for a in arrays),
        in_specs=blocks,
        out_specs=tuple(blocks),
    )(*arrays)


epsilon = 1e-05


def to_partner(block):
    return lax.ppermute(block, "mod", [(0, 1), (1, 0)])


def take_side(array, axis, side):
    half = array.shape[axis] // 2
    return lax.dynamic_slice_in_dim(array, side * half, half, axis)


def gather_sequences(array, side, away):
    own = take_side(array, 0, side)
    other = to_partner(away)
    both = jnp.where(side == 0, jnp.concatenate((own, other), axis=1), jnp.concatenate((other, own), axis=1))
    return both.reshape(-1, array.shape[2])


def return_rows(array, side):
    own = take_side(array, 1, side)
    other = to_partner(take_side(array, 1, 1 - side))
    return jnp.where(side == 0, jnp.concatenate((own, other)), jnp.concatenate((other, own)))


def linear(rows, weight_matrix):
    return lax.dot_general(rows, weight_matrix, (((1,), (0,)), ((), ())), preferred_element_type=jnp.float32)


def back_linear(gradient_rows, weight_matrix):
    return lax.dot_general(gradient_rows, weight_matrix, (((1,), (1,)), ((), ())), preferred_element_type=jnp.float32)


def weight_grad(layer_inputs, gradient_rows):
    return lax.dot_general(
        layer_inputs, gradient_rows, (((0,), (0,)), ((), ())), preferred_element_type=jnp.float32
    ).astype(jnp.bfloat16)


def row_total(values):
    return jnp.sum(values.astype(jnp.float32), axis=0, keepdims=True)


def layer_norm(rows):
    centre = rows - jnp.mean(rows, axis=-1, keepdims=True)
    factor = lax.rsqrt(jnp.mean(centre * centre, axis=-1, keepdims=True) + epsilon)
    return (centre * factor, factor)


def norm_back(gradient_rows, normed, factor):
    return factor * (
        gradient_rows
        - jnp.mean(gradient_rows, axis=-1, keepdims=True)
        - normed * jnp.mean(gradient_rows * normed, axis=-1, keepdims=True)
    )


def on_device(
    hidden_in,
    text_mask,
    region_count,
    w_query,
    b_query,
    w_key,
    w_value,
    b_value,
    w_attn_out,
    b_attn_out,
    gain_attn,
    shift_attn,
    w_inner,
    b_inner,
    w_outer,
    b_outer,
    gain_ffn,
    shift_ffn,
    cotangent,
):
    seq_count, half_len, width = hidden_in.shape
    length = 2 * half_len
    side = lax.axis_index("mod")
    f32 = jnp.float32
    rows_b = gather_sequences(hidden_in, side, take_side(hidden_in, 0, 1 - side))
    rows_b, away = lax.optimization_barrier((rows_b, take_side(cotangent, 0, 1 - side)))
    upstream = gather_sequences(cotangent, side, away).astype(f32)
    mask = take_side(text_mask, 0, side) == 1
    regions = take_side(region_count, 0, side)
    slot_ok = lax.broadcasted_iota(jnp.int32, mask.shape, 1) < regions[:, None]
    bias = jnp.where(jnp.concatenate((mask, slot_ok), axis=1), f32(0.0), f32(-1000000000.0)).reshape(-1, 1)
    bias = jnp.broadcast_to(bias, (bias.shape[0], 128))

    query_b = ((linear(rows_b, w_query) + b_query.astype(f32)).astype(jnp.bfloat16) * jnp.bfloat16(0.125))
    key_b = linear(rows_b, w_key).astype(jnp.bfloat16)
    value_b = (linear(rows_b, w_value) + b_value.astype(f32)).astype(jnp.bfloat16)
    context_b, lse = attention_forward(query_b, key_b, value_b, bias, length)
    branch = linear(context_b, w_attn_out) + b_attn_out.astype(f32)
    normed_one, factor_one = layer_norm(rows_b.astype(f32) + branch)
    middle = normed_one * gain_attn.astype(f32) + shift_attn.astype(f32)
    middle_b = middle.astype(jnp.bfloat16)
    pre_act = linear(middle_b, w_inner) + b_inner.astype(f32)
    below = 0.5 * (1.0 + lax.erf(pre_act * f32(0.7071067811865476)))
    slope_b = (below + pre_act * (jnp.exp(-0.5 * pre_act * pre_act) * f32(0.3989422804014327))).astype(jnp.bfloat16)
    activ_b = (pre_act * below).astype(jnp.bfloat16)
    ffn_out = linear(activ_b, w_outer) + b_outer.astype(f32)
    normed_two, factor_two = layer_norm(middle + ffn_out)
    layer_out = (normed_two * gain_ffn.astype(f32) + shift_ffn.astype(f32)).astype(jnp.bfloat16)
    layer_out = return_rows(layer_out.reshape(seq_count // 2, length, width), side)
    grad_gain_ffn = row_total(upstream * normed_two)
    grad_shift_ffn = row_total(upstream)
    d_res_two = norm_back(upstream * gain_ffn.astype(f32), normed_two, factor_two)
    d_ffn_b = d_res_two.astype(jnp.bfloat16)
    grad_b_outer = row_total(d_ffn_b)
    grad_w_outer = weight_grad(activ_b, d_ffn_b)
    s_outer, s_inner, s_query, s_key, s_value, s_attn_out, small, input_grad = backward(
        grad_w_outer, w_outer, w_inner, slope_b,
        (
            query_b, key_b, value_b, context_b, rows_b, middle_b, d_ffn_b, d_res_two, normed_one,
            w_query, w_key, w_value, w_attn_out,
        ),
        (factor_one, gain_attn.astype(f32).reshape(1, -1), lse, bias, grad_b_outer, grad_gain_ffn, grad_shift_ffn),
        hidden_in.shape,
    )
    s_outer, s_inner, s_query, s_key, s_value, s_attn_out = to_float32(
        (s_outer, s_inner, s_query, s_key, s_value, s_attn_out)
    )
    return (
        layer_out,
        input_grad,
        s_query,
        small[0],
        s_key,
        s_value,
        small[1],
        s_attn_out,
        small[2],
        small[3],
        small[4],
        s_inner,
        small[8:12].reshape(-1),
        s_outer,
        small[5],
        small[6],
        small[7],
    )


def solution(mesh):
    in_specs = (
        P("batch", "mod", None),
        P("batch", None),
        P("batch"),
        P(),
        P(),
        P(),
        P(),
        P(),
        P(),
        P(),
        P(),
        P(),
        P(),
        P(),
        P(),
        P(),
        P(),
        P(),
        P("batch", "mod", None),
    )
    out_specs = (
        P("batch", "mod", None),
        P("batch", "mod", None),
        P(),
        P(),
        P(),
        P(),
        P(),
        P(),
        P(),
        P(),
        P(),
        P(),
        P(),
        P(),
        P(),
        P(),
        P(),
    )
    return jax.shard_map(
        on_device, mesh=mesh, in_specs=in_specs, out_specs=out_specs, check_vma=False
    )
```
